256 devices in a mesh: pts: 64 (over z, x, core), rhs: 4 (over y).
Axes of the slice: x: 4, y: 4, z: 8, core: 2. Of those that a mesh axis runs over, the one named last changes fastest.
Arguments:
- points: bfloat16 [131072, 32], P('pts'), may hold values from -0.5 to 0.5
- noise_var: float32 [131072], P('pts'), may hold values from 0.5 to 0.6
- right_side: float32 [64, 131072], P('rhs', 'pts'), may hold values from -12 to 12
- pattern: int32 [1024, 33], P('pts'), may hold values from 0 to 1, as said below
Outputs:
- solution: float32 [64, 131072], P('rhs', 'pts')
- residual: float32 [64, 131072], P('rhs', 'pts')
- res_image: float32 [64, 131072], P('rhs', 'pts')
The draws below stay inside these ranges and needn't reach their ends.
Inputs may be any that keep to these rules, and one draw needn't show every extreme that they name: Symmetric: pattern[b, 16 + d] = pattern[b + d, 16 - d]; the centre column is 1; entries naming a block outside 0 to 1023 are 0.
All inputs are finite; a program needn't handle non-finite values.
Results may differ from the reference program's by a relative error of at most 0.0036.
Values may be sent and summed in bfloat16 or wider, within the bound.
A program may use at most 64 MiB of HBM per device.

```python
import math
import jax
import jax.numpy as jnp
from jax import lax

F = 32
R = 64
BLK = 128
REACH = 16
ITERS = 2
BLK_DEV = 16
WIDE = 33
WEXP = 18
NBLK = 1024
POINTS = 131072


def draw_points(key, part):
    first_key, second_key, third_key = jax.random.split(key, 3)
    freqs = jax.random.uniform(first_key, (F // 2,), jnp.float32, 0.002, 0.004)
    position = jnp.arange(POINTS, dtype=jnp.float32) / BLK
    angles = position[:, None] * freqs[None, :]
    centre = 0.25 * jnp.concatenate([jnp.cos(angles), jnp.sin(angles)], axis=1)
    rough = jnp.exp(jax.random.uniform(second_key, (POINTS, 1), jnp.float32, math.log(0.5), math.log(2.0)))
    jitter = jax.random.truncated_normal(third_key, -4.0, 4.0, (POINTS, F), jnp.float32)
    return (centre + 0.02 * rough * jitter).astype(jnp.bfloat16)


def draw_right_side(key, part):
    first_key = jax.random.fold_in(key, 0)
    scales = 1.0 + 2.0 * jnp.arange(POINTS, dtype=jnp.float32) / POINTS
    values = jax.random.truncated_normal(first_key, -4.0, 4.0, (R, POINTS), jnp.float32)
    return values * scales[None, :]


def draw_pattern(key, part):
    first_key, second_key = jax.random.split(key, 2)
    thresholds = jax.random.randint(first_key, (NBLK // BLK_DEV,), 3, 13)
    raw_bits = jax.random.randint(second_key, (NBLK, REACH), 0, 16)
    block_ids = jnp.arange(NBLK, dtype=jnp.int32)
    inside = block_ids[:, None] + jnp.arange(1, REACH + 1, dtype=jnp.int32)[None, :] < NBLK
    upper = ((raw_bits < thresholds[block_ids // BLK_DEV][:, None]) & inside).astype(jnp.int32)
    columns = []
    for distance in range(REACH, 0, -1):
        columns.append(jnp.concatenate([jnp.zeros((distance,), jnp.int32), upper[:NBLK - distance, distance - 1]]))
    columns.append(jnp.ones((NBLK,), jnp.int32))
    for distance in range(1, REACH + 1):
        columns.append(upper[:, distance - 1])
    return jnp.stack(columns, axis=1)


def steps_of(own_key, shape, cuts, low, high):
    def one(axis_at, parts):
        steps = jax.random.uniform(jax.random.fold_in(jax.random.fold_in(own_key, 6), axis_at), (parts,), jnp.float32, low / len(cuts), high / len(cuts))
        return jnp.repeat(jnp.exp(steps), shape[axis_at] // parts).reshape((-1,) + (1,) * (len(shape) - axis_at - 1))

    loudness = one(*cuts[0])
    for cut in cuts[1:]:
        loudness = loudness * one(*cut)
    return loudness


def setup_inputs(seed: int = 0) -> dict:
    seeds = jax.random.split(jax.random.key(seed), 5)
    points = draw_points(jax.random.fold_in(seeds[4], 71), 0)
    noise_var = jnp.clip(0.5 + 0.100000024 * jax.random.uniform(seeds[1], (POINTS,), jnp.float32) ** steps_of(seeds[1], (POINTS,), ((0, 64),), -0.2, 0.2), 0.5, 0.6)
    right_side = draw_right_side(jax.random.fold_in(seeds[4], 71), 0)
    pattern = draw_pattern(jax.random.fold_in(seeds[4], 71), 0)
    return dict(points=points, noise_var=noise_var, right_side=right_side, pattern=pattern)


def kernel_block(left_points, right_points, left_squares, right_squares):
    cross_terms = jnp.einsum('gif,gjf->gij', left_points, right_points, precision=lax.Precision.HIGHEST)
    dist_squared = jnp.maximum(left_squares[:, :, None] + right_squares[:, None, :] - 2.0 * cross_terms, 0.0)
    radius = jnp.sqrt(dist_squared)
    return jnp.maximum(1.0 - radius, 0.0) ** WEXP * (WEXP * radius + 1.0)

def reference(points, noise_var, right_side, pattern):
    point_blocks = points.astype(jnp.float32).reshape(NBLK, BLK, F)
    squares = lax.optimization_barrier(jnp.sum(point_blocks * point_blocks, axis=2))
    padded_points = jnp.pad(point_blocks, ((REACH, REACH), (0, 0), (0, 0)))
    padded_squares = jnp.pad(squares, ((REACH, REACH), (0, 0)))
    kernel_scale = 1.0 / (4 * BLK)

    def apply_operator(vector):
        vec_low = lax.optimization_barrier(vector.astype(jnp.bfloat16))
        vec_blocks = jnp.pad(vec_low.astype(jnp.float32).T.reshape(NBLK, BLK, R), ((REACH, REACH), (0, 0), (0, 0)))

        def one_offset(running, offset):
            other_points = lax.dynamic_slice_in_dim(padded_points, offset, NBLK, 0)
            other_squares = lax.dynamic_slice_in_dim(padded_squares, offset, NBLK, 0)
            other_vec = lax.dynamic_slice_in_dim(vec_blocks, offset, NBLK, 0)
            profile = kernel_block(point_blocks, other_points, squares, other_squares)
            pattern_col = lax.dynamic_index_in_dim(pattern, offset, 1, keepdims=False).astype(jnp.float32)
            weights_low = lax.optimization_barrier((profile * pattern_col[:, None, None]).astype(jnp.bfloat16))
            weights = weights_low.astype(jnp.float32)
            running = running + jnp.einsum('gij,gjc->gic', weights, other_vec, precision=lax.Precision.HIGHEST)
            return (running, offset)
        summed = lax.scan(one_offset, jnp.zeros((NBLK, BLK, R), jnp.float32), jnp.arange(WIDE, dtype=jnp.int32))[0]
        return noise_var[None, :] * vector + kernel_scale * summed.reshape(POINTS, R).T
    solution = jnp.zeros_like(right_side)
    residual = right_side
    res_image = apply_operator(residual)
    direction = jnp.zeros_like(right_side)
    dir_image = jnp.zeros_like(right_side)
    dir_twice = jnp.zeros_like(right_side)
    norm_prev = None
    step_prev = None
    for iteration in range(ITERS):
        norm_now = lax.optimization_barrier(jnp.sum(residual * residual, axis=1))[:, None]
        curvature = lax.optimization_barrier(jnp.sum(res_image * residual, axis=1))[:, None]
        square_image = apply_operator(res_image)
        if iteration == 0:
            step_len = norm_now / curvature
            direction = residual
            dir_image = res_image
            dir_twice = square_image
        else:
            mix_ratio = norm_now / norm_prev
            step_len = norm_now / (curvature - mix_ratio * norm_now / step_prev)
            direction = residual + mix_ratio * direction
            dir_image = res_image + mix_ratio * dir_image
            dir_twice = square_image + mix_ratio * dir_twice
        solution = solution + step_len * direction
        residual = residual - step_len * dir_image
        res_image = res_image - step_len * dir_twice
        norm_prev = norm_now
        step_prev = step_len
    return (solution, residual, res_image)
```

```python
import functools

import jax
import jax.numpy as jnp
from jax import lax
from jax.experimental import pallas as pl
from jax.experimental.pallas import tpu as pltpu
from jax.sharding import PartitionSpec as P

F = 32
BLK = 128
REACH = 16
ITERS = 2
WIDE = 33
WEXP = 18


def with_halo(cells, axis, dim, width):
    count = lax.axis_size(axis)
    ends = count - 1
    head = lax.slice_in_dim(cells, 0, width, axis=dim)
    tail = lax.slice_in_dim(cells, cells.shape[dim] - width, cells.shape[dim], axis=dim)
    return jnp.concatenate(
        [
            lax.ppermute(tail, axis, [(i, (i + 1) % count) for i in range(ends)]),
            cells,
            lax.ppermute(head, axis, [((i + 1) % count, i) for i in range(ends)]),
        ],
        axis=dim,
    )


def profile_tile(left, right_t, pat):
    left_f = left.astype(jnp.float32)
    right_f = right_t.astype(jnp.float32)
    sq_left = jnp.sum(left_f * left_f, axis=1, keepdims=True)
    sq_right = jnp.sum(right_f * right_f, axis=0, keepdims=True)
    cross = jnp.dot(left, right_t, preferred_element_type=jnp.float32)
    dist = jnp.maximum(sq_left + sq_right - 2.0 * cross, 0.0)
    radius = jnp.sqrt(dist)
    base = jnp.maximum(1.0 - radius, 0.0)
    b2 = base * base
    b4 = b2 * b2
    b8 = b4 * b4
    b16 = b8 * b8
    value = (b16 * b2) * (WEXP * radius + 1.0)
    return (value * pat).astype(jnp.bfloat16)


def build_kernel(pat_ref, pw_ref, pwt_ref, k_ref):
    a = pl.program_id(0)
    start = pl.multiple_of((a + REACH) * BLK, BLK)
    left = pw_ref[pl.ds(start, BLK), :]

    def body(o, carry):
        col = pl.multiple_of((a + o) * BLK, BLK)
        right_t = pwt_ref[:, pl.ds(col, BLK)]
        pat = pat_ref[a * WIDE + o].astype(jnp.float32)
        k_ref[0, :, pl.ds(pl.multiple_of(o * BLK, BLK), BLK)] = profile_tile(left, right_t, pat)
        return carry

    lax.fori_loop(0, WIDE, body, 0)


def apply_kernel(v_ref, k_ref, out_ref):
    a = pl.program_id(0)
    start = pl.multiple_of(a * BLK, BLK)
    v_cat = v_ref[:, pl.ds(start, WIDE * BLK)]
    out_ref[...] = lax.dot_general(
        v_cat, k_ref[0], (((1,), (1,)), ((), ())), preferred_element_type=jnp.float32
    )


def build_k(pattern_flat, wide_points, wide_points_t, blocks):
    wide_rows = wide_points.shape[0]
    return pl.pallas_call(
        build_kernel,
        out_shape=jax.ShapeDtypeStruct((blocks, BLK, WIDE * BLK), jnp.bfloat16),
        grid_spec=pltpu.PrefetchScalarGridSpec(
            num_scalar_prefetch=1,
            grid=(blocks,),
            in_specs=[
                pl.BlockSpec((wide_rows, F), lambda a, p: (0, 0)),
                pl.BlockSpec((F, wide_rows), lambda a, p: (0, 0)),
            ],
            out_specs=pl.BlockSpec((1, BLK, WIDE * BLK), lambda a, p: (a, 0, 0)),
        ),
        compiler_params=pltpu.CompilerParams(dimension_semantics=("arbitrary",)),
    )(pattern_flat, wide_points, wide_points_t)


def apply_k(wide_vec, kmat):
    rows, wide_cols = wide_vec.shape
    blocks = kmat.shape[0]
    return pl.pallas_call(
        apply_kernel,
        out_shape=jax.ShapeDtypeStruct((rows, blocks * BLK), jnp.float32),
        grid=(blocks,),
        in_specs=[
            pl.BlockSpec((rows, wide_cols), lambda a: (0, 0)),
            pl.BlockSpec((1, BLK, WIDE * BLK), lambda a: (a, 0, 0)),
        ],
        out_specs=pl.BlockSpec((rows, BLK), lambda a: (0, a)),
        compiler_params=pltpu.CompilerParams(dimension_semantics=("arbitrary",)),
    )(wide_vec, kmat)


def per_device(points, noise_var, right_side, pattern):
    local_rows = points.shape[0]
    block_count = local_rows // BLK
    rim_rows = REACH * BLK
    kernel_scale = 1.0 / (4 * BLK)
    wide_points = with_halo(points, "pts", 0, rim_rows)
    kmat = build_k(pattern.reshape(-1), wide_points, wide_points.T, block_count)

    rhs_count = lax.axis_size("rhs")
    rhs_index = lax.axis_index("rhs")

    def total(parts):
        slots = jnp.zeros((rhs_count,) + parts.shape, parts.dtype)
        slots = lax.dynamic_update_index_in_dim(slots, parts, rhs_index, 0)
        summed = lax.psum(slots, ("pts", "rhs"))
        return lax.dynamic_index_in_dim(summed, rhs_index, 0, keepdims=False)

    def apply_operator(vector):
        vec_low = vector.astype(jnp.bfloat16)
        wide_vec = with_halo(vec_low, "pts", 1, rim_rows)
        image_part = apply_k(wide_vec, kmat)
        return noise_var[None, :] * vector + kernel_scale * image_part

    solution = jnp.zeros_like(right_side)
    residual = right_side
    res_image = apply_operator(residual)
    direction = jnp.zeros_like(right_side)
    dir_image = jnp.zeros_like(right_side)
    dir_twice = jnp.zeros_like(right_side)
    norm_prev = None
    step_prev = None
    for iteration in range(ITERS):
        sums = total(
            jnp.stack([jnp.sum(residual * residual, axis=1), jnp.sum(res_image * residual, axis=1)])
        )
        norm_now = sums[0][:, None]
        curvature = sums[1][:, None]
        square_image = apply_operator(res_image)
        if iteration == 0:
            step_len = norm_now / curvature
            direction = residual
            dir_image = res_image
            dir_twice = square_image
        else:
            mix_ratio = norm_now / norm_prev
            step_len = norm_now / (curvature - mix_ratio * norm_now / step_prev)
            direction = residual + mix_ratio * direction
            dir_image = res_image + mix_ratio * dir_image
            dir_twice = square_image + mix_ratio * dir_twice
        solution = solution + step_len * direction
        residual = residual - step_len * dir_image
        res_image = res_image - step_len * dir_twice
        norm_prev = norm_now
        step_prev = step_len
    return (solution, residual, res_image)


def solution(mesh):
    placed = (P("pts", None), P("pts"), P("rhs", "pts"), P("pts", None))
    return jax.shard_map(
        per_device,
        mesh=mesh,
        in_specs=placed,
        out_specs=(P("rhs", "pts"), P("rhs", "pts"), P("rhs", "pts")),
        check_vma=False,
    )
```

```python
import functools

import jax
import jax.numpy as jnp
from jax import lax
from jax.experimental import pallas as pl
from jax.experimental.pallas import tpu as pltpu
from jax.sharding import PartitionSpec as P

F = 32
BLK = 128
REACH = 16
ITERS = 2
WIDE = 33
WEXP = 18


def with_halo(cells, axis, dim, width):
    count = lax.axis_size(axis)
    ends = count - 1
    head = lax.slice_in_dim(cells, 0, width, axis=dim)
    tail = lax.slice_in_dim(cells, cells.shape[dim] - width, cells.shape[dim], axis=dim)
    return jnp.concatenate(
        [
            lax.ppermute(tail, axis, [(i, (i + 1) % count) for i in range(ends)]),
            cells,
            lax.ppermute(head, axis, [((i + 1) % count, i) for i in range(ends)]),
        ],
        axis=dim,
    )


def profile_tile(left, right_t, pat):
    left_f = left.astype(jnp.float32)
    right_f = right_t.astype(jnp.float32)
    sq_left = jnp.sum(left_f * left_f, axis=1, keepdims=True)
    sq_right = jnp.sum(right_f * right_f, axis=0, keepdims=True)
    cross = jnp.dot(left, right_t, preferred_element_type=jnp.float32)
    dist = jnp.maximum(sq_left + sq_right - 2.0 * cross, 0.0)
    radius = jnp.sqrt(dist)
    base = jnp.maximum(1.0 - radius, 0.0)
    b2 = base * base
    b4 = b2 * b2
    b8 = b4 * b4
    b16 = b8 * b8
    value = (b16 * b2) * (WEXP * radius + 1.0)
    return (value * pat).astype(jnp.bfloat16)


def build_kernel(pat_ref, pw_ref, pwt_ref, k_ref):
    a = pl.program_id(0)
    start = pl.multiple_of((a + REACH) * BLK, BLK)
    left = pw_ref[pl.ds(start, BLK), :]

    def body(o, carry):
        col = pl.multiple_of((a + o) * BLK, BLK)
        right_t = pwt_ref[:, pl.ds(col, BLK)]
        pat = pat_ref[a * WIDE + o].astype(jnp.float32)
        k_ref[0, :, pl.ds(pl.multiple_of(o * BLK, BLK), BLK)] = profile_tile(left, right_t, pat)
        return carry

    lax.fori_loop(0, WIDE, body, 0)


def apply_kernel(v_ref, k_ref, out_ref):
    a = pl.program_id(0)
    start = pl.multiple_of(a * BLK, BLK)
    v_cat = v_ref[:, pl.ds(start, WIDE * BLK)]
    out_ref[...] = lax.dot_general(
        v_cat, k_ref[0], (((1,), (1,)), ((), ())), preferred_element_type=jnp.float32
    )


def build_k(pattern_flat, wide_points, wide_points_t, blocks):
    wide_rows = wide_points.shape[0]
    return pl.pallas_call(
        build_kernel,
        out_shape=jax.ShapeDtypeStruct((blocks, BLK, WIDE * BLK), jnp.bfloat16),
        grid_spec=pltpu.PrefetchScalarGridSpec(
            num_scalar_prefetch=1,
            grid=(blocks,),
            in_specs=[
                pl.BlockSpec((wide_rows, F), lambda a, p: (0, 0)),
                pl.BlockSpec((F, wide_rows), lambda a, p: (0, 0)),
            ],
            out_specs=pl.BlockSpec((1, BLK, WIDE * BLK), lambda a, p: (a, 0, 0)),
        ),
        compiler_params=pltpu.CompilerParams(dimension_semantics=("arbitrary",)),
    )(pattern_flat, wide_points, wide_points_t)


def apply_k(wide_vec, kmat):
    rows, wide_cols = wide_vec.shape
    blocks = kmat.shape[0]
    return pl.pallas_call(
        apply_kernel,
        out_shape=jax.ShapeDtypeStruct((rows, blocks * BLK), jnp.float32),
        grid=(blocks,),
        in_specs=[
            pl.BlockSpec((rows, wide_cols), lambda a: (0, 0)),
            pl.BlockSpec((1, BLK, WIDE * BLK), lambda a: (a, 0, 0)),
        ],
        out_specs=pl.BlockSpec((rows, BLK), lambda a: (0, a)),
        compiler_params=pltpu.CompilerParams(dimension_semantics=("arbitrary",)),
    )(wide_vec, kmat)


def per_device(points, noise_var, right_side, pattern):
    local_rows = points.shape[0]
    block_count = local_rows // BLK
    rim_rows = REACH * BLK
    kernel_scale = 1.0 / (4 * BLK)
    wide_points = with_halo(points, "pts", 0, rim_rows)
    kmat = build_k(pattern.reshape(-1), wide_points, wide_points.T, block_count)

    rhs_count = lax.axis_size("rhs")
    rhs_index = lax.axis_index("rhs")

    def total(parts):
        slots = jnp.zeros((128, 128), parts.dtype)
        slots = lax.dynamic_update_slice(slots, parts, (0, 0))
        summed = lax.psum(slots, "pts")
        return summed[:2, :16]

    def apply_operator(vector):
        vec_low = vector.astype(jnp.bfloat16)
        wide_vec = with_halo(vec_low, "pts", 1, rim_rows)
        image_part = apply_k(wide_vec, kmat)
        return noise_var[None, :] * vector + kernel_scale * image_part

    solution = jnp.zeros_like(right_side)
    residual = right_side
    res_image = apply_operator(residual)
    direction = jnp.zeros_like(right_side)
    dir_image = jnp.zeros_like(right_side)
    dir_twice = jnp.zeros_like(right_side)
    norm_prev = None
    step_prev = None
    for iteration in range(ITERS):
        sums = total(
            jnp.stack([jnp.sum(residual * residual, axis=1), jnp.sum(res_image * residual, axis=1)])
        )
        norm_now = sums[0][:, None]
        curvature = sums[1][:, None]
        square_image = apply_operator(res_image)
        if iteration == 0:
            step_len = norm_now / curvature
            direction = residual
            dir_image = res_image
            dir_twice = square_image
        else:
            mix_ratio = norm_now / norm_prev
            step_len = norm_now / (curvature - mix_ratio * norm_now / step_prev)
            direction = residual + mix_ratio * direction
            dir_image = res_image + mix_ratio * dir_image
            dir_twice = square_image + mix_ratio * dir_twice
        solution = solution + step_len * direction
        residual = residual - step_len * dir_image
        res_image = res_image - step_len * dir_twice
        norm_prev = norm_now
        step_prev = step_len
    return (solution, residual, res_image)


def solution(mesh):
    placed = (P("pts", None), P("pts"), P("rhs", "pts"), P("pts", None))
    return jax.shard_map(
        per_device,
        mesh=mesh,
        in_specs=placed,
        out_specs=(P("rhs", "pts"), P("rhs", "pts"), P("rhs", "pts")),
        check_vma=False,
    )
```

```python
import functools

import jax
import jax.numpy as jnp
from jax import lax
from jax.experimental import pallas as pl
from jax.experimental.pallas import tpu as pltpu
from jax.sharding import PartitionSpec as P

F = 32
BLK = 128
REACH = 16
ITERS = 2
WIDE = 33
WEXP = 18
MESH = pl.DeviceIdType.MESH


def with_halo(cells, axis, dim, width):
    count = lax.axis_size(axis)
    ends = count - 1
    head = lax.slice_in_dim(cells, 0, width, axis=dim)
    tail = lax.slice_in_dim(cells, cells.shape[dim] - width, cells.shape[dim], axis=dim)
    return jnp.concatenate(
        [
            lax.ppermute(tail, axis, [(i, (i + 1) % count) for i in range(ends)]),
            cells,
            lax.ppermute(head, axis, [((i + 1) % count, i) for i in range(ends)]),
        ],
        axis=dim,
    )


def profile_tile(left, right_t, pat):
    left_f = left.astype(jnp.float32)
    right_f = right_t.astype(jnp.float32)
    sq_left = jnp.sum(left_f * left_f, axis=1, keepdims=True)
    sq_right = jnp.sum(right_f * right_f, axis=0, keepdims=True)
    cross = jnp.dot(left, right_t, preferred_element_type=jnp.float32)
    dist = jnp.maximum(sq_left + sq_right - 2.0 * cross, 0.0)
    radius = jnp.sqrt(dist)
    base = jnp.maximum(1.0 - radius, 0.0)
    b2 = base * base
    b4 = b2 * b2
    b8 = b4 * b4
    b16 = b8 * b8
    value = (b16 * b2) * (WEXP * radius + 1.0)
    return (value * pat).astype(jnp.bfloat16)


def build_kernel(pat_ref, pw_ref, pwt_ref, k_ref):
    a = pl.program_id(0)
    start = pl.multiple_of((a + REACH) * BLK, BLK)
    left = pw_ref[pl.ds(start, BLK), :]

    def body(o, carry):
        col = pl.multiple_of((a + o) * BLK, BLK)
        right_t = pwt_ref[:, pl.ds(col, BLK)]
        pat = pat_ref[a * WIDE + o].astype(jnp.float32)
        k_ref[0, :, pl.ds(pl.multiple_of(o * BLK, BLK), BLK)] = profile_tile(left, right_t, pat)
        return carry

    lax.fori_loop(0, WIDE, body, 0)


def apply_kernel(v_ref, k_ref, out_ref):
    a = pl.program_id(0)
    start = pl.multiple_of(a * BLK, BLK)
    v_cat = v_ref[:, pl.ds(start, WIDE * BLK)]
    out_ref[...] = lax.dot_general(
        v_cat, k_ref[0], (((1,), (1,)), ((), ())), preferred_element_type=jnp.float32
    )


def build_k(pattern_flat, wide_points, wide_points_t, blocks):
    wide_rows = wide_points.shape[0]
    return pl.pallas_call(
        build_kernel,
        out_shape=jax.ShapeDtypeStruct((blocks, BLK, WIDE * BLK), jnp.bfloat16),
        grid_spec=pltpu.PrefetchScalarGridSpec(
            num_scalar_prefetch=1,
            grid=(blocks,),
            in_specs=[
                pl.BlockSpec((wide_rows, F), lambda a, p: (0, 0)),
                pl.BlockSpec((F, wide_rows), lambda a, p: (0, 0)),
            ],
            out_specs=pl.BlockSpec((1, BLK, WIDE * BLK), lambda a, p: (a, 0, 0)),
        ),
        compiler_params=pltpu.CompilerParams(dimension_semantics=("arbitrary",)),
    )(pattern_flat, wide_points, wide_points_t)


def apply_k(wide_vec, kmat):
    rows, wide_cols = wide_vec.shape
    blocks = kmat.shape[0]
    return pl.pallas_call(
        apply_kernel,
        out_shape=jax.ShapeDtypeStruct((rows, blocks * BLK), jnp.float32),
        grid=(blocks,),
        in_specs=[
            pl.BlockSpec((rows, wide_cols), lambda a: (0, 0)),
            pl.BlockSpec((1, BLK, WIDE * BLK), lambda a: (a, 0, 0)),
        ],
        out_specs=pl.BlockSpec((rows, BLK), lambda a: (0, a)),
        compiler_params=pltpu.CompilerParams(dimension_semantics=("arbitrary",)),
    )(wide_vec, kmat)


def sum_kernel(count, part_ref, out_ref, recv, send_sem, recv_sem):
    me = lax.axis_index("pts")
    row = lax.axis_index("rhs")

    barrier = pltpu.get_barrier_semaphore()

    def greet(k, carry):
        peer = lax.rem(me + k, count)
        pl.semaphore_signal(barrier, inc=1, device_id=(peer, row), device_id_type=MESH)
        return carry

    lax.fori_loop(1, count, greet, 0)
    pl.semaphore_wait(barrier, count - 1)

    def outgoing(peer):
        return pltpu.make_async_remote_copy(
            src_ref=part_ref,
            dst_ref=recv.at[me],
            send_sem=send_sem.at[peer],
            recv_sem=recv_sem.at[me],
            device_id=(peer, row),
            device_id_type=MESH,
        )

    def incoming(peer):
        return pltpu.make_async_remote_copy(
            src_ref=part_ref,
            dst_ref=recv.at[peer],
            send_sem=send_sem.at[peer],
            recv_sem=recv_sem.at[peer],
            device_id=(peer, row),
            device_id_type=MESH,
        )

    def send(k, carry):
        outgoing(lax.rem(me + k, count)).start()
        return carry

    lax.fori_loop(1, count, send, 0)
    recv[me] = part_ref[...]

    def finish(k, carry):
        peer = lax.rem(me + k, count)
        outgoing(peer).wait_send()
        incoming(peer).wait_recv()
        return carry

    lax.fori_loop(1, count, finish, 0)
    out_ref[...] = jnp.sum(recv[...], axis=0)


def all_sum(tile):
    count = lax.axis_size("pts")
    return pl.pallas_call(
        functools.partial(sum_kernel, count),
        out_shape=jax.ShapeDtypeStruct(tile.shape, jnp.float32),
        in_specs=[pl.BlockSpec(memory_space=pltpu.VMEM)],
        out_specs=pl.BlockSpec(memory_space=pltpu.VMEM),
        scratch_shapes=[
            pltpu.VMEM((count,) + tile.shape, jnp.float32),
            pltpu.SemaphoreType.DMA((count,)),
            pltpu.SemaphoreType.DMA((count,)),
        ],
        compiler_params=pltpu.CompilerParams(collective_id=0, has_side_effects=True),
    )(tile)


def per_device(points, noise_var, right_side, pattern):
    local_rows = points.shape[0]
    block_count = local_rows // BLK
    rim_rows = REACH * BLK
    kernel_scale = 1.0 / (4 * BLK)
    wide_points = with_halo(points, "pts", 0, rim_rows)
    kmat = build_k(pattern.reshape(-1), wide_points, wide_points.T, block_count)

    rhs_count = lax.axis_size("rhs")
    rhs_index = lax.axis_index("rhs")

    def total(parts):
        tile = jnp.zeros((8, 128), jnp.float32)
        tile = lax.dynamic_update_slice(tile, parts, (0, 0))
        summed = all_sum(tile)
        return summed[: parts.shape[0], : parts.shape[1]]

    def apply_operator(vector):
        vec_low = vector.astype(jnp.bfloat16)
        wide_vec = with_halo(vec_low, "pts", 1, rim_rows)
        image_part = apply_k(wide_vec, kmat)
        return noise_var[None, :] * vector + kernel_scale * image_part

    solution = jnp.zeros_like(right_side)
    residual = right_side
    res_image = apply_operator(residual)
    direction = jnp.zeros_like(right_side)
    dir_image = jnp.zeros_like(right_side)
    dir_twice = jnp.zeros_like(right_side)
    norm_prev = None
    step_prev = None
    for iteration in range(ITERS):
        sums = total(
            jnp.stack([jnp.sum(residual * residual, axis=1), jnp.sum(res_image * residual, axis=1)])
        )
        norm_now = sums[0][:, None]
        curvature = sums[1][:, None]
        square_image = apply_operator(res_image)
        if iteration == 0:
            step_len = norm_now / curvature
            direction = residual
            dir_image = res_image
            dir_twice = square_image
        else:
            mix_ratio = norm_now / norm_prev
            step_len = norm_now / (curvature - mix_ratio * norm_now / step_prev)
            direction = residual + mix_ratio * direction
            dir_image = res_image + mix_ratio * dir_image
            dir_twice = square_image + mix_ratio * dir_twice
        solution = solution + step_len * direction
        residual = residual - step_len * dir_image
        res_image = res_image - step_len * dir_twice
        norm_prev = norm_now
        step_prev = step_len
    return (solution, residual, res_image)


def solution(mesh):
    placed = (P("pts", None), P("pts"), P("rhs", "pts"), P("pts", None))
    return jax.shard_map(
        per_device,
        mesh=mesh,
        in_specs=placed,
        out_specs=(P("rhs", "pts"), P("rhs", "pts"), P("rhs", "pts")),
        check_vma=False,
    )
```

```python
import functools

import jax
import jax.numpy as jnp
from jax import lax
from jax.experimental import pallas as pl
from jax.experimental.pallas import tpu as pltpu
from jax.sharding import PartitionSpec as P

F = 32
BLK = 128
REACH = 16
ITERS = 2
WIDE = 33
WEXP = 18
MESH = pl.DeviceIdType.MESH


def with_halo(cells, axis, dim, width):
    count = lax.axis_size(axis)
    ends = count - 1
    head = lax.slice_in_dim(cells, 0, width, axis=dim)
    tail = lax.slice_in_dim(cells, cells.shape[dim] - width, cells.shape[dim], axis=dim)
    return jnp.concatenate(
        [
            lax.ppermute(tail, axis, [(i, (i + 1) % count) for i in range(ends)]),
            cells,
            lax.ppermute(head, axis, [((i + 1) % count, i) for i in range(ends)]),
        ],
        axis=dim,
    )


def profile_tile(left_m2, sq_left, right_t, sq_right):
    cross = jnp.dot(left_m2, right_t, preferred_element_type=jnp.float32)
    dist = jnp.maximum((sq_left + sq_right) + cross, 0.0)
    radius = jnp.sqrt(dist)
    base = jnp.maximum(1.0 - radius, 0.0)
    b2 = base * base
    b4 = b2 * b2
    b8 = b4 * b4
    b16 = b8 * b8
    value = (b16 * b2) * (WEXP * radius + 1.0)
    return value.astype(jnp.bfloat16)


def build_kernel(pat_ref, pw_ref, pwt_ref, sqr_ref, k_ref):
    a = pl.program_id(0)
    start = pl.multiple_of((a + REACH) * BLK, BLK)
    left = pw_ref[pl.ds(start, BLK), :]
    left_f = left.astype(jnp.float32)
    sq_left = jnp.sum(left_f * left_f, axis=1, keepdims=True)
    left_m2 = left * jnp.asarray(-2.0, jnp.bfloat16)

    def body(o, carry):
        col = pl.multiple_of((a + o) * BLK, BLK)
        dst = pl.ds(pl.multiple_of(o * BLK, BLK), BLK)
        live = pat_ref[a * WIDE + o] != 0

        @pl.when(live)
        def _():
            right_t = pwt_ref[:, pl.ds(col, BLK)]
            sq_right = sqr_ref[:, pl.ds(col, BLK)]
            k_ref[0, :, dst] = profile_tile(left_m2, sq_left, right_t, sq_right)

        @pl.when(jnp.logical_not(live))
        def _():
            k_ref[0, :, dst] = jnp.zeros((BLK, BLK), jnp.bfloat16)

        return carry

    lax.fori_loop(0, WIDE, body, 0)


def apply_kernel(v_ref, k_ref, out_ref):
    a = pl.program_id(0)
    start = pl.multiple_of(a * BLK, BLK)
    v_cat = v_ref[:, pl.ds(start, WIDE * BLK)]
    out_ref[...] = lax.dot_general(
        v_cat, k_ref[0], (((1,), (1,)), ((), ())), preferred_element_type=jnp.float32
    )


def build_k(pattern_flat, wide_points, blocks):
    wide_rows = wide_points.shape[0]
    wide_points_t = wide_points.T
    wide_f = wide_points_t.astype(jnp.float32)
    sq_row = jnp.sum(wide_f * wide_f, axis=0, keepdims=True)
    return pl.pallas_call(
        build_kernel,
        out_shape=jax.ShapeDtypeStruct((blocks, BLK, WIDE * BLK), jnp.bfloat16),
        grid_spec=pltpu.PrefetchScalarGridSpec(
            num_scalar_prefetch=1,
            grid=(blocks,),
            in_specs=[
                pl.BlockSpec((wide_rows, F), lambda a, p: (0, 0)),
                pl.BlockSpec((F, wide_rows), lambda a, p: (0, 0)),
                pl.BlockSpec((1, wide_rows), lambda a, p: (0, 0)),
            ],
            out_specs=pl.BlockSpec((1, BLK, WIDE * BLK), lambda a, p: (a, 0, 0)),
        ),
        compiler_params=pltpu.CompilerParams(dimension_semantics=("arbitrary",)),
    )(pattern_flat, wide_points, wide_points_t, sq_row)


def apply_k(wide_vec, kmat):
    rows, wide_cols = wide_vec.shape
    blocks = kmat.shape[0]
    return pl.pallas_call(
        apply_kernel,
        out_shape=jax.ShapeDtypeStruct((rows, blocks * BLK), jnp.float32),
        grid=(blocks,),
        in_specs=[
            pl.BlockSpec((rows, wide_cols), lambda a: (0, 0)),
            pl.BlockSpec((1, BLK, WIDE * BLK), lambda a: (a, 0, 0)),
        ],
        out_specs=pl.BlockSpec((rows, BLK), lambda a: (0, a)),
        compiler_params=pltpu.CompilerParams(dimension_semantics=("arbitrary",)),
    )(wide_vec, kmat)


def sum_kernel(count, part_ref, out_ref, recv, send_sem, recv_sem):
    me = lax.axis_index("pts")
    row = lax.axis_index("rhs")

    barrier = pltpu.get_barrier_semaphore()

    def greet(k, carry):
        peer = lax.rem(me + k, count)
        pl.semaphore_signal(barrier, inc=1, device_id=(peer, row), device_id_type=MESH)
        return carry

    lax.fori_loop(1, count, greet, 0)
    pl.semaphore_wait(barrier, count - 1)

    def outgoing(peer):
        return pltpu.make_async_remote_copy(
            src_ref=part_ref,
            dst_ref=recv.at[me],
            send_sem=send_sem.at[peer],
            recv_sem=recv_sem.at[me],
            device_id=(peer, row),
            device_id_type=MESH,
        )

    def incoming(peer):
        return pltpu.make_async_remote_copy(
            src_ref=part_ref,
            dst_ref=recv.at[peer],
            send_sem=send_sem.at[peer],
            recv_sem=recv_sem.at[peer],
            device_id=(peer, row),
            device_id_type=MESH,
        )

    def send(k, carry):
        outgoing(lax.rem(me + k, count)).start()
        return carry

    lax.fori_loop(1, count, send, 0)
    recv[me] = part_ref[...]

    def finish(k, carry):
        peer = lax.rem(me + k, count)
        outgoing(peer).wait_send()
        incoming(peer).wait_recv()
        return carry

    lax.fori_loop(1, count, finish, 0)
    out_ref[...] = jnp.sum(recv[...], axis=0)


def all_sum(tile):
    count = lax.axis_size("pts")
    return pl.pallas_call(
        functools.partial(sum_kernel, count),
        out_shape=jax.ShapeDtypeStruct(tile.shape, jnp.float32),
        in_specs=[pl.BlockSpec(memory_space=pltpu.VMEM)],
        out_specs=pl.BlockSpec(memory_space=pltpu.VMEM),
        scratch_shapes=[
            pltpu.VMEM((count,) + tile.shape, jnp.float32),
            pltpu.SemaphoreType.DMA((count,)),
            pltpu.SemaphoreType.DMA((count,)),
        ],
        compiler_params=pltpu.CompilerParams(collective_id=0, has_side_effects=True),
    )(tile)


def per_device(points, noise_var, right_side, pattern):
    local_rows = points.shape[0]
    block_count = local_rows // BLK
    rim_rows = REACH * BLK
    kernel_scale = 1.0 / (4 * BLK)
    wide_points = with_halo(points, "pts", 0, rim_rows)
    kmat = build_k(pattern.reshape(-1), wide_points, block_count)

    rhs_count = lax.axis_size("rhs")
    rhs_index = lax.axis_index("rhs")

    def total(parts):
        tile = jnp.zeros((8, 128), jnp.float32)
        tile = lax.dynamic_update_slice(tile, parts, (0, 0))
        summed = all_sum(tile)
        return summed[: parts.shape[0], : parts.shape[1]]

    def apply_operator(vector):
        vec_low = vector.astype(jnp.bfloat16)
        wide_vec = with_halo(vec_low, "pts", 1, rim_rows)
        image_part = apply_k(wide_vec, kmat)
        return noise_var[None, :] * vector + kernel_scale * image_part

    solution = jnp.zeros_like(right_side)
    residual = right_side
    res_image = apply_operator(residual)
    direction = jnp.zeros_like(right_side)
    dir_image = jnp.zeros_like(right_side)
    dir_twice = jnp.zeros_like(right_side)
    norm_prev = None
    step_prev = None
    for iteration in range(ITERS):
        sums = total(
            jnp.stack([jnp.sum(residual * residual, axis=1), jnp.sum(res_image * residual, axis=1)])
        )
        norm_now = sums[0][:, None]
        curvature = sums[1][:, None]
        square_image = apply_operator(res_image)
        if iteration == 0:
            step_len = norm_now / curvature
            direction = residual
            dir_image = res_image
            dir_twice = square_image
        else:
            mix_ratio = norm_now / norm_prev
            step_len = norm_now / (curvature - mix_ratio * norm_now / step_prev)
            direction = residual + mix_ratio * direction
            dir_image = res_image + mix_ratio * dir_image
            dir_twice = square_image + mix_ratio * dir_twice
        solution = solution + step_len * direction
        residual = residual - step_len * dir_image
        res_image = res_image - step_len * dir_twice
        norm_prev = norm_now
        step_prev = step_len
    return (solution, residual, res_image)


def solution(mesh):
    placed = (P("pts", None), P("pts"), P("rhs", "pts"), P("pts", None))
    return jax.shard_map(
        per_device,
        mesh=mesh,
        in_specs=placed,
        out_specs=(P("rhs", "pts"), P("rhs", "pts"), P("rhs", "pts")),
        check_vma=False,
    )
```

```python
import functools

import jax
import jax.numpy as jnp
from jax import lax
from jax.experimental import pallas as pl
from jax.experimental.pallas import tpu as pltpu
from jax.sharding import PartitionSpec as P

F = 32
BLK = 128
REACH = 16
ITERS = 2
WIDE = 33
WEXP = 18
MESH = pl.DeviceIdType.MESH


def with_halo(cells, axis, dim, width):
    count = lax.axis_size(axis)
    ends = count - 1
    head = lax.slice_in_dim(cells, 0, width, axis=dim)
    tail = lax.slice_in_dim(cells, cells.shape[dim] - width, cells.shape[dim], axis=dim)
    return jnp.concatenate(
        [
            lax.ppermute(tail, axis, [(i, (i + 1) % count) for i in range(ends)]),
            cells,
            lax.ppermute(head, axis, [((i + 1) % count, i) for i in range(ends)]),
        ],
        axis=dim,
    )


def profile_tile(left_m2, sq_left, right_t, sq_right):
    cross = jnp.dot(left_m2, right_t, preferred_element_type=jnp.float32)
    dist = jnp.maximum((sq_left + sq_right) + cross, 0.0)
    radius = jnp.sqrt(dist)
    base = jnp.maximum(1.0 - radius, 0.0)
    b2 = base * base
    b4 = b2 * b2
    b8 = b4 * b4
    b16 = b8 * b8
    value = (b16 * b2) * (WEXP * radius + 1.0)
    return value.astype(jnp.bfloat16)


def build_kernel(pat_ref, pw_ref, pwt_ref, sqr_ref, k_ref):
    a = pl.program_id(0)
    start = pl.multiple_of((a + REACH) * BLK, BLK)
    left = pw_ref[pl.ds(start, BLK), :]
    left_f = left.astype(jnp.float32)
    sq_left = jnp.sum(left_f * left_f, axis=1, keepdims=True)
    left_m2 = left * jnp.asarray(-2.0, jnp.bfloat16)

    def body(o, carry):
        col = pl.multiple_of((a + o) * BLK, BLK)
        dst = pl.ds(pl.multiple_of(o * BLK, BLK), BLK)
        live = pat_ref[a * WIDE + o] != 0

        @pl.when(live)
        def _():
            right_t = pwt_ref[:, pl.ds(col, BLK)]
            sq_right = sqr_ref[:, pl.ds(col, BLK)]
            k_ref[0, :, dst] = profile_tile(left_m2, sq_left, right_t, sq_right)

        @pl.when(jnp.logical_not(live))
        def _():
            k_ref[0, :, dst] = jnp.zeros((BLK, BLK), jnp.bfloat16)

        return carry

    lax.fori_loop(0, WIDE, body, 0)


def apply_kernel(v_ref, k_ref, out_ref):
    a = pl.program_id(0)
    start = pl.multiple_of(a * BLK, BLK)
    v_cat = v_ref[:, pl.ds(start, WIDE * BLK)]
    out_ref[...] = lax.dot_general(
        v_cat, k_ref[0], (((1,), (1,)), ((), ())), preferred_element_type=jnp.float32
    )


def build_k(pattern_flat, wide_points, blocks):
    wide_rows = wide_points.shape[0]
    wide_points_t = wide_points.T
    wide_f = wide_points_t.astype(jnp.float32)
    sq_row = jnp.sum(wide_f * wide_f, axis=0, keepdims=True)
    return pl.pallas_call(
        build_kernel,
        out_shape=jax.ShapeDtypeStruct((blocks, BLK, WIDE * BLK), jnp.bfloat16),
        grid_spec=pltpu.PrefetchScalarGridSpec(
            num_scalar_prefetch=1,
            grid=(blocks,),
            in_specs=[
                pl.BlockSpec((wide_rows, F), lambda a, p: (0, 0)),
                pl.BlockSpec((F, wide_rows), lambda a, p: (0, 0)),
                pl.BlockSpec((1, wide_rows), lambda a, p: (0, 0)),
            ],
            out_specs=pl.BlockSpec((1, BLK, WIDE * BLK), lambda a, p: (a, 0, 0)),
        ),
        compiler_params=pltpu.CompilerParams(dimension_semantics=("arbitrary",)),
    )(pattern_flat, wide_points, wide_points_t, sq_row)


def apply_k(wide_vec, kmat):
    rows, wide_cols = wide_vec.shape
    blocks = kmat.shape[0]
    return pl.pallas_call(
        apply_kernel,
        out_shape=jax.ShapeDtypeStruct((rows, blocks * BLK), jnp.float32),
        grid=(blocks,),
        in_specs=[
            pl.BlockSpec((rows, wide_cols), lambda a: (0, 0)),
            pl.BlockSpec((1, BLK, WIDE * BLK), lambda a: (a, 0, 0)),
        ],
        out_specs=pl.BlockSpec((rows, BLK), lambda a: (0, a)),
        compiler_params=pltpu.CompilerParams(dimension_semantics=("arbitrary",)),
    )(wide_vec, kmat)


def sum_kernel(inner, outer, part_ref, out_ref, stage1, stage2, local_sem, send1, recv1, send2, recv2):
    me = lax.axis_index("pts")
    row = lax.axis_index("rhs")
    zc = me // inner
    rc = me % inner

    barrier = pltpu.get_barrier_semaphore()

    def greet_inner(k, carry):
        peer = zc * inner + lax.rem(rc + k, inner)
        pl.semaphore_signal(barrier, inc=1, device_id=(peer, row), device_id_type=MESH)
        return carry

    def greet_outer(k, carry):
        peer = lax.rem(zc + k, outer) * inner + rc
        pl.semaphore_signal(barrier, inc=1, device_id=(peer, row), device_id_type=MESH)
        return carry

    lax.fori_loop(1, inner, greet_inner, 0)
    lax.fori_loop(1, outer, greet_outer, 0)
    pl.semaphore_wait(barrier, (inner - 1) + (outer - 1))

    def first(slot, other):
        return pltpu.make_async_remote_copy(
            src_ref=part_ref,
            dst_ref=stage1.at[slot],
            send_sem=send1.at[other],
            recv_sem=recv1.at[slot],
            device_id=(zc * inner + other, row),
            device_id_type=MESH,
        )

    own1 = pltpu.make_async_copy(part_ref, stage1.at[rc], local_sem.at[0])
    own1.start()

    def send_first(k, carry):
        first(rc, lax.rem(rc + k, inner)).start()
        return carry

    lax.fori_loop(1, inner, send_first, 0)

    def finish_first(k, carry):
        other = lax.rem(rc + k, inner)
        first(rc, other).wait_send()
        first(other, other).wait_recv()
        return carry

    lax.fori_loop(1, inner, finish_first, 0)
    own1.wait()

    def second(slot, other):
        return pltpu.make_async_remote_copy(
            src_ref=stage1,
            dst_ref=stage2.at[slot],
            send_sem=send2.at[other],
            recv_sem=recv2.at[slot],
            device_id=(other * inner + rc, row),
            device_id_type=MESH,
        )

    own2 = pltpu.make_async_copy(stage1, stage2.at[zc], local_sem.at[1])
    own2.start()

    def send_second(k, carry):
        second(zc, lax.rem(zc + k, outer)).start()
        return carry

    lax.fori_loop(1, outer, send_second, 0)

    def finish_second(k, carry):
        other = lax.rem(zc + k, outer)
        second(zc, other).wait_send()
        second(other, other).wait_recv()
        return carry

    lax.fori_loop(1, outer, finish_second, 0)
    own2.wait()
    out_ref[...] = jnp.sum(jnp.sum(stage2[...], axis=0), axis=0)


def all_sum(tile):
    count = lax.axis_size("pts")
    inner = 8 if count % 8 == 0 else count
    outer = count // inner
    return pl.pallas_call(
        functools.partial(sum_kernel, inner, outer),
        out_shape=jax.ShapeDtypeStruct(tile.shape, jnp.float32),
        in_specs=[pl.BlockSpec(memory_space=pltpu.VMEM)],
        out_specs=pl.BlockSpec(memory_space=pltpu.VMEM),
        scratch_shapes=[
            pltpu.VMEM((inner,) + tile.shape, jnp.float32),
            pltpu.VMEM((outer, inner) + tile.shape, jnp.float32),
            pltpu.SemaphoreType.DMA((2,)),
            pltpu.SemaphoreType.DMA((inner,)),
            pltpu.SemaphoreType.DMA((inner,)),
            pltpu.SemaphoreType.DMA((outer,)),
            pltpu.SemaphoreType.DMA((outer,)),
        ],
        compiler_params=pltpu.CompilerParams(collective_id=0, has_side_effects=True),
    )(tile)


def per_device(points, noise_var, right_side, pattern):
    local_rows = points.shape[0]
    block_count = local_rows // BLK
    rim_rows = REACH * BLK
    kernel_scale = 1.0 / (4 * BLK)
    wide_points = with_halo(points, "pts", 0, rim_rows)
    kmat = build_k(pattern.reshape(-1), wide_points, block_count)

    rhs_count = lax.axis_size("rhs")
    rhs_index = lax.axis_index("rhs")

    def total(parts):
        tile = jnp.zeros((8, 128), jnp.float32)
        tile = lax.dynamic_update_slice(tile, parts, (0, 0))
        summed = all_sum(tile)
        return summed[: parts.shape[0], : parts.shape[1]]

    def apply_operator(vector):
        vec_low = vector.astype(jnp.bfloat16)
        wide_vec = with_halo(vec_low, "pts", 1, rim_rows)
        image_part = apply_k(wide_vec, kmat)
        return noise_var[None, :] * vector + kernel_scale * image_part

    solution = jnp.zeros_like(right_side)
    residual = right_side
    res_image = apply_operator(residual)
    direction = jnp.zeros_like(right_side)
    dir_image = jnp.zeros_like(right_side)
    dir_twice = jnp.zeros_like(right_side)
    norm_prev = None
    step_prev = None
    for iteration in range(ITERS):
        sums = total(
            jnp.stack([jnp.sum(residual * residual, axis=1), jnp.sum(res_image * residual, axis=1)])
        )
        norm_now = sums[0][:, None]
        curvature = sums[1][:, None]
        square_image = apply_operator(res_image)
        if iteration == 0:
            step_len = norm_now / curvature
            direction = residual
            dir_image = res_image
            dir_twice = square_image
        else:
            mix_ratio = norm_now / norm_prev
            step_len = norm_now / (curvature - mix_ratio * norm_now / step_prev)
            direction = residual + mix_ratio * direction
            dir_image = res_image + mix_ratio * dir_image
            dir_twice = square_image + mix_ratio * dir_twice
        solution = solution + step_len * direction
        residual = residual - step_len * dir_image
        res_image = res_image - step_len * dir_twice
        norm_prev = norm_now
        step_prev = step_len
    return (solution, residual, res_image)


def solution(mesh):
    placed = (P("pts", None), P("pts"), P("rhs", "pts"), P("pts", None))
    return jax.shard_map(
        per_device,
        mesh=mesh,
        in_specs=placed,
        out_specs=(P("rhs", "pts"), P("rhs", "pts"), P("rhs", "pts")),
        check_vma=False,
    )
```

```python
import functools

import jax
import jax.numpy as jnp
from jax import lax
from jax.experimental import pallas as pl
from jax.experimental.pallas import tpu as pltpu
from jax.sharding import PartitionSpec as P

F = 32
BLK = 128
REACH = 16
ITERS = 2
WIDE = 33
WEXP = 18
MESH = pl.DeviceIdType.MESH


def with_halo(cells, axis, dim, width):
    count = lax.axis_size(axis)
    ends = count - 1
    head = lax.slice_in_dim(cells, 0, width, axis=dim)
    tail = lax.slice_in_dim(cells, cells.shape[dim] - width, cells.shape[dim], axis=dim)
    return jnp.concatenate(
        [
            lax.ppermute(tail, axis, [(i, (i + 1) % count) for i in range(ends)]),
            cells,
            lax.ppermute(head, axis, [((i + 1) % count, i) for i in range(ends)]),
        ],
        axis=dim,
    )


def profile_tile(left_m2, sq_left, right_t, sq_right):
    cross = jnp.dot(left_m2, right_t, preferred_element_type=jnp.float32)
    dist = jnp.maximum((sq_left + sq_right) + cross, 0.0)
    radius = jnp.sqrt(dist)
    base = jnp.maximum(1.0 - radius, 0.0)
    b2 = base * base
    b4 = b2 * b2
    b8 = b4 * b4
    b16 = b8 * b8
    value = (b16 * b2) * (WEXP * radius + 1.0)
    return value.astype(jnp.bfloat16)


def build_kernel(pat_ref, pw_ref, pwt_ref, sqr_ref, k_ref):
    a = pl.program_id(0)
    start = pl.multiple_of((a + REACH) * BLK, BLK)
    left = pw_ref[pl.ds(start, BLK), :]
    left_f = left.astype(jnp.float32)
    sq_left = jnp.sum(left_f * left_f, axis=1, keepdims=True)
    left_m2 = left * jnp.asarray(-2.0, jnp.bfloat16)

    def body(o, carry):
        col = pl.multiple_of((a + o) * BLK, BLK)
        dst = pl.ds(pl.multiple_of(o * BLK, BLK), BLK)
        live = pat_ref[a * WIDE + o] != 0

        @pl.when(live)
        def _():
            right_t = pwt_ref[:, pl.ds(col, BLK)]
            sq_right = sqr_ref[:, pl.ds(col, BLK)]
            k_ref[0, :, dst] = profile_tile(left_m2, sq_left, right_t, sq_right)

        @pl.when(jnp.logical_not(live))
        def _():
            k_ref[0, :, dst] = jnp.zeros((BLK, BLK), jnp.bfloat16)

        return carry

    lax.fori_loop(0, WIDE, body, 0)


def apply_kernel(v_ref, k_ref, out_ref):
    a = pl.program_id(0)
    start = pl.multiple_of(a * BLK, BLK)
    v_cat = v_ref[:, pl.ds(start, WIDE * BLK)]
    out_ref[...] = lax.dot_general(
        v_cat, k_ref[0], (((1,), (1,)), ((), ())), preferred_element_type=jnp.float32
    )


def build_k(pattern_flat, wide_points, blocks):
    wide_rows = wide_points.shape[0]
    wide_points_t = wide_points.T
    wide_f = wide_points_t.astype(jnp.float32)
    sq_row = jnp.sum(wide_f * wide_f, axis=0, keepdims=True)
    return pl.pallas_call(
        build_kernel,
        out_shape=jax.ShapeDtypeStruct((blocks, BLK, WIDE * BLK), jnp.bfloat16),
        grid_spec=pltpu.PrefetchScalarGridSpec(
            num_scalar_prefetch=1,
            grid=(blocks,),
            in_specs=[
                pl.BlockSpec((wide_rows, F), lambda a, p: (0, 0)),
                pl.BlockSpec((F, wide_rows), lambda a, p: (0, 0)),
                pl.BlockSpec((1, wide_rows), lambda a, p: (0, 0)),
            ],
            out_specs=pl.BlockSpec((1, BLK, WIDE * BLK), lambda a, p: (a, 0, 0)),
        ),
        compiler_params=pltpu.CompilerParams(dimension_semantics=("arbitrary",)),
    )(pattern_flat, wide_points, wide_points_t, sq_row)


def apply_k(wide_vec, kmat):
    rows, wide_cols = wide_vec.shape
    blocks = kmat.shape[0]
    return pl.pallas_call(
        apply_kernel,
        out_shape=jax.ShapeDtypeStruct((rows, blocks * BLK), jnp.float32),
        grid=(blocks,),
        in_specs=[
            pl.BlockSpec((rows, wide_cols), lambda a: (0, 0)),
            pl.BlockSpec((1, BLK, WIDE * BLK), lambda a: (a, 0, 0)),
        ],
        out_specs=pl.BlockSpec((rows, BLK), lambda a: (0, a)),
        compiler_params=pltpu.CompilerParams(dimension_semantics=("arbitrary",)),
    )(wide_vec, kmat)


def reduction_steps(inner, outer, part_ref, stage1, stage2, local_sem, send1, recv1, send2, recv2):
    me = lax.axis_index("pts")
    row = lax.axis_index("rhs")
    zc = me // inner
    rc = me % inner

    def greet():
        barrier = pltpu.get_barrier_semaphore()

        def greet_inner(k, carry):
            peer = zc * inner + lax.rem(rc + k, inner)
            pl.semaphore_signal(barrier, inc=1, device_id=(peer, row), device_id_type=MESH)
            return carry

        def greet_outer(k, carry):
            peer = lax.rem(zc + k, outer) * inner + rc
            pl.semaphore_signal(barrier, inc=1, device_id=(peer, row), device_id_type=MESH)
            return carry

        lax.fori_loop(1, inner, greet_inner, 0)
        lax.fori_loop(1, outer, greet_outer, 0)

    def first(slot, other):
        return pltpu.make_async_remote_copy(
            src_ref=part_ref,
            dst_ref=stage1.at[slot],
            send_sem=send1.at[other],
            recv_sem=recv1.at[slot],
            device_id=(zc * inner + other, row),
            device_id_type=MESH,
        )

    def second(slot, other):
        return pltpu.make_async_remote_copy(
            src_ref=stage1,
            dst_ref=stage2.at[slot],
            send_sem=send2.at[other],
            recv_sem=recv2.at[slot],
            device_id=(other * inner + rc, row),
            device_id_type=MESH,
        )

    own1 = pltpu.make_async_copy(part_ref, stage1.at[rc], local_sem.at[0])
    own2 = pltpu.make_async_copy(stage1, stage2.at[zc], local_sem.at[1])

    def start_first():
        pl.semaphore_wait(pltpu.get_barrier_semaphore(), (inner - 1) + (outer - 1))
        own1.start()

        def send_first(k, carry):
            first(rc, lax.rem(rc + k, inner)).start()
            return carry

        lax.fori_loop(1, inner, send_first, 0)

    def start_second():
        def finish_first(k, carry):
            other = lax.rem(rc + k, inner)
            first(rc, other).wait_send()
            first(other, other).wait_recv()
            return carry

        lax.fori_loop(1, inner, finish_first, 0)
        own1.wait()
        own2.start()

        def send_second(k, carry):
            second(zc, lax.rem(zc + k, outer)).start()
            return carry

        lax.fori_loop(1, outer, send_second, 0)

    def finish():
        def finish_second(k, carry):
            other = lax.rem(zc + k, outer)
            second(zc, other).wait_send()
            second(other, other).wait_recv()
            return carry

        lax.fori_loop(1, outer, finish_second, 0)
        own2.wait()
        return jnp.sum(jnp.sum(stage2[...], axis=0), axis=0)

    return greet, start_first, start_second, finish


def apply_sum_kernel(inner, outer, v_ref, k_ref, part_ref, out_ref, sum_ref, *scratch):
    a = pl.program_id(0)
    last = pl.num_programs(0) - 1
    greet, start_first, start_second, finish = reduction_steps(inner, outer, part_ref, *scratch)

    @pl.when(a == 0)
    def _():
        greet()

    blocks = v_ref.shape[1] // BLK - 2 * REACH

    @pl.when(a == min(2, blocks - 1))
    def _():
        start_first()

    @pl.when(a == min(blocks // 2, blocks - 1))
    def _():
        start_second()

    start = pl.multiple_of(a * BLK, BLK)
    v_cat = v_ref[:, pl.ds(start, WIDE * BLK)]
    out_ref[...] = lax.dot_general(
        v_cat, k_ref[0], (((1,), (1,)), ((), ())), preferred_element_type=jnp.float32
    )

    @pl.when(a == last)
    def _():
        sum_ref[...] = finish()


def apply_sum(wide_vec, kmat, tile):
    rows, wide_cols = wide_vec.shape
    blocks = kmat.shape[0]
    count = lax.axis_size("pts")
    inner = 8 if count % 8 == 0 else count
    outer = count // inner
    return pl.pallas_call(
        functools.partial(apply_sum_kernel, inner, outer),
        out_shape=(
            jax.ShapeDtypeStruct((rows, blocks * BLK), jnp.float32),
            jax.ShapeDtypeStruct(tile.shape, jnp.float32),
        ),
        grid=(blocks,),
        in_specs=[
            pl.BlockSpec((rows, wide_cols), lambda a: (0, 0)),
            pl.BlockSpec((1, BLK, WIDE * BLK), lambda a: (a, 0, 0)),
            pl.BlockSpec(tile.shape, lambda a: (0, 0)),
        ],
        out_specs=(
            pl.BlockSpec((rows, BLK), lambda a: (0, a)),
            pl.BlockSpec(tile.shape, lambda a: (0, 0)),
        ),
        scratch_shapes=[
            pltpu.VMEM((inner,) + tile.shape, jnp.float32),
            pltpu.VMEM((outer, inner) + tile.shape, jnp.float32),
            pltpu.SemaphoreType.DMA((2,)),
            pltpu.SemaphoreType.DMA((inner,)),
            pltpu.SemaphoreType.DMA((inner,)),
            pltpu.SemaphoreType.DMA((outer,)),
            pltpu.SemaphoreType.DMA((outer,)),
        ],
        compiler_params=pltpu.CompilerParams(
            dimension_semantics=("arbitrary",), collective_id=0, has_side_effects=True
        ),
    )(wide_vec, kmat, tile)


def per_device(points, noise_var, right_side, pattern):
    local_rows = points.shape[0]
    block_count = local_rows // BLK
    rim_rows = REACH * BLK
    kernel_scale = 1.0 / (4 * BLK)
    wide_points = with_halo(points, "pts", 0, rim_rows)
    kmat = build_k(pattern.reshape(-1), wide_points, block_count)

    rhs_count = lax.axis_size("rhs")
    rhs_index = lax.axis_index("rhs")

    def apply_operator(vector):
        vec_low = vector.astype(jnp.bfloat16)
        wide_vec = with_halo(vec_low, "pts", 1, rim_rows)
        image_part = apply_k(wide_vec, kmat)
        return noise_var[None, :] * vector + kernel_scale * image_part

    def apply_and_total(vector, parts):
        tile = jnp.zeros((8, 128), jnp.float32)
        tile = lax.dynamic_update_slice(tile, parts, (0, 0))
        vec_low = vector.astype(jnp.bfloat16)
        wide_vec = with_halo(vec_low, "pts", 1, rim_rows)
        image_part, summed = apply_sum(wide_vec, kmat, tile)
        image = noise_var[None, :] * vector + kernel_scale * image_part
        return image, summed[: parts.shape[0], : parts.shape[1]]

    solution = jnp.zeros_like(right_side)
    residual = right_side
    res_image = apply_operator(residual)
    direction = jnp.zeros_like(right_side)
    dir_image = jnp.zeros_like(right_side)
    dir_twice = jnp.zeros_like(right_side)
    norm_prev = None
    step_prev = None
    for iteration in range(ITERS):
        square_image, sums = apply_and_total(
            res_image,
            jnp.stack([jnp.sum(residual * residual, axis=1), jnp.sum(res_image * residual, axis=1)]),
        )
        norm_now = sums[0][:, None]
        curvature = sums[1][:, None]
        if iteration == 0:
            step_len = norm_now / curvature
            direction = residual
            dir_image = res_image
            dir_twice = square_image
        else:
            mix_ratio = norm_now / norm_prev
            step_len = norm_now / (curvature - mix_ratio * norm_now / step_prev)
            direction = residual + mix_ratio * direction
            dir_image = res_image + mix_ratio * dir_image
            dir_twice = square_image + mix_ratio * dir_twice
        solution = solution + step_len * direction
        residual = residual - step_len * dir_image
        res_image = res_image - step_len * dir_twice
        norm_prev = norm_now
        step_prev = step_len
    return (solution, residual, res_image)


def solution(mesh):
    placed = (P("pts", None), P("pts"), P("rhs", "pts"), P("pts", None))
    return jax.shard_map(
        per_device,
        mesh=mesh,
        in_specs=placed,
        out_specs=(P("rhs", "pts"), P("rhs", "pts"), P("rhs", "pts")),
        check_vma=False,
    )
```

```python
import functools

import jax
import jax.numpy as jnp
from jax import lax
from jax.experimental import pallas as pl
from jax.experimental.pallas import tpu as pltpu
from jax.sharding import PartitionSpec as P

F = 32
BLK = 128
REACH = 16
ITERS = 2
WIDE = 33
WEXP = 18
MESH = pl.DeviceIdType.MESH


def with_halo(cells, axis, dim, width):
    count = lax.axis_size(axis)
    ends = count - 1
    head = lax.slice_in_dim(cells, 0, width, axis=dim)
    tail = lax.slice_in_dim(cells, cells.shape[dim] - width, cells.shape[dim], axis=dim)
    return jnp.concatenate(
        [
            lax.ppermute(tail, axis, [(i, (i + 1) % count) for i in range(ends)]),
            cells,
            lax.ppermute(head, axis, [((i + 1) % count, i) for i in range(ends)]),
        ],
        axis=dim,
    )


def profile_tile(left_m2, sq_left, right_t, sq_right):
    cross = jnp.dot(left_m2, right_t, preferred_element_type=jnp.float32)
    dist = jnp.maximum((sq_left + sq_right) + cross, 0.0)
    radius = jnp.sqrt(dist)
    base = jnp.maximum(1.0 - radius, 0.0)
    b2 = base * base
    b4 = b2 * b2
    b8 = b4 * b4
    b16 = b8 * b8
    return (b16 * b2) * (WEXP * radius + 1.0)


def build_kernel(pat_ref, pw_ref, pwt_ref, sqr_ref, k_ref, mirror):
    a = pl.program_id(0)
    blocks = pl.num_programs(0)
    start = pl.multiple_of((a + REACH) * BLK, BLK)
    left = pw_ref[pl.ds(start, BLK), :]
    left_f = left.astype(jnp.float32)
    sq_left = jnp.sum(left_f * left_f, axis=1, keepdims=True)
    left_m2 = left * jnp.asarray(-2.0, jnp.bfloat16)

    def body(o, carry):
        col = pl.multiple_of((a + o) * BLK, BLK)
        dst = pl.ds(pl.multiple_of(o * BLK, BLK), BLK)
        live = pat_ref[a * WIDE + o] != 0
        other = a + o - REACH
        lower = jnp.logical_and(other >= 0, other < a)
        upper = jnp.logical_and(other > a, other < blocks)

        @pl.when(jnp.logical_and(live, lower))
        def _():
            k_ref[0, :, dst] = mirror[a, other]

        @pl.when(jnp.logical_and(live, jnp.logical_not(lower)))
        def _():
            right_t = pwt_ref[:, pl.ds(col, BLK)]
            sq_right = sqr_ref[:, pl.ds(col, BLK)]
            value = profile_tile(left_m2, sq_left, right_t, sq_right)
            k_ref[0, :, dst] = value.astype(jnp.bfloat16)

            @pl.when(upper)
            def _():
                mirror[other, a] = value.T.astype(jnp.bfloat16)

        @pl.when(jnp.logical_not(live))
        def _():
            k_ref[0, :, dst] = jnp.zeros((BLK, BLK), jnp.bfloat16)

        return carry

    lax.fori_loop(0, WIDE, body, 0)


def apply_kernel(v_ref, k_ref, out_ref):
    a = pl.program_id(0)
    start = pl.multiple_of(a * BLK, BLK)
    v_cat = v_ref[:, pl.ds(start, WIDE * BLK)]
    out_ref[...] = lax.dot_general(
        v_cat, k_ref[0], (((1,), (1,)), ((), ())), preferred_element_type=jnp.float32
    )


def build_k(pattern_flat, wide_points, blocks):
    wide_rows = wide_points.shape[0]
    wide_points_t = wide_points.T
    wide_f = wide_points_t.astype(jnp.float32)
    sq_row = jnp.sum(wide_f * wide_f, axis=0, keepdims=True)
    return pl.pallas_call(
        build_kernel,
        out_shape=jax.ShapeDtypeStruct((blocks, BLK, WIDE * BLK), jnp.bfloat16),
        grid_spec=pltpu.PrefetchScalarGridSpec(
            num_scalar_prefetch=1,
            grid=(blocks,),
            in_specs=[
                pl.BlockSpec((wide_rows, F), lambda a, p: (0, 0)),
                pl.BlockSpec((F, wide_rows), lambda a, p: (0, 0)),
                pl.BlockSpec((1, wide_rows), lambda a, p: (0, 0)),
            ],
            out_specs=pl.BlockSpec((1, BLK, WIDE * BLK), lambda a, p: (a, 0, 0)),
            scratch_shapes=[pltpu.VMEM((blocks, blocks, BLK, BLK), jnp.bfloat16)],
        ),
        compiler_params=pltpu.CompilerParams(dimension_semantics=("arbitrary",)),
    )(pattern_flat, wide_points, wide_points_t, sq_row)


def apply_k(wide_vec, kmat):
    rows, wide_cols = wide_vec.shape
    blocks = kmat.shape[0]
    return pl.pallas_call(
        apply_kernel,
        out_shape=jax.ShapeDtypeStruct((rows, blocks * BLK), jnp.float32),
        grid=(blocks,),
        in_specs=[
            pl.BlockSpec((rows, wide_cols), lambda a: (0, 0)),
            pl.BlockSpec((1, BLK, WIDE * BLK), lambda a: (a, 0, 0)),
        ],
        out_specs=pl.BlockSpec((rows, BLK), lambda a: (0, a)),
        compiler_params=pltpu.CompilerParams(dimension_semantics=("arbitrary",)),
    )(wide_vec, kmat)


def reduction_steps(inner, outer, part_ref, stage1, stage2, local_sem, send1, recv1, send2, recv2):
    me = lax.axis_index("pts")
    row = lax.axis_index("rhs")
    zc = me // inner
    rc = me % inner

    def greet():
        barrier = pltpu.get_barrier_semaphore()

        def greet_inner(k, carry):
            peer = zc * inner + lax.rem(rc + k, inner)
            pl.semaphore_signal(barrier, inc=1, device_id=(peer, row), device_id_type=MESH)
            return carry

        def greet_outer(k, carry):
            peer = lax.rem(zc + k, outer) * inner + rc
            pl.semaphore_signal(barrier, inc=1, device_id=(peer, row), device_id_type=MESH)
            return carry

        lax.fori_loop(1, inner, greet_inner, 0)
        lax.fori_loop(1, outer, greet_outer, 0)

    def first(slot, other):
        return pltpu.make_async_remote_copy(
            src_ref=part_ref,
            dst_ref=stage1.at[slot],
            send_sem=send1.at[other],
            recv_sem=recv1.at[slot],
            device_id=(zc * inner + other, row),
            device_id_type=MESH,
        )

    def second(slot, other):
        return pltpu.make_async_remote_copy(
            src_ref=stage1,
            dst_ref=stage2.at[slot],
            send_sem=send2.at[other],
            recv_sem=recv2.at[slot],
            device_id=(other * inner + rc, row),
            device_id_type=MESH,
        )

    own1 = pltpu.make_async_copy(part_ref, stage1.at[rc], local_sem.at[0])
    own2 = pltpu.make_async_copy(stage1, stage2.at[zc], local_sem.at[1])

    def start_first():
        pl.semaphore_wait(pltpu.get_barrier_semaphore(), (inner - 1) + (outer - 1))
        own1.start()

        def send_first(k, carry):
            first(rc, lax.rem(rc + k, inner)).start()
            return carry

        lax.fori_loop(1, inner, send_first, 0)

    def start_second():
        def finish_first(k, carry):
            other = lax.rem(rc + k, inner)
            first(rc, other).wait_send()
            first(other, other).wait_recv()
            return carry

        lax.fori_loop(1, inner, finish_first, 0)
        own1.wait()
        own2.start()

        def send_second(k, carry):
            second(zc, lax.rem(zc + k, outer)).start()
            return carry

        lax.fori_loop(1, outer, send_second, 0)

    def finish():
        def finish_second(k, carry):
            other = lax.rem(zc + k, outer)
            second(zc, other).wait_send()
            second(other, other).wait_recv()
            return carry

        lax.fori_loop(1, outer, finish_second, 0)
        own2.wait()
        return jnp.sum(jnp.sum(stage2[...], axis=0), axis=0)

    return greet, start_first, start_second, finish


def apply_sum_kernel(inner, outer, v_ref, k_ref, part_ref, out_ref, sum_ref, *scratch):
    a = pl.program_id(0)
    last = pl.num_programs(0) - 1
    greet, start_first, start_second, finish = reduction_steps(inner, outer, part_ref, *scratch)

    @pl.when(a == 0)
    def _():
        greet()

    blocks = v_ref.shape[1] // BLK - 2 * REACH

    @pl.when(a == min(2, blocks - 1))
    def _():
        start_first()

    @pl.when(a == min(blocks // 2, blocks - 1))
    def _():
        start_second()

    start = pl.multiple_of(a * BLK, BLK)
    v_cat = v_ref[:, pl.ds(start, WIDE * BLK)]
    out_ref[...] = lax.dot_general(
        v_cat, k_ref[0], (((1,), (1,)), ((), ())), preferred_element_type=jnp.float32
    )

    @pl.when(a == last)
    def _():
        sum_ref[...] = finish()


def apply_sum(wide_vec, kmat, tile):
    rows, wide_cols = wide_vec.shape
    blocks = kmat.shape[0]
    count = lax.axis_size("pts")
    inner = 8 if count % 8 == 0 else count
    outer = count // inner
    return pl.pallas_call(
        functools.partial(apply_sum_kernel, inner, outer),
        out_shape=(
            jax.ShapeDtypeStruct((rows, blocks * BLK), jnp.float32),
            jax.ShapeDtypeStruct(tile.shape, jnp.float32),
        ),
        grid=(blocks,),
        in_specs=[
            pl.BlockSpec((rows, wide_cols), lambda a: (0, 0)),
            pl.BlockSpec((1, BLK, WIDE * BLK), lambda a: (a, 0, 0)),
            pl.BlockSpec(tile.shape, lambda a: (0, 0)),
        ],
        out_specs=(
            pl.BlockSpec((rows, BLK), lambda a: (0, a)),
            pl.BlockSpec(tile.shape, lambda a: (0, 0)),
        ),
        scratch_shapes=[
            pltpu.VMEM((inner,) + tile.shape, jnp.float32),
            pltpu.VMEM((outer, inner) + tile.shape, jnp.float32),
            pltpu.SemaphoreType.DMA((2,)),
            pltpu.SemaphoreType.DMA((inner,)),
            pltpu.SemaphoreType.DMA((inner,)),
            pltpu.SemaphoreType.DMA((outer,)),
            pltpu.SemaphoreType.DMA((outer,)),
        ],
        compiler_params=pltpu.CompilerParams(
            dimension_semantics=("arbitrary",), collective_id=0, has_side_effects=True
        ),
    )(wide_vec, kmat, tile)


def per_device(points, noise_var, right_side, pattern):
    local_rows = points.shape[0]
    block_count = local_rows // BLK
    rim_rows = REACH * BLK
    kernel_scale = 1.0 / (4 * BLK)
    wide_points = with_halo(points, "pts", 0, rim_rows)
    kmat = build_k(pattern.reshape(-1), wide_points, block_count)

    rhs_count = lax.axis_size("rhs")
    rhs_index = lax.axis_index("rhs")

    def apply_operator(vector):
        vec_low = vector.astype(jnp.bfloat16)
        wide_vec = with_halo(vec_low, "pts", 1, rim_rows)
        image_part = apply_k(wide_vec, kmat)
        return noise_var[None, :] * vector + kernel_scale * image_part

    def apply_and_total(vector, parts):
        tile = jnp.zeros((8, 128), jnp.float32)
        tile = lax.dynamic_update_slice(tile, parts, (0, 0))
        vec_low = vector.astype(jnp.bfloat16)
        wide_vec = with_halo(vec_low, "pts", 1, rim_rows)
        image_part, summed = apply_sum(wide_vec, kmat, tile)
        image = noise_var[None, :] * vector + kernel_scale * image_part
        return image, summed[: parts.shape[0], : parts.shape[1]]

    solution = jnp.zeros_like(right_side)
    residual = right_side
    res_image = apply_operator(residual)
    direction = jnp.zeros_like(right_side)
    dir_image = jnp.zeros_like(right_side)
    dir_twice = jnp.zeros_like(right_side)
    norm_prev = None
    step_prev = None
    for iteration in range(ITERS):
        square_image, sums = apply_and_total(
            res_image,
            jnp.stack([jnp.sum(residual * residual, axis=1), jnp.sum(res_image * residual, axis=1)]),
        )
        norm_now = sums[0][:, None]
        curvature = sums[1][:, None]
        if iteration == 0:
            step_len = norm_now / curvature
            direction = residual
            dir_image = res_image
            dir_twice = square_image
        else:
            mix_ratio = norm_now / norm_prev
            step_len = norm_now / (curvature - mix_ratio * norm_now / step_prev)
            direction = residual + mix_ratio * direction
            dir_image = res_image + mix_ratio * dir_image
            dir_twice = square_image + mix_ratio * dir_twice
        solution = solution + step_len * direction
        residual = residual - step_len * dir_image
        res_image = res_image - step_len * dir_twice
        norm_prev = norm_now
        step_prev = step_len
    return (solution, residual, res_image)


def solution(mesh):
    placed = (P("pts", None), P("pts"), P("rhs", "pts"), P("pts", None))
    return jax.shard_map(
        per_device,
        mesh=mesh,
        in_specs=placed,
        out_specs=(P("rhs", "pts"), P("rhs", "pts"), P("rhs", "pts")),
        check_vma=False,
    )
```

```python
import functools

import jax
import jax.numpy as jnp
from jax import lax
from jax.experimental import pallas as pl
from jax.experimental.pallas import tpu as pltpu
from jax.sharding import PartitionSpec as P

F = 32
BLK = 128
REACH = 16
ITERS = 2
WIDE = 33
WEXP = 18
MESH = pl.DeviceIdType.MESH


def with_halo(cells, axis, dim, width):
    count = lax.axis_size(axis)
    ends = count - 1
    head = lax.slice_in_dim(cells, 0, width, axis=dim)
    tail = lax.slice_in_dim(cells, cells.shape[dim] - width, cells.shape[dim], axis=dim)
    return jnp.concatenate(
        [
            lax.ppermute(tail, axis, [(i, (i + 1) % count) for i in range(ends)]),
            cells,
            lax.ppermute(head, axis, [((i + 1) % count, i) for i in range(ends)]),
        ],
        axis=dim,
    )


def profile_tile(sq_left, sq_right, cross):
    dist = jnp.maximum((sq_left + sq_right) + cross, 0.0)
    radius = jnp.sqrt(dist)
    base = jnp.maximum(1.0 - radius, 0.0)
    b2 = base * base
    b4 = b2 * b2
    b8 = b4 * b4
    b16 = b8 * b8
    return (b16 * b2) * (WEXP * radius + 1.0)


def build_kernel(pat_ref, pw_ref, pwt_ref, sqr_ref, k_ref, mirror, cross_ref):
    a = pl.program_id(0)
    blocks = pl.num_programs(0)
    start = pl.multiple_of((a + REACH) * BLK, BLK)
    left = pw_ref[pl.ds(start, BLK), :]
    left_f = left.astype(jnp.float32)
    sq_left = jnp.sum(left_f * left_f, axis=1, keepdims=True)
    left_m2 = left * jnp.asarray(-2.0, jnp.bfloat16)
    window = pwt_ref[:, pl.ds(pl.multiple_of(a * BLK, BLK), WIDE * BLK)]
    cross_ref[...] = jnp.dot(left_m2, window, preferred_element_type=jnp.float32)

    def body(o, carry):
        col = pl.multiple_of((a + o) * BLK, BLK)
        dst = pl.ds(pl.multiple_of(o * BLK, BLK), BLK)
        live = pat_ref[a * WIDE + o] != 0
        other = a + o - REACH
        lower = jnp.logical_and(other >= 0, other < a)
        upper = jnp.logical_and(other > a, other < blocks)

        @pl.when(jnp.logical_and(live, lower))
        def _():
            k_ref[0, :, dst] = mirror[a, other]

        @pl.when(jnp.logical_and(live, jnp.logical_not(lower)))
        def _():
            sq_right = sqr_ref[:, pl.ds(col, BLK)]
            value = profile_tile(sq_left, sq_right, cross_ref[:, dst])
            k_ref[0, :, dst] = value.astype(jnp.bfloat16)

            @pl.when(upper)
            def _():
                mirror[other, a] = value.T.astype(jnp.bfloat16)

        @pl.when(jnp.logical_not(live))
        def _():
            k_ref[0, :, dst] = jnp.zeros((BLK, BLK), jnp.bfloat16)

        return carry

    lax.fori_loop(0, WIDE, body, 0)


def apply_kernel(v_ref, k_ref, out_ref):
    a = pl.program_id(0)
    start = pl.multiple_of(a * BLK, BLK)
    v_cat = v_ref[:, pl.ds(start, WIDE * BLK)]
    out_ref[...] = lax.dot_general(
        v_cat, k_ref[0], (((1,), (1,)), ((), ())), preferred_element_type=jnp.float32
    )


def build_k(pattern_flat, wide_points, blocks):
    wide_rows = wide_points.shape[0]
    wide_points_t = wide_points.T
    wide_f = wide_points_t.astype(jnp.float32)
    sq_row = jnp.sum(wide_f * wide_f, axis=0, keepdims=True)
    return pl.pallas_call(
        build_kernel,
        out_shape=jax.ShapeDtypeStruct((blocks, BLK, WIDE * BLK), jnp.bfloat16),
        grid_spec=pltpu.PrefetchScalarGridSpec(
            num_scalar_prefetch=1,
            grid=(blocks,),
            in_specs=[
                pl.BlockSpec((wide_rows, F), lambda a, p: (0, 0)),
                pl.BlockSpec((F, wide_rows), lambda a, p: (0, 0)),
                pl.BlockSpec((1, wide_rows), lambda a, p: (0, 0)),
            ],
            out_specs=pl.BlockSpec((1, BLK, WIDE * BLK), lambda a, p: (a, 0, 0)),
            scratch_shapes=[
                pltpu.VMEM((blocks, blocks, BLK, BLK), jnp.bfloat16),
                pltpu.VMEM((BLK, WIDE * BLK), jnp.float32),
            ],
        ),
        compiler_params=pltpu.CompilerParams(dimension_semantics=("arbitrary",)),
    )(pattern_flat, wide_points, wide_points_t, sq_row)


def apply_k(wide_vec, kmat):
    rows, wide_cols = wide_vec.shape
    blocks = kmat.shape[0]
    return pl.pallas_call(
        apply_kernel,
        out_shape=jax.ShapeDtypeStruct((rows, blocks * BLK), jnp.float32),
        grid=(blocks,),
        in_specs=[
            pl.BlockSpec((rows, wide_cols), lambda a: (0, 0)),
            pl.BlockSpec((1, BLK, WIDE * BLK), lambda a: (a, 0, 0)),
        ],
        out_specs=pl.BlockSpec((rows, BLK), lambda a: (0, a)),
        compiler_params=pltpu.CompilerParams(dimension_semantics=("arbitrary",)),
    )(wide_vec, kmat)


def reduction_steps(inner, outer, part_ref, stage1, stage2, local_sem, send1, recv1, send2, recv2):
    me = lax.axis_index("pts")
    row = lax.axis_index("rhs")
    zc = me // inner
    rc = me % inner

    def greet():
        barrier = pltpu.get_barrier_semaphore()

        def greet_inner(k, carry):
            peer = zc * inner + lax.rem(rc + k, inner)
            pl.semaphore_signal(barrier, inc=1, device_id=(peer, row), device_id_type=MESH)
            return carry

        def greet_outer(k, carry):
            peer = lax.rem(zc + k, outer) * inner + rc
            pl.semaphore_signal(barrier, inc=1, device_id=(peer, row), device_id_type=MESH)
            return carry

        lax.fori_loop(1, inner, greet_inner, 0)
        lax.fori_loop(1, outer, greet_outer, 0)

    def first(slot, other):
        return pltpu.make_async_remote_copy(
            src_ref=part_ref,
            dst_ref=stage1.at[slot],
            send_sem=send1.at[other],
            recv_sem=recv1.at[slot],
            device_id=(zc * inner + other, row),
            device_id_type=MESH,
        )

    def second(slot, other):
        return pltpu.make_async_remote_copy(
            src_ref=stage1,
            dst_ref=stage2.at[slot],
            send_sem=send2.at[other],
            recv_sem=recv2.at[slot],
            device_id=(other * inner + rc, row),
            device_id_type=MESH,
        )

    own1 = pltpu.make_async_copy(part_ref, stage1.at[rc], local_sem.at[0])
    own2 = pltpu.make_async_copy(stage1, stage2.at[zc], local_sem.at[1])

    def start_first():
        pl.semaphore_wait(pltpu.get_barrier_semaphore(), (inner - 1) + (outer - 1))
        own1.start()

        def send_first(k, carry):
            first(rc, lax.rem(rc + k, inner)).start()
            return carry

        lax.fori_loop(1, inner, send_first, 0)

    def start_second():
        def finish_first(k, carry):
            other = lax.rem(rc + k, inner)
            first(rc, other).wait_send()
            first(other, other).wait_recv()
            return carry

        lax.fori_loop(1, inner, finish_first, 0)
        own1.wait()
        own2.start()

        def send_second(k, carry):
            second(zc, lax.rem(zc + k, outer)).start()
            return carry

        lax.fori_loop(1, outer, send_second, 0)

    def finish():
        def finish_second(k, carry):
            other = lax.rem(zc + k, outer)
            second(zc, other).wait_send()
            second(other, other).wait_recv()
            return carry

        lax.fori_loop(1, outer, finish_second, 0)
        own2.wait()
        return jnp.sum(jnp.sum(stage2[...], axis=0), axis=0)

    return greet, start_first, start_second, finish


def apply_sum_kernel(inner, outer, v_ref, k_ref, part_ref, out_ref, sum_ref, *scratch):
    a = pl.program_id(0)
    last = pl.num_programs(0) - 1
    greet, start_first, start_second, finish = reduction_steps(inner, outer, part_ref, *scratch)

    @pl.when(a == 0)
    def _():
        greet()

    blocks = v_ref.shape[1] // BLK - 2 * REACH

    @pl.when(a == min(2, blocks - 1))
    def _():
        start_first()

    @pl.when(a == min(blocks // 2, blocks - 1))
    def _():
        start_second()

    start = pl.multiple_of(a * BLK, BLK)
    v_cat = v_ref[:, pl.ds(start, WIDE * BLK)]
    out_ref[...] = lax.dot_general(
        v_cat, k_ref[0], (((1,), (1,)), ((), ())), preferred_element_type=jnp.float32
    )

    @pl.when(a == last)
    def _():
        sum_ref[...] = finish()


def apply_sum(wide_vec, kmat, tile):
    rows, wide_cols = wide_vec.shape
    blocks = kmat.shape[0]
    count = lax.axis_size("pts")
    inner = 8 if count % 8 == 0 else count
    outer = count // inner
    return pl.pallas_call(
        functools.partial(apply_sum_kernel, inner, outer),
        out_shape=(
            jax.ShapeDtypeStruct((rows, blocks * BLK), jnp.float32),
            jax.ShapeDtypeStruct(tile.shape, jnp.float32),
        ),
        grid=(blocks,),
        in_specs=[
            pl.BlockSpec((rows, wide_cols), lambda a: (0, 0)),
            pl.BlockSpec((1, BLK, WIDE * BLK), lambda a: (a, 0, 0)),
            pl.BlockSpec(tile.shape, lambda a: (0, 0)),
        ],
        out_specs=(
            pl.BlockSpec((rows, BLK), lambda a: (0, a)),
            pl.BlockSpec(tile.shape, lambda a: (0, 0)),
        ),
        scratch_shapes=[
            pltpu.VMEM((inner,) + tile.shape, jnp.float32),
            pltpu.VMEM((outer, inner) + tile.shape, jnp.float32),
            pltpu.SemaphoreType.DMA((2,)),
            pltpu.SemaphoreType.DMA((inner,)),
            pltpu.SemaphoreType.DMA((inner,)),
            pltpu.SemaphoreType.DMA((outer,)),
            pltpu.SemaphoreType.DMA((outer,)),
        ],
        compiler_params=pltpu.CompilerParams(
            dimension_semantics=("arbitrary",), collective_id=0, has_side_effects=True
        ),
    )(wide_vec, kmat, tile)


def per_device(points, noise_var, right_side, pattern):
    local_rows = points.shape[0]
    block_count = local_rows // BLK
    rim_rows = REACH * BLK
    kernel_scale = 1.0 / (4 * BLK)
    wide_points = with_halo(points, "pts", 0, rim_rows)
    kmat = build_k(pattern.reshape(-1), wide_points, block_count)

    rhs_count = lax.axis_size("rhs")
    rhs_index = lax.axis_index("rhs")

    def apply_operator(vector):
        vec_low = vector.astype(jnp.bfloat16)
        wide_vec = with_halo(vec_low, "pts", 1, rim_rows)
        image_part = apply_k(wide_vec, kmat)
        return noise_var[None, :] * vector + kernel_scale * image_part

    def apply_and_total(vector, parts):
        tile = jnp.zeros((8, 128), jnp.float32)
        tile = lax.dynamic_update_slice(tile, parts, (0, 0))
        vec_low = vector.astype(jnp.bfloat16)
        wide_vec = with_halo(vec_low, "pts", 1, rim_rows)
        image_part, summed = apply_sum(wide_vec, kmat, tile)
        image = noise_var[None, :] * vector + kernel_scale * image_part
        return image, summed[: parts.shape[0], : parts.shape[1]]

    solution = jnp.zeros_like(right_side)
    residual = right_side
    res_image = apply_operator(residual)
    direction = jnp.zeros_like(right_side)
    dir_image = jnp.zeros_like(right_side)
    dir_twice = jnp.zeros_like(right_side)
    norm_prev = None
    step_prev = None
    for iteration in range(ITERS):
        square_image, sums = apply_and_total(
            res_image,
            jnp.stack([jnp.sum(residual * residual, axis=1), jnp.sum(res_image * residual, axis=1)]),
        )
        norm_now = sums[0][:, None]
        curvature = sums[1][:, None]
        if iteration == 0:
            step_len = norm_now / curvature
            direction = residual
            dir_image = res_image
            dir_twice = square_image
        else:
            mix_ratio = norm_now / norm_prev
            step_len = norm_now / (curvature - mix_ratio * norm_now / step_prev)
            direction = residual + mix_ratio * direction
            dir_image = res_image + mix_ratio * dir_image
            dir_twice = square_image + mix_ratio * dir_twice
        solution = solution + step_len * direction
        residual = residual - step_len * dir_image
        res_image = res_image - step_len * dir_twice
        norm_prev = norm_now
        step_prev = step_len
    return (solution, residual, res_image)


def solution(mesh):
    placed = (P("pts", None), P("pts"), P("rhs", "pts"), P("pts", None))
    return jax.shard_map(
        per_device,
        mesh=mesh,
        in_specs=placed,
        out_specs=(P("rhs", "pts"), P("rhs", "pts"), P("rhs", "pts")),
        check_vma=False,
    )
```

```python
import functools

import jax
import jax.numpy as jnp
from jax import lax
from jax.experimental import pallas as pl
from jax.experimental.pallas import tpu as pltpu
from jax.sharding import PartitionSpec as P

F = 32
BLK = 128
REACH = 16
ITERS = 2
WIDE = 33
WEXP = 18
MESH = pl.DeviceIdType.MESH


def with_halo(cells, axis, dim, width):
    count = lax.axis_size(axis)
    ends = count - 1
    head = lax.slice_in_dim(cells, 0, width, axis=dim)
    tail = lax.slice_in_dim(cells, cells.shape[dim] - width, cells.shape[dim], axis=dim)
    return jnp.concatenate(
        [
            lax.ppermute(tail, axis, [(i, (i + 1) % count) for i in range(ends)]),
            cells,
            lax.ppermute(head, axis, [((i + 1) % count, i) for i in range(ends)]),
        ],
        axis=dim,
    )


def profile_tile(sq_left, sq_right, cross):
    dist = jnp.maximum((sq_left + sq_right) + cross, 0.0)
    radius = jnp.sqrt(dist)
    base = jnp.maximum(1.0 - radius, 0.0)
    b2 = base * base
    b4 = b2 * b2
    b8 = b4 * b4
    b16 = b8 * b8
    return (b16 * b2) * (WEXP * radius + 1.0)


def build_kernel(pat_ref, pw_ref, pwt_ref, sqr_ref, k_ref, mirror, cross_ref):
    a = pl.program_id(0)
    blocks = pl.num_programs(0)
    start = pl.multiple_of((a + REACH) * BLK, BLK)
    left = pw_ref[pl.ds(start, BLK), :]
    left_f = left.astype(jnp.float32)
    sq_left = jnp.sum(left_f * left_f, axis=1, keepdims=True)
    left_m2 = left * jnp.asarray(-2.0, jnp.bfloat16)
    window = pwt_ref[:, pl.ds(pl.multiple_of(a * BLK, BLK), WIDE * BLK)]
    cross_ref[...] = jnp.dot(left_m2, window, preferred_element_type=jnp.float32)

    def body(o, carry):
        col = pl.multiple_of((a + o) * BLK, BLK)
        dst = pl.ds(pl.multiple_of(o * BLK, BLK), BLK)
        live = pat_ref[a * WIDE + o] != 0
        other = a + o - REACH
        lower = jnp.logical_and(other >= 0, other < a)
        upper = jnp.logical_and(other > a, other < blocks)

        @pl.when(jnp.logical_and(live, lower))
        def _():
            k_ref[0, :, dst] = mirror[a, other]

        @pl.when(jnp.logical_and(live, jnp.logical_not(lower)))
        def _():
            sq_right = sqr_ref[:, pl.ds(col, BLK)]
            value = profile_tile(sq_left, sq_right, cross_ref[:, dst])
            k_ref[0, :, dst] = value.astype(jnp.bfloat16)

            @pl.when(upper)
            def _():
                mirror[other, a] = value.T.astype(jnp.bfloat16)

        @pl.when(jnp.logical_not(live))
        def _():
            k_ref[0, :, dst] = jnp.zeros((BLK, BLK), jnp.bfloat16)

        return carry

    lax.fori_loop(0, WIDE, body, 0)


def apply_kernel(v_ref, k_ref, out_ref):
    a = pl.program_id(0)
    start = pl.multiple_of(a * BLK, BLK)
    v_cat = v_ref[:, pl.ds(start, WIDE * BLK)]
    out_ref[...] = lax.dot_general(
        v_cat, k_ref[0], (((1,), (1,)), ((), ())), preferred_element_type=jnp.float32
    )


def build_k(pattern_flat, wide_points, blocks):
    wide_rows = wide_points.shape[0]
    wide_points_t = wide_points.T
    wide_f = wide_points_t.astype(jnp.float32)
    sq_row = jnp.sum(wide_f * wide_f, axis=0, keepdims=True)
    return pl.pallas_call(
        build_kernel,
        out_shape=jax.ShapeDtypeStruct((blocks, BLK, WIDE * BLK), jnp.bfloat16),
        grid_spec=pltpu.PrefetchScalarGridSpec(
            num_scalar_prefetch=1,
            grid=(blocks,),
            in_specs=[
                pl.BlockSpec((wide_rows, F), lambda a, p: (0, 0)),
                pl.BlockSpec((F, wide_rows), lambda a, p: (0, 0)),
                pl.BlockSpec((1, wide_rows), lambda a, p: (0, 0)),
            ],
            out_specs=pl.BlockSpec((1, BLK, WIDE * BLK), lambda a, p: (a, 0, 0)),
            scratch_shapes=[
                pltpu.VMEM((blocks, blocks, BLK, BLK), jnp.bfloat16),
                pltpu.VMEM((BLK, WIDE * BLK), jnp.float32),
            ],
        ),
        compiler_params=pltpu.CompilerParams(dimension_semantics=("arbitrary",)),
    )(pattern_flat, wide_points, wide_points_t, sq_row)


def apply_k(wide_vec, kmat):
    rows, wide_cols = wide_vec.shape
    blocks = kmat.shape[0]
    return pl.pallas_call(
        apply_kernel,
        out_shape=jax.ShapeDtypeStruct((rows, blocks * BLK), jnp.float32),
        grid=(blocks,),
        in_specs=[
            pl.BlockSpec((rows, wide_cols), lambda a: (0, 0)),
            pl.BlockSpec((1, BLK, WIDE * BLK), lambda a: (a, 0, 0)),
        ],
        out_specs=pl.BlockSpec((rows, BLK), lambda a: (0, a)),
        compiler_params=pltpu.CompilerParams(dimension_semantics=("arbitrary",)),
    )(wide_vec, kmat)


def reduction_steps(inner, outer, part_ref, stage1, stage2, local_sem, send1, recv1, send2, recv2):
    me = lax.axis_index("pts")
    row = lax.axis_index("rhs")
    zc = me // inner
    rc = me % inner

    def greet():
        barrier = pltpu.get_barrier_semaphore()

        def greet_inner(k, carry):
            peer = zc * inner + lax.rem(rc + k, inner)
            pl.semaphore_signal(barrier, inc=1, device_id=(peer, row), device_id_type=MESH)
            return carry

        def greet_outer(k, carry):
            peer = lax.rem(zc + k, outer) * inner + rc
            pl.semaphore_signal(barrier, inc=1, device_id=(peer, row), device_id_type=MESH)
            return carry

        lax.fori_loop(1, inner, greet_inner, 0)
        lax.fori_loop(1, outer, greet_outer, 0)

    def first(slot, other):
        return pltpu.make_async_remote_copy(
            src_ref=part_ref,
            dst_ref=stage1.at[slot],
            send_sem=send1.at[other],
            recv_sem=recv1.at[slot],
            device_id=(zc * inner + other, row),
            device_id_type=MESH,
        )

    def second(slot, other):
        return pltpu.make_async_remote_copy(
            src_ref=stage1,
            dst_ref=stage2.at[slot],
            send_sem=send2.at[other],
            recv_sem=recv2.at[slot],
            device_id=(other * inner + rc, row),
            device_id_type=MESH,
        )

    own1 = pltpu.make_async_copy(part_ref, stage1.at[rc], local_sem.at[0])
    own2 = pltpu.make_async_copy(stage1, stage2.at[zc], local_sem.at[1])

    def start_first():
        pl.semaphore_wait(pltpu.get_barrier_semaphore(), (inner - 1) + (outer - 1))
        own1.start()

        def send_first(k, carry):
            first(rc, lax.rem(rc + k, inner)).start()
            return carry

        lax.fori_loop(1, inner, send_first, 0)

    def start_second():
        def finish_first(k, carry):
            other = lax.rem(rc + k, inner)
            first(rc, other).wait_send()
            first(other, other).wait_recv()
            return carry

        lax.fori_loop(1, inner, finish_first, 0)
        own1.wait()
        own2.start()

        def send_second(k, carry):
            second(zc, lax.rem(zc + k, outer)).start()
            return carry

        lax.fori_loop(1, outer, send_second, 0)

    def finish():
        def finish_second(k, carry):
            other = lax.rem(zc + k, outer)
            second(zc, other).wait_send()
            second(other, other).wait_recv()
            return carry

        lax.fori_loop(1, outer, finish_second, 0)
        own2.wait()
        return jnp.sum(jnp.sum(stage2[...], axis=0), axis=0)

    return greet, start_first, start_second, finish


def apply_sum_kernel(inner, outer, v_ref, k_ref, part_ref, out_ref, sum_ref, *scratch):
    a = pl.program_id(0)
    last = pl.num_programs(0) - 1
    greet, start_first, start_second, finish = reduction_steps(inner, outer, part_ref, *scratch)

    @pl.when(a == 0)
    def _():
        greet()
        start_first()

    blocks = v_ref.shape[1] // BLK - 2 * REACH

    @pl.when(a == min(blocks // 2 - 2, blocks - 1))
    def _():
        start_second()

    start = pl.multiple_of(a * BLK, BLK)
    v_cat = v_ref[:, pl.ds(start, WIDE * BLK)]
    out_ref[...] = lax.dot_general(
        v_cat, k_ref[0], (((1,), (1,)), ((), ())), preferred_element_type=jnp.float32
    )

    @pl.when(a == last)
    def _():
        sum_ref[...] = finish()


def apply_sum(wide_vec, kmat, tile):
    rows, wide_cols = wide_vec.shape
    blocks = kmat.shape[0]
    count = lax.axis_size("pts")
    inner = 8 if count % 8 == 0 else count
    outer = count // inner
    return pl.pallas_call(
        functools.partial(apply_sum_kernel, inner, outer),
        out_shape=(
            jax.ShapeDtypeStruct((rows, blocks * BLK), jnp.float32),
            jax.ShapeDtypeStruct(tile.shape, jnp.float32),
        ),
        grid=(blocks,),
        in_specs=[
            pl.BlockSpec((rows, wide_cols), lambda a: (0, 0)),
            pl.BlockSpec((1, BLK, WIDE * BLK), lambda a: (a, 0, 0)),
            pl.BlockSpec(tile.shape, lambda a: (0, 0)),
        ],
        out_specs=(
            pl.BlockSpec((rows, BLK), lambda a: (0, a)),
            pl.BlockSpec(tile.shape, lambda a: (0, 0)),
        ),
        scratch_shapes=[
            pltpu.VMEM((inner,) + tile.shape, jnp.float32),
            pltpu.VMEM((outer, inner) + tile.shape, jnp.float32),
            pltpu.SemaphoreType.DMA((2,)),
            pltpu.SemaphoreType.DMA((inner,)),
            pltpu.SemaphoreType.DMA((inner,)),
            pltpu.SemaphoreType.DMA((outer,)),
            pltpu.SemaphoreType.DMA((outer,)),
        ],
        compiler_params=pltpu.CompilerParams(
            dimension_semantics=("arbitrary",), collective_id=0, has_side_effects=True
        ),
    )(wide_vec, kmat, tile)


def per_device(points, noise_var, right_side, pattern):
    local_rows = points.shape[0]
    block_count = local_rows // BLK
    rim_rows = REACH * BLK
    kernel_scale = 1.0 / (4 * BLK)
    first_low = right_side.astype(jnp.bfloat16)
    point_rows = points.size // 128
    packed = jnp.concatenate([points.reshape(point_rows, 128), first_low.reshape(-1, 128)], axis=0)
    count = lax.axis_size("pts")
    from_left = lax.ppermute(packed, "pts", [(i, i + 1) for i in range(count - 1)])
    from_right = lax.ppermute(packed, "pts", [(i + 1, i) for i in range(count - 1)])
    wide_points = jnp.concatenate(
        [from_left[:point_rows].reshape(points.shape), points, from_right[:point_rows].reshape(points.shape)], axis=0
    )
    first_wide = jnp.concatenate(
        [
            from_left[point_rows:].reshape(first_low.shape),
            first_low,
            from_right[point_rows:].reshape(first_low.shape),
        ],
        axis=1,
    )
    kmat = build_k(pattern.reshape(-1), wide_points, block_count)

    rhs_count = lax.axis_size("rhs")
    rhs_index = lax.axis_index("rhs")

    def apply_operator(vector):
        vec_low = vector.astype(jnp.bfloat16)
        wide_vec = with_halo(vec_low, "pts", 1, rim_rows)
        image_part = apply_k(wide_vec, kmat)
        return noise_var[None, :] * vector + kernel_scale * image_part

    def apply_and_total(vector, parts):
        tile = jnp.zeros((8, 128), jnp.float32)
        tile = lax.dynamic_update_slice(tile, parts, (0, 0))
        vec_low = vector.astype(jnp.bfloat16)
        wide_vec = with_halo(vec_low, "pts", 1, rim_rows)
        image_part, summed = apply_sum(wide_vec, kmat, tile)
        image = noise_var[None, :] * vector + kernel_scale * image_part
        return image, summed[: parts.shape[0], : parts.shape[1]]

    solution = jnp.zeros_like(right_side)
    residual = right_side
    res_image = noise_var[None, :] * residual + kernel_scale * apply_k(first_wide, kmat)
    direction = jnp.zeros_like(right_side)
    dir_image = jnp.zeros_like(right_side)
    dir_twice = jnp.zeros_like(right_side)
    norm_prev = None
    step_prev = None
    for iteration in range(ITERS):
        square_image, sums = apply_and_total(
            res_image,
            jnp.stack([jnp.sum(residual * residual, axis=1), jnp.sum(res_image * residual, axis=1)]),
        )
        norm_now = sums[0][:, None]
        curvature = sums[1][:, None]
        if iteration == 0:
            step_len = norm_now / curvature
            direction = residual
            dir_image = res_image
            dir_twice = square_image
        else:
            mix_ratio = norm_now / norm_prev
            step_len = norm_now / (curvature - mix_ratio * norm_now / step_prev)
            direction = residual + mix_ratio * direction
            dir_image = res_image + mix_ratio * dir_image
            dir_twice = square_image + mix_ratio * dir_twice
        solution = solution + step_len * direction
        residual = residual - step_len * dir_image
        res_image = res_image - step_len * dir_twice
        norm_prev = norm_now
        step_prev = step_len
    return (solution, residual, res_image)


def solution(mesh):
    placed = (P("pts", None), P("pts"), P("rhs", "pts"), P("pts", None))
    return jax.shard_map(
        per_device,
        mesh=mesh,
        in_specs=placed,
        out_specs=(P("rhs", "pts"), P("rhs", "pts"), P("rhs", "pts")),
        check_vma=False,
    )
```

```python
import functools

import jax
import jax.numpy as jnp
from jax import lax
from jax.experimental import pallas as pl
from jax.experimental.pallas import tpu as pltpu
from jax.sharding import PartitionSpec as P

F = 32
BLK = 128
REACH = 16
ITERS = 2
WIDE = 33
WEXP = 18
SLAB = 32
MESH = pl.DeviceIdType.MESH


def with_halo(cells, axis, dim, width):
    count = lax.axis_size(axis)
    ends = count - 1
    head = lax.slice_in_dim(cells, 0, width, axis=dim)
    tail = lax.slice_in_dim(cells, cells.shape[dim] - width, cells.shape[dim], axis=dim)
    return jnp.concatenate(
        [
            lax.ppermute(tail, axis, [(i, (i + 1) % count) for i in range(ends)]),
            cells,
            lax.ppermute(head, axis, [((i + 1) % count, i) for i in range(ends)]),
        ],
        axis=dim,
    )


def profile_tile(sq_left, sq_right, cross):
    dist = jnp.maximum((sq_left + sq_right) + cross, 0.0)
    radius = jnp.sqrt(dist)
    base = jnp.maximum(1.0 - radius, 0.0)
    b2 = base * base
    b4 = b2 * b2
    b8 = b4 * b4
    b16 = b8 * b8
    return (b16 * b2) * (WEXP * radius + 1.0)


def build_kernel(pat_ref, pw_ref, pwt_ref, sqr_ref, k_ref, mirror, cross_ref, sq_left_ref):
    a = pl.program_id(0)
    blocks = pl.num_programs(0)
    start = pl.multiple_of((a + REACH) * BLK, BLK)
    left = pw_ref[pl.ds(start, BLK), :]
    left_f = left.astype(jnp.float32)
    sq_left_ref[...] = jnp.sum(left_f * left_f, axis=1, keepdims=True)
    left_m2 = left * jnp.asarray(-2.0, jnp.bfloat16)
    window = pwt_ref[:, pl.ds(pl.multiple_of(a * BLK, BLK), WIDE * BLK)]
    cross_ref[...] = jnp.dot(left_m2, window, preferred_element_type=jnp.float32)

    def body(o, carry):
        col = pl.multiple_of((a + o) * BLK, BLK)
        dst = pl.ds(pl.multiple_of(o * BLK, BLK), BLK)
        live = pat_ref[a * WIDE + o] != 0
        other = a + o - REACH
        lower = jnp.logical_and(other >= 0, other < a)
        upper = jnp.logical_and(other > a, other < blocks)

        @pl.when(jnp.logical_and(live, lower))
        def _():
            k_ref[0, :, dst] = mirror[a, other]

        @pl.when(jnp.logical_and(live, jnp.logical_not(lower)))
        def _():
            sq_right = sqr_ref[:, pl.ds(col, BLK)]
            for h in range(BLK // SLAB):
                rows = pl.ds(h * SLAB, SLAB)
                value = profile_tile(sq_left_ref[rows, :], sq_right, cross_ref[rows, dst])
                k_ref[0, rows, dst] = value.astype(jnp.bfloat16)

            @pl.when(upper)
            def _():
                mirror[other, a] = k_ref[0, :, dst].astype(jnp.float32).T.astype(jnp.bfloat16)

        @pl.when(jnp.logical_not(live))
        def _():
            k_ref[0, :, dst] = jnp.zeros((BLK, BLK), jnp.bfloat16)

        return carry

    lax.fori_loop(0, WIDE, body, 0)


def apply_kernel(v_ref, k_ref, out_ref):
    a = pl.program_id(0)
    start = pl.multiple_of(a * BLK, BLK)
    v_cat = v_ref[:, pl.ds(start, WIDE * BLK)]
    out_ref[...] = lax.dot_general(
        v_cat, k_ref[0], (((1,), (1,)), ((), ())), preferred_element_type=jnp.float32
    )


def build_k(pattern_flat, wide_points, blocks):
    wide_rows = wide_points.shape[0]
    wide_points_t = wide_points.T
    wide_f = wide_points_t.astype(jnp.float32)
    sq_row = jnp.sum(wide_f * wide_f, axis=0, keepdims=True)
    return pl.pallas_call(
        build_kernel,
        out_shape=jax.ShapeDtypeStruct((blocks, BLK, WIDE * BLK), jnp.bfloat16),
        grid_spec=pltpu.PrefetchScalarGridSpec(
            num_scalar_prefetch=1,
            grid=(blocks,),
            in_specs=[
                pl.BlockSpec((wide_rows, F), lambda a, p: (0, 0)),
                pl.BlockSpec((F, wide_rows), lambda a, p: (0, 0)),
                pl.BlockSpec((1, wide_rows), lambda a, p: (0, 0)),
            ],
            out_specs=pl.BlockSpec((1, BLK, WIDE * BLK), lambda a, p: (a, 0, 0)),
            scratch_shapes=[
                pltpu.VMEM((blocks, blocks, BLK, BLK), jnp.bfloat16),
                pltpu.VMEM((BLK, WIDE * BLK), jnp.float32),
                pltpu.VMEM((BLK, 1), jnp.float32),
            ],
        ),
        compiler_params=pltpu.CompilerParams(dimension_semantics=("arbitrary",)),
    )(pattern_flat, wide_points, wide_points_t, sq_row)


def apply_k(wide_vec, kmat):
    rows, wide_cols = wide_vec.shape
    blocks = kmat.shape[0]
    return pl.pallas_call(
        apply_kernel,
        out_shape=jax.ShapeDtypeStruct((rows, blocks * BLK), jnp.float32),
        grid=(blocks,),
        in_specs=[
            pl.BlockSpec((rows, wide_cols), lambda a: (0, 0)),
            pl.BlockSpec((1, BLK, WIDE * BLK), lambda a: (a, 0, 0)),
        ],
        out_specs=pl.BlockSpec((rows, BLK), lambda a: (0, a)),
        compiler_params=pltpu.CompilerParams(dimension_semantics=("arbitrary",)),
    )(wide_vec, kmat)


def reduction_steps(inner, outer, part_ref, stage1, stage2, local_sem, send1, recv1, send2, recv2):
    me = lax.axis_index("pts")
    row = lax.axis_index("rhs")
    zc = me // inner
    rc = me % inner

    def greet():
        barrier = pltpu.get_barrier_semaphore()

        def greet_inner(k, carry):
            peer = zc * inner + lax.rem(rc + k, inner)
            pl.semaphore_signal(barrier, inc=1, device_id=(peer, row), device_id_type=MESH)
            return carry

        def greet_outer(k, carry):
            peer = lax.rem(zc + k, outer) * inner + rc
            pl.semaphore_signal(barrier, inc=1, device_id=(peer, row), device_id_type=MESH)
            return carry

        lax.fori_loop(1, inner, greet_inner, 0)
        lax.fori_loop(1, outer, greet_outer, 0)

    def first(slot, other):
        return pltpu.make_async_remote_copy(
            src_ref=part_ref,
            dst_ref=stage1.at[slot],
            send_sem=send1.at[other],
            recv_sem=recv1.at[slot],
            device_id=(zc * inner + other, row),
            device_id_type=MESH,
        )

    def second(slot, other):
        return pltpu.make_async_remote_copy(
            src_ref=stage1,
            dst_ref=stage2.at[slot],
            send_sem=send2.at[other],
            recv_sem=recv2.at[slot],
            device_id=(other * inner + rc, row),
            device_id_type=MESH,
        )

    own1 = pltpu.make_async_copy(part_ref, stage1.at[rc], local_sem.at[0])
    own2 = pltpu.make_async_copy(stage1, stage2.at[zc], local_sem.at[1])

    def start_first():
        pl.semaphore_wait(pltpu.get_barrier_semaphore(), (inner - 1) + (outer - 1))
        own1.start()

        def send_first(k, carry):
            first(rc, lax.rem(rc + k, inner)).start()
            return carry

        lax.fori_loop(1, inner, send_first, 0)

    def start_second():
        def finish_first(k, carry):
            other = lax.rem(rc + k, inner)
            first(rc, other).wait_send()
            first(other, other).wait_recv()
            return carry

        lax.fori_loop(1, inner, finish_first, 0)
        own1.wait()
        own2.start()

        def send_second(k, carry):
            second(zc, lax.rem(zc + k, outer)).start()
            return carry

        lax.fori_loop(1, outer, send_second, 0)

    def finish():
        def finish_second(k, carry):
            other = lax.rem(zc + k, outer)
            second(zc, other).wait_send()
            second(other, other).wait_recv()
            return carry

        lax.fori_loop(1, outer, finish_second, 0)
        own2.wait()
        return jnp.sum(jnp.sum(stage2[...], axis=0), axis=0)

    return greet, start_first, start_second, finish


def apply_sum_kernel(inner, outer, v_ref, k_ref, part_ref, out_ref, sum_ref, *scratch):
    a = pl.program_id(0)
    last = pl.num_programs(0) - 1
    greet, start_first, start_second, finish = reduction_steps(inner, outer, part_ref, *scratch)

    @pl.when(a == 0)
    def _():
        greet()
        start_first()

    blocks = v_ref.shape[1] // BLK - 2 * REACH

    @pl.when(a == min(blocks // 2 - 2, blocks - 1))
    def _():
        start_second()

    start = pl.multiple_of(a * BLK, BLK)
    v_cat = v_ref[:, pl.ds(start, WIDE * BLK)]
    out_ref[...] = lax.dot_general(
        v_cat, k_ref[0], (((1,), (1,)), ((), ())), preferred_element_type=jnp.float32
    )

    @pl.when(a == last)
    def _():
        sum_ref[...] = finish()


def apply_sum(wide_vec, kmat, tile):
    rows, wide_cols = wide_vec.shape
    blocks = kmat.shape[0]
    count = lax.axis_size("pts")
    inner = 8 if count % 8 == 0 else count
    outer = count // inner
    return pl.pallas_call(
        functools.partial(apply_sum_kernel, inner, outer),
        out_shape=(
            jax.ShapeDtypeStruct((rows, blocks * BLK), jnp.float32),
            jax.ShapeDtypeStruct(tile.shape, jnp.float32),
        ),
        grid=(blocks,),
        in_specs=[
            pl.BlockSpec((rows, wide_cols), lambda a: (0, 0)),
            pl.BlockSpec((1, BLK, WIDE * BLK), lambda a: (a, 0, 0)),
            pl.BlockSpec(tile.shape, lambda a: (0, 0)),
        ],
        out_specs=(
            pl.BlockSpec((rows, BLK), lambda a: (0, a)),
            pl.BlockSpec(tile.shape, lambda a: (0, 0)),
        ),
        scratch_shapes=[
            pltpu.VMEM((inner,) + tile.shape, jnp.float32),
            pltpu.VMEM((outer, inner) + tile.shape, jnp.float32),
            pltpu.SemaphoreType.DMA((2,)),
            pltpu.SemaphoreType.DMA((inner,)),
            pltpu.SemaphoreType.DMA((inner,)),
            pltpu.SemaphoreType.DMA((outer,)),
            pltpu.SemaphoreType.DMA((outer,)),
        ],
        compiler_params=pltpu.CompilerParams(
            dimension_semantics=("arbitrary",), collective_id=0, has_side_effects=True
        ),
    )(wide_vec, kmat, tile)


def per_device(points, noise_var, right_side, pattern):
    local_rows = points.shape[0]
    block_count = local_rows // BLK
    rim_rows = REACH * BLK
    kernel_scale = 1.0 / (4 * BLK)
    first_low = right_side.astype(jnp.bfloat16)
    point_rows = points.size // 128
    packed = jnp.concatenate([points.reshape(point_rows, 128), first_low.reshape(-1, 128)], axis=0)
    count = lax.axis_size("pts")
    from_left = lax.ppermute(packed, "pts", [(i, i + 1) for i in range(count - 1)])
    from_right = lax.ppermute(packed, "pts", [(i + 1, i) for i in range(count - 1)])
    wide_points = jnp.concatenate(
        [from_left[:point_rows].reshape(points.shape), points, from_right[:point_rows].reshape(points.shape)], axis=0
    )
    first_wide = jnp.concatenate(
        [
            from_left[point_rows:].reshape(first_low.shape),
            first_low,
            from_right[point_rows:].reshape(first_low.shape),
        ],
        axis=1,
    )
    kmat = build_k(pattern.reshape(-1), wide_points, block_count)

    rhs_count = lax.axis_size("rhs")
    rhs_index = lax.axis_index("rhs")

    def apply_operator(vector):
        vec_low = vector.astype(jnp.bfloat16)
        wide_vec = with_halo(vec_low, "pts", 1, rim_rows)
        image_part = apply_k(wide_vec, kmat)
        return noise_var[None, :] * vector + kernel_scale * image_part

    def apply_and_total(vector, parts):
        tile = jnp.zeros((8, 128), jnp.float32)
        tile = lax.dynamic_update_slice(tile, parts, (0, 0))
        vec_low = vector.astype(jnp.bfloat16)
        wide_vec = with_halo(vec_low, "pts", 1, rim_rows)
        image_part, summed = apply_sum(wide_vec, kmat, tile)
        image = noise_var[None, :] * vector + kernel_scale * image_part
        return image, summed[: parts.shape[0], : parts.shape[1]]

    solution = jnp.zeros_like(right_side)
    residual = right_side
    res_image = noise_var[None, :] * residual + kernel_scale * apply_k(first_wide, kmat)
    direction = jnp.zeros_like(right_side)
    dir_image = jnp.zeros_like(right_side)
    dir_twice = jnp.zeros_like(right_side)
    norm_prev = None
    step_prev = None
    for iteration in range(ITERS):
        square_image, sums = apply_and_total(
            res_image,
            jnp.stack([jnp.sum(residual * residual, axis=1), jnp.sum(res_image * residual, axis=1)]),
        )
        norm_now = sums[0][:, None]
        curvature = sums[1][:, None]
        if iteration == 0:
            step_len = norm_now / curvature
            direction = residual
            dir_image = res_image
            dir_twice = square_image
        else:
            mix_ratio = norm_now / norm_prev
            step_len = norm_now / (curvature - mix_ratio * norm_now / step_prev)
            direction = residual + mix_ratio * direction
            dir_image = res_image + mix_ratio * dir_image
            dir_twice = square_image + mix_ratio * dir_twice
        solution = solution + step_len * direction
        residual = residual - step_len * dir_image
        res_image = res_image - step_len * dir_twice
        norm_prev = norm_now
        step_prev = step_len
    return (solution, residual, res_image)


def solution(mesh):
    placed = (P("pts", None), P("pts"), P("rhs", "pts"), P("pts", None))
    return jax.shard_map(
        per_device,
        mesh=mesh,
        in_specs=placed,
        out_specs=(P("rhs", "pts"), P("rhs", "pts"), P("rhs", "pts")),
        check_vma=False,
    )
```

```python
import functools

import jax
import jax.numpy as jnp
from jax import lax
from jax.experimental import pallas as pl
from jax.experimental.pallas import tpu as pltpu
from jax.sharding import PartitionSpec as P

F = 32
BLK = 128
REACH = 16
ITERS = 2
WIDE = 33
WEXP = 18
MESH = pl.DeviceIdType.MESH


def with_halo(cells, axis, dim, width):
    count = lax.axis_size(axis)
    ends = count - 1
    head = lax.slice_in_dim(cells, 0, width, axis=dim)
    tail = lax.slice_in_dim(cells, cells.shape[dim] - width, cells.shape[dim], axis=dim)
    return jnp.concatenate(
        [
            lax.ppermute(tail, axis, [(i, (i + 1) % count) for i in range(ends)]),
            cells,
            lax.ppermute(head, axis, [((i + 1) % count, i) for i in range(ends)]),
        ],
        axis=dim,
    )


def profile_tile(sq_left, sq_right, cross):
    dist = jnp.maximum((sq_left + sq_right) + cross, 0.0)
    radius = jnp.sqrt(dist)
    base = jnp.maximum(1.0 - radius, 0.0)
    b2 = base * base
    b4 = b2 * b2
    b8 = b4 * b4
    b16 = b8 * b8
    return (b16 * b2) * (WEXP * radius + 1.0)


def build_kernel(pat_ref, pw_ref, pwt_ref, sqr_ref, k_ref, mirror, cross_ref):
    a = pl.program_id(0)
    blocks = pl.num_programs(0)
    start = pl.multiple_of((a + REACH) * BLK, BLK)
    left = pw_ref[pl.ds(start, BLK), :]
    left_f = left.astype(jnp.float32)
    sq_left = jnp.sum(left_f * left_f, axis=1, keepdims=True)
    left_m2 = left * jnp.asarray(-2.0, jnp.bfloat16)
    window = pwt_ref[:, pl.ds(pl.multiple_of(a * BLK, BLK), WIDE * BLK)]
    cross_ref[...] = jnp.dot(left_m2, window, preferred_element_type=jnp.float32)

    def body(o, carry):
        col = pl.multiple_of((a + o) * BLK, BLK)
        dst = pl.ds(pl.multiple_of(o * BLK, BLK), BLK)
        live = pat_ref[a * WIDE + o] != 0
        other = a + o - REACH
        lower = jnp.logical_and(other >= 0, other < a)
        upper = jnp.logical_and(other > a, other < blocks)

        @pl.when(jnp.logical_and(live, lower))
        def _():
            k_ref[0, :, dst] = mirror[a, other]

        @pl.when(jnp.logical_and(live, jnp.logical_not(lower)))
        def _():
            sq_right = sqr_ref[:, pl.ds(col, BLK)]
            value = profile_tile(sq_left, sq_right, cross_ref[:, dst])
            k_ref[0, :, dst] = value.astype(jnp.bfloat16)

            @pl.when(upper)
            def _():
                mirror[other, a] = value.T.astype(jnp.bfloat16)

        @pl.when(jnp.logical_not(live))
        def _():
            k_ref[0, :, dst] = jnp.zeros((BLK, BLK), jnp.bfloat16)

        return carry

    lax.fori_loop(0, WIDE, body, 0)


def apply_kernel(v_ref, k_ref, out_ref):
    a = pl.program_id(0)
    start = pl.multiple_of(a * BLK, BLK)
    v_cat = v_ref[:, pl.ds(start, WIDE * BLK)]
    out_ref[...] = lax.dot_general(
        v_cat, k_ref[0], (((1,), (1,)), ((), ())), preferred_element_type=jnp.float32
    )


def build_k(pattern_flat, wide_points, blocks):
    wide_rows = wide_points.shape[0]
    wide_points_t = wide_points.T
    wide_f = wide_points_t.astype(jnp.float32)
    sq_row = jnp.sum(wide_f * wide_f, axis=0, keepdims=True)
    return pl.pallas_call(
        build_kernel,
        out_shape=jax.ShapeDtypeStruct((blocks, BLK, WIDE * BLK), jnp.bfloat16),
        grid_spec=pltpu.PrefetchScalarGridSpec(
            num_scalar_prefetch=1,
            grid=(blocks,),
            in_specs=[
                pl.BlockSpec((wide_rows, F), lambda a, p: (0, 0)),
                pl.BlockSpec((F, wide_rows), lambda a, p: (0, 0)),
                pl.BlockSpec((1, wide_rows), lambda a, p: (0, 0)),
            ],
            out_specs=pl.BlockSpec((1, BLK, WIDE * BLK), lambda a, p: (a, 0, 0)),
            scratch_shapes=[
                pltpu.VMEM((blocks, blocks, BLK, BLK), jnp.bfloat16),
                pltpu.VMEM((BLK, WIDE * BLK), jnp.float32),
            ],
        ),
        compiler_params=pltpu.CompilerParams(dimension_semantics=("arbitrary",)),
    )(pattern_flat, wide_points, wide_points_t, sq_row)


def apply_k(wide_vec, kmat):
    rows, wide_cols = wide_vec.shape
    blocks = kmat.shape[0]
    return pl.pallas_call(
        apply_kernel,
        out_shape=jax.ShapeDtypeStruct((rows, blocks * BLK), jnp.float32),
        grid=(blocks,),
        in_specs=[
            pl.BlockSpec((rows, wide_cols), lambda a: (0, 0)),
            pl.BlockSpec((1, BLK, WIDE * BLK), lambda a: (a, 0, 0)),
        ],
        out_specs=pl.BlockSpec((rows, BLK), lambda a: (0, a)),
        compiler_params=pltpu.CompilerParams(dimension_semantics=("arbitrary",)),
    )(wide_vec, kmat)


def reduction_steps(inner, outer, part_ref, stage1, stage2, local_sem, send1, recv1, send2, recv2):
    me = lax.axis_index("pts")
    row = lax.axis_index("rhs")
    zc = me // inner
    rc = me % inner

    def greet():
        barrier = pltpu.get_barrier_semaphore()

        def greet_inner(k, carry):
            peer = zc * inner + lax.rem(rc + k, inner)
            pl.semaphore_signal(barrier, inc=1, device_id=(peer, row), device_id_type=MESH)
            return carry

        def greet_outer(k, carry):
            peer = lax.rem(zc + k, outer) * inner + rc
            pl.semaphore_signal(barrier, inc=1, device_id=(peer, row), device_id_type=MESH)
            return carry

        lax.fori_loop(1, inner, greet_inner, 0)
        lax.fori_loop(1, outer, greet_outer, 0)

    def first(slot, other):
        return pltpu.make_async_remote_copy(
            src_ref=part_ref,
            dst_ref=stage1.at[slot],
            send_sem=send1.at[other],
            recv_sem=recv1.at[slot],
            device_id=(zc * inner + other, row),
            device_id_type=MESH,
        )

    def second(slot, other):
        return pltpu.make_async_remote_copy(
            src_ref=stage1,
            dst_ref=stage2.at[slot],
            send_sem=send2.at[other],
            recv_sem=recv2.at[slot],
            device_id=(other * inner + rc, row),
            device_id_type=MESH,
        )

    own1 = pltpu.make_async_copy(part_ref, stage1.at[rc], local_sem.at[0])
    own2 = pltpu.make_async_copy(stage1, stage2.at[zc], local_sem.at[1])

    def start_first():
        own1.start()

        def send_first(k, carry):
            first(rc, lax.rem(rc + k, inner)).start()
            return carry

        lax.fori_loop(1, inner, send_first, 0)

    def start_second():
        def finish_first(k, carry):
            other = lax.rem(rc + k, inner)
            first(rc, other).wait_send()
            first(other, other).wait_recv()
            return carry

        lax.fori_loop(1, inner, finish_first, 0)
        own1.wait()
        own2.start()

        def send_second(k, carry):
            second(zc, lax.rem(zc + k, outer)).start()
            return carry

        lax.fori_loop(1, outer, send_second, 0)

    def finish():
        def finish_second(k, carry):
            other = lax.rem(zc + k, outer)
            second(zc, other).wait_send()
            second(other, other).wait_recv()
            return carry

        lax.fori_loop(1, outer, finish_second, 0)
        own2.wait()
        return jnp.sum(jnp.sum(stage2[...], axis=0), axis=0)

    return greet, start_first, start_second, finish


def apply_sum_kernel(inner, outer, vloc_ref, k_ref, part_ref, out_ref, sum_ref, v_ref, halo_send, halo_recv, halo_local, *scratch):
    a = pl.program_id(0)
    last = pl.num_programs(0) - 1
    greet, start_first, start_second, finish = reduction_steps(inner, outer, part_ref, *scratch)
    me = lax.axis_index("pts")
    row = lax.axis_index("rhs")
    count = inner * outer
    rc = me % inner
    width = vloc_ref.shape[1]
    has_left = me > 0
    has_right = me < count - 1
    extra = jnp.logical_or(
        jnp.logical_and(rc == 0, has_left), jnp.logical_and(rc == inner - 1, has_right)
    )

    def to_right():
        return pltpu.make_async_remote_copy(
            src_ref=vloc_ref,
            dst_ref=v_ref.at[:, pl.ds(0, width)],
            send_sem=halo_send.at[0],
            recv_sem=halo_recv.at[0],
            device_id=(me + 1, row),
            device_id_type=MESH,
        )

    def to_left():
        return pltpu.make_async_remote_copy(
            src_ref=vloc_ref,
            dst_ref=v_ref.at[:, pl.ds(2 * width, width)],
            send_sem=halo_send.at[1],
            recv_sem=halo_recv.at[1],
            device_id=(me - 1, row),
            device_id_type=MESH,
        )

    def from_left():
        return pltpu.make_async_remote_copy(
            src_ref=vloc_ref,
            dst_ref=v_ref.at[:, pl.ds(0, width)],
            send_sem=halo_send.at[0],
            recv_sem=halo_recv.at[0],
            device_id=(me - 1, row),
            device_id_type=MESH,
        )

    def from_right():
        return pltpu.make_async_remote_copy(
            src_ref=vloc_ref,
            dst_ref=v_ref.at[:, pl.ds(2 * width, width)],
            send_sem=halo_send.at[1],
            recv_sem=halo_recv.at[1],
            device_id=(me + 1, row),
            device_id_type=MESH,
        )

    own = pltpu.make_async_copy(vloc_ref, v_ref.at[:, pl.ds(width, width)], halo_local.at[0])

    @pl.when(a == 0)
    def _():
        greet()
        barrier = pltpu.get_barrier_semaphore()

        @pl.when(jnp.logical_and(extra, rc == 0))
        def _():
            pl.semaphore_signal(barrier, inc=1, device_id=(me - 1, row), device_id_type=MESH)

        @pl.when(jnp.logical_and(extra, rc == inner - 1))
        def _():
            pl.semaphore_signal(barrier, inc=1, device_id=(me + 1, row), device_id_type=MESH)

        peers = (inner - 1) + (outer - 1)

        @pl.when(extra)
        def _():
            pl.semaphore_wait(barrier, peers + 1)

        @pl.when(jnp.logical_not(extra))
        def _():
            pl.semaphore_wait(barrier, peers)

        start_first()
        own.start()

        @pl.when(has_right)
        def _():
            to_right().start()

        @pl.when(has_left)
        def _():
            to_left().start()

        @pl.when(jnp.logical_not(has_left))
        def _():
            v_ref[:, pl.ds(0, width)] = jnp.zeros((v_ref.shape[0], width), v_ref.dtype)

        @pl.when(jnp.logical_not(has_right))
        def _():
            v_ref[:, pl.ds(2 * width, width)] = jnp.zeros((v_ref.shape[0], width), v_ref.dtype)

        own.wait()

        @pl.when(has_right)
        def _():
            to_right().wait_send()
            from_right().wait_recv()

        @pl.when(has_left)
        def _():
            to_left().wait_send()
            from_left().wait_recv()

    blocks = v_ref.shape[1] // BLK - 2 * REACH

    @pl.when(a == min(blocks // 2 - 2, blocks - 1))
    def _():
        start_second()

    start = pl.multiple_of(a * BLK, BLK)
    v_cat = v_ref[:, pl.ds(start, WIDE * BLK)]
    out_ref[...] = lax.dot_general(
        v_cat, k_ref[0], (((1,), (1,)), ((), ())), preferred_element_type=jnp.float32
    )

    @pl.when(a == last)
    def _():
        sum_ref[...] = finish()


def apply_sum(local_vec, kmat, tile):
    rows, width = local_vec.shape
    wide_cols = width + 2 * REACH * BLK
    blocks = kmat.shape[0]
    count = lax.axis_size("pts")
    inner = 8 if count % 8 == 0 else count
    outer = count // inner
    return pl.pallas_call(
        functools.partial(apply_sum_kernel, inner, outer),
        out_shape=(
            jax.ShapeDtypeStruct((rows, blocks * BLK), jnp.float32),
            jax.ShapeDtypeStruct(tile.shape, jnp.float32),
        ),
        grid=(blocks,),
        in_specs=[
            pl.BlockSpec((rows, width), lambda a: (0, 0)),
            pl.BlockSpec((1, BLK, WIDE * BLK), lambda a: (a, 0, 0)),
            pl.BlockSpec(tile.shape, lambda a: (0, 0)),
        ],
        out_specs=(
            pl.BlockSpec((rows, BLK), lambda a: (0, a)),
            pl.BlockSpec(tile.shape, lambda a: (0, 0)),
        ),
        scratch_shapes=[
            pltpu.VMEM((rows, wide_cols), local_vec.dtype),
            pltpu.SemaphoreType.DMA((2,)),
            pltpu.SemaphoreType.DMA((2,)),
            pltpu.SemaphoreType.DMA((1,)),
            pltpu.VMEM((inner,) + tile.shape, jnp.float32),
            pltpu.VMEM((outer, inner) + tile.shape, jnp.float32),
            pltpu.SemaphoreType.DMA((2,)),
            pltpu.SemaphoreType.DMA((inner,)),
            pltpu.SemaphoreType.DMA((inner,)),
            pltpu.SemaphoreType.DMA((outer,)),
            pltpu.SemaphoreType.DMA((outer,)),
        ],
        compiler_params=pltpu.CompilerParams(
            dimension_semantics=("arbitrary",), collective_id=0, has_side_effects=True
        ),
    )(local_vec, kmat, tile)


def per_device(points, noise_var, right_side, pattern):
    local_rows = points.shape[0]
    block_count = local_rows // BLK
    rim_rows = REACH * BLK
    kernel_scale = 1.0 / (4 * BLK)
    first_low = right_side.astype(jnp.bfloat16)
    point_rows = points.size // 128
    packed = jnp.concatenate([points.reshape(point_rows, 128), first_low.reshape(-1, 128)], axis=0)
    count = lax.axis_size("pts")
    from_left = lax.ppermute(packed, "pts", [(i, i + 1) for i in range(count - 1)])
    from_right = lax.ppermute(packed, "pts", [(i + 1, i) for i in range(count - 1)])
    wide_points = jnp.concatenate(
        [from_left[:point_rows].reshape(points.shape), points, from_right[:point_rows].reshape(points.shape)], axis=0
    )
    first_wide = jnp.concatenate(
        [
            from_left[point_rows:].reshape(first_low.shape),
            first_low,
            from_right[point_rows:].reshape(first_low.shape),
        ],
        axis=1,
    )
    kmat = build_k(pattern.reshape(-1), wide_points, block_count)

    rhs_count = lax.axis_size("rhs")
    rhs_index = lax.axis_index("rhs")

    def apply_operator(vector):
        vec_low = vector.astype(jnp.bfloat16)
        wide_vec = with_halo(vec_low, "pts", 1, rim_rows)
        image_part = apply_k(wide_vec, kmat)
        return noise_var[None, :] * vector + kernel_scale * image_part

    def apply_and_total(vector, parts):
        tile = jnp.zeros((8, 128), jnp.float32)
        tile = lax.dynamic_update_slice(tile, parts, (0, 0))
        vec_low = vector.astype(jnp.bfloat16)
        image_part, summed = apply_sum(vec_low, kmat, tile)
        image = noise_var[None, :] * vector + kernel_scale * image_part
        return image, summed[: parts.shape[0], : parts.shape[1]]

    solution = jnp.zeros_like(right_side)
    residual = right_side
    res_image = noise_var[None, :] * residual + kernel_scale * apply_k(first_wide, kmat)
    direction = jnp.zeros_like(right_side)
    dir_image = jnp.zeros_like(right_side)
    dir_twice = jnp.zeros_like(right_side)
    norm_prev = None
    step_prev = None
    for iteration in range(ITERS):
        square_image, sums = apply_and_total(
            res_image,
            jnp.stack([jnp.sum(residual * residual, axis=1), jnp.sum(res_image * residual, axis=1)]),
        )
        norm_now = sums[0][:, None]
        curvature = sums[1][:, None]
        if iteration == 0:
            step_len = norm_now / curvature
            direction = residual
            dir_image = res_image
            dir_twice = square_image
        else:
            mix_ratio = norm_now / norm_prev
            step_len = norm_now / (curvature - mix_ratio * norm_now / step_prev)
            direction = residual + mix_ratio * direction
            dir_image = res_image + mix_ratio * dir_image
            dir_twice = square_image + mix_ratio * dir_twice
        solution = solution + step_len * direction
        residual = residual - step_len * dir_image
        res_image = res_image - step_len * dir_twice
        norm_prev = norm_now
        step_prev = step_len
    return (solution, residual, res_image)


def solution(mesh):
    placed = (P("pts", None), P("pts"), P("rhs", "pts"), P("pts", None))
    return jax.shard_map(
        per_device,
        mesh=mesh,
        in_specs=placed,
        out_specs=(P("rhs", "pts"), P("rhs", "pts"), P("rhs", "pts")),
        check_vma=False,
    )
```

```python
import functools

import jax
import jax.numpy as jnp
from jax import lax
from jax.experimental import pallas as pl
from jax.experimental.pallas import tpu as pltpu
from jax.sharding import PartitionSpec as P

F = 32
BLK = 128
REACH = 16
ITERS = 2
WIDE = 33
WEXP = 18
MESH = pl.DeviceIdType.MESH


def with_halo(cells, axis, dim, width):
    count = lax.axis_size(axis)
    ends = count - 1
    head = lax.slice_in_dim(cells, 0, width, axis=dim)
    tail = lax.slice_in_dim(cells, cells.shape[dim] - width, cells.shape[dim], axis=dim)
    return jnp.concatenate(
        [
            lax.ppermute(tail, axis, [(i, (i + 1) % count) for i in range(ends)]),
            cells,
            lax.ppermute(head, axis, [((i + 1) % count, i) for i in range(ends)]),
        ],
        axis=dim,
    )


def profile_tile(sq_left, sq_right, cross):
    dist = jnp.maximum((sq_left + sq_right) + cross, 0.0)
    radius = jnp.sqrt(dist)
    base = jnp.maximum(1.0 - radius, 0.0)
    b2 = base * base
    b4 = b2 * b2
    b8 = b4 * b4
    b16 = b8 * b8
    return (b16 * b2) * (WEXP * radius + 1.0)


def build_kernel(pat_ref, pw_ref, pwt_ref, k_ref, mirror, cross_ref, sqr_ref):
    a = pl.program_id(0)
    blocks = pl.num_programs(0)
    start = pl.multiple_of(a * BLK, BLK)
    left = pw_ref[pl.ds(start, BLK), :]
    left_f = left.astype(jnp.float32)
    sq_left = jnp.sum(left_f * left_f, axis=1, keepdims=True)
    left_m2 = left * jnp.asarray(-2.0, jnp.bfloat16)
    window = pwt_ref[:, pl.ds(pl.multiple_of(a * BLK, BLK), WIDE * BLK)]
    cross_ref[...] = jnp.dot(left_m2, window, preferred_element_type=jnp.float32)
    window_f = window.astype(jnp.float32)
    sqr_ref[...] = jnp.sum(window_f * window_f, axis=0, keepdims=True)

    def body(o, carry):
        col = pl.multiple_of((a + o) * BLK, BLK)
        dst = pl.ds(pl.multiple_of(o * BLK, BLK), BLK)
        live = pat_ref[a, o] != 0
        other = a + o - REACH
        lower = jnp.logical_and(other >= 0, other < a)
        upper = jnp.logical_and(other > a, other < blocks)

        @pl.when(jnp.logical_and(live, lower))
        def _():
            k_ref[0, :, dst] = mirror[a, other]

        @pl.when(jnp.logical_and(live, jnp.logical_not(lower)))
        def _():
            sq_right = sqr_ref[:, dst]
            value = profile_tile(sq_left, sq_right, cross_ref[:, dst])
            k_ref[0, :, dst] = value.astype(jnp.bfloat16)

            @pl.when(upper)
            def _():
                mirror[other, a] = value.T.astype(jnp.bfloat16)

        @pl.when(jnp.logical_not(live))
        def _():
            k_ref[0, :, dst] = jnp.zeros((BLK, BLK), jnp.bfloat16)

        return carry

    lax.fori_loop(0, WIDE, body, 0)


def apply_kernel(v_ref, k_ref, out_ref):
    a = pl.program_id(0)
    start = pl.multiple_of(a * BLK, BLK)
    v_cat = v_ref[:, pl.ds(start, WIDE * BLK)]
    out_ref[...] = lax.dot_general(
        v_cat, k_ref[0], (((1,), (1,)), ((), ())), preferred_element_type=jnp.float32
    )


def build_k(pattern, points, wide_points_t, blocks):
    rows = points.shape[0]
    wide_cols = wide_points_t.shape[1]
    return pl.pallas_call(
        build_kernel,
        out_shape=jax.ShapeDtypeStruct((blocks, BLK, WIDE * BLK), jnp.bfloat16),
        grid_spec=pltpu.PrefetchScalarGridSpec(
            num_scalar_prefetch=1,
            grid=(blocks,),
            in_specs=[
                pl.BlockSpec((rows, F), lambda a, p: (0, 0)),
                pl.BlockSpec((F, wide_cols), lambda a, p: (0, 0)),
            ],
            out_specs=pl.BlockSpec((1, BLK, WIDE * BLK), lambda a, p: (a, 0, 0)),
            scratch_shapes=[
                pltpu.VMEM((blocks, blocks, BLK, BLK), jnp.bfloat16),
                pltpu.VMEM((BLK, WIDE * BLK), jnp.float32),
                pltpu.VMEM((1, WIDE * BLK), jnp.float32),
            ],
        ),
        compiler_params=pltpu.CompilerParams(dimension_semantics=("arbitrary",)),
    )(pattern, points, wide_points_t)


def apply_k(wide_vec, kmat):
    rows, wide_cols = wide_vec.shape
    blocks = kmat.shape[0]
    return pl.pallas_call(
        apply_kernel,
        out_shape=jax.ShapeDtypeStruct((rows, blocks * BLK), jnp.float32),
        grid=(blocks,),
        in_specs=[
            pl.BlockSpec((rows, wide_cols), lambda a: (0, 0)),
            pl.BlockSpec((1, BLK, WIDE * BLK), lambda a: (a, 0, 0)),
        ],
        out_specs=pl.BlockSpec((rows, BLK), lambda a: (0, a)),
        compiler_params=pltpu.CompilerParams(dimension_semantics=("arbitrary",)),
    )(wide_vec, kmat)


def reduction_steps(inner, outer, part_ref, stage1, stage2, local_sem, send1, recv1, send2, recv2):
    me = lax.axis_index("pts")
    row = lax.axis_index("rhs")
    zc = me // inner
    rc = me % inner

    def greet():
        barrier = pltpu.get_barrier_semaphore()

        def greet_inner(k, carry):
            peer = zc * inner + lax.rem(rc + k, inner)
            pl.semaphore_signal(barrier, inc=1, device_id=(peer, row), device_id_type=MESH)
            return carry

        def greet_outer(k, carry):
            peer = lax.rem(zc + k, outer) * inner + rc
            pl.semaphore_signal(barrier, inc=1, device_id=(peer, row), device_id_type=MESH)
            return carry

        lax.fori_loop(1, inner, greet_inner, 0)
        lax.fori_loop(1, outer, greet_outer, 0)

    def first(slot, other):
        return pltpu.make_async_remote_copy(
            src_ref=part_ref,
            dst_ref=stage1.at[slot],
            send_sem=send1.at[other],
            recv_sem=recv1.at[slot],
            device_id=(zc * inner + other, row),
            device_id_type=MESH,
        )

    def second(slot, other):
        return pltpu.make_async_remote_copy(
            src_ref=stage1,
            dst_ref=stage2.at[slot],
            send_sem=send2.at[other],
            recv_sem=recv2.at[slot],
            device_id=(other * inner + rc, row),
            device_id_type=MESH,
        )

    own1 = pltpu.make_async_copy(part_ref, stage1.at[rc], local_sem.at[0])
    own2 = pltpu.make_async_copy(stage1, stage2.at[zc], local_sem.at[1])

    def start_first():
        own1.start()

        def send_first(k, carry):
            first(rc, lax.rem(rc + k, inner)).start()
            return carry

        lax.fori_loop(1, inner, send_first, 0)

    def start_second():
        def finish_first(k, carry):
            other = lax.rem(rc + k, inner)
            first(rc, other).wait_send()
            first(other, other).wait_recv()
            return carry

        lax.fori_loop(1, inner, finish_first, 0)
        own1.wait()
        own2.start()

        def send_second(k, carry):
            second(zc, lax.rem(zc + k, outer)).start()
            return carry

        lax.fori_loop(1, outer, send_second, 0)

    def finish():
        def finish_second(k, carry):
            other = lax.rem(zc + k, outer)
            second(zc, other).wait_send()
            second(other, other).wait_recv()
            return carry

        lax.fori_loop(1, outer, finish_second, 0)
        own2.wait()
        return jnp.sum(jnp.sum(stage2[...], axis=0), axis=0)

    return greet, start_first, start_second, finish


def apply_sum_kernel(inner, outer, vloc_ref, k_ref, part_ref, out_ref, sum_ref, v_ref, halo_send, halo_recv, halo_local, *scratch):
    a = pl.program_id(0)
    last = pl.num_programs(0) - 1
    greet, start_first, start_second, finish = reduction_steps(inner, outer, part_ref, *scratch)
    me = lax.axis_index("pts")
    row = lax.axis_index("rhs")
    count = inner * outer
    rc = me % inner
    width = vloc_ref.shape[1]
    has_left = me > 0
    has_right = me < count - 1
    extra = jnp.logical_or(
        jnp.logical_and(rc == 0, has_left), jnp.logical_and(rc == inner - 1, has_right)
    )

    def to_right():
        return pltpu.make_async_remote_copy(
            src_ref=vloc_ref,
            dst_ref=v_ref.at[:, pl.ds(0, width)],
            send_sem=halo_send.at[0],
            recv_sem=halo_recv.at[0],
            device_id=(me + 1, row),
            device_id_type=MESH,
        )

    def to_left():
        return pltpu.make_async_remote_copy(
            src_ref=vloc_ref,
            dst_ref=v_ref.at[:, pl.ds(2 * width, width)],
            send_sem=halo_send.at[1],
            recv_sem=halo_recv.at[1],
            device_id=(me - 1, row),
            device_id_type=MESH,
        )

    def from_left():
        return pltpu.make_async_remote_copy(
            src_ref=vloc_ref,
            dst_ref=v_ref.at[:, pl.ds(0, width)],
            send_sem=halo_send.at[0],
            recv_sem=halo_recv.at[0],
            device_id=(me - 1, row),
            device_id_type=MESH,
        )

    def from_right():
        return pltpu.make_async_remote_copy(
            src_ref=vloc_ref,
            dst_ref=v_ref.at[:, pl.ds(2 * width, width)],
            send_sem=halo_send.at[1],
            recv_sem=halo_recv.at[1],
            device_id=(me + 1, row),
            device_id_type=MESH,
        )

    own = pltpu.make_async_copy(vloc_ref, v_ref.at[:, pl.ds(width, width)], halo_local.at[0])

    @pl.when(a == 0)
    def _():
        greet()
        barrier = pltpu.get_barrier_semaphore()

        @pl.when(jnp.logical_and(extra, rc == 0))
        def _():
            pl.semaphore_signal(barrier, inc=1, device_id=(me - 1, row), device_id_type=MESH)

        @pl.when(jnp.logical_and(extra, rc == inner - 1))
        def _():
            pl.semaphore_signal(barrier, inc=1, device_id=(me + 1, row), device_id_type=MESH)

        peers = (inner - 1) + (outer - 1)

        @pl.when(extra)
        def _():
            pl.semaphore_wait(barrier, peers + 1)

        @pl.when(jnp.logical_not(extra))
        def _():
            pl.semaphore_wait(barrier, peers)

        start_first()
        own.start()

        @pl.when(has_right)
        def _():
            to_right().start()

        @pl.when(has_left)
        def _():
            to_left().start()

        @pl.when(jnp.logical_not(has_left))
        def _():
            v_ref[:, pl.ds(0, width)] = jnp.zeros((v_ref.shape[0], width), v_ref.dtype)

        @pl.when(jnp.logical_not(has_right))
        def _():
            v_ref[:, pl.ds(2 * width, width)] = jnp.zeros((v_ref.shape[0], width), v_ref.dtype)

        own.wait()

        @pl.when(has_right)
        def _():
            to_right().wait_send()
            from_right().wait_recv()

        @pl.when(has_left)
        def _():
            to_left().wait_send()
            from_left().wait_recv()

    blocks = v_ref.shape[1] // BLK - 2 * REACH

    @pl.when(a == min(blocks // 2 - 2, blocks - 1))
    def _():
        start_second()

    start = pl.multiple_of(a * BLK, BLK)
    v_cat = v_ref[:, pl.ds(start, WIDE * BLK)]
    out_ref[...] = lax.dot_general(
        v_cat, k_ref[0], (((1,), (1,)), ((), ())), preferred_element_type=jnp.float32
    )

    @pl.when(a == last)
    def _():
        sum_ref[...] = finish()


def apply_sum(local_vec, kmat, tile):
    rows, width = local_vec.shape
    wide_cols = width + 2 * REACH * BLK
    blocks = kmat.shape[0]
    count = lax.axis_size("pts")
    inner = 8 if count % 8 == 0 else count
    outer = count // inner
    return pl.pallas_call(
        functools.partial(apply_sum_kernel, inner, outer),
        out_shape=(
            jax.ShapeDtypeStruct((rows, blocks * BLK), jnp.float32),
            jax.ShapeDtypeStruct(tile.shape, jnp.float32),
        ),
        grid=(blocks,),
        in_specs=[
            pl.BlockSpec((rows, width), lambda a: (0, 0)),
            pl.BlockSpec((1, BLK, WIDE * BLK), lambda a: (a, 0, 0)),
            pl.BlockSpec(tile.shape, lambda a: (0, 0)),
        ],
        out_specs=(
            pl.BlockSpec((rows, BLK), lambda a: (0, a)),
            pl.BlockSpec(tile.shape, lambda a: (0, 0)),
        ),
        scratch_shapes=[
            pltpu.VMEM((rows, wide_cols), local_vec.dtype),
            pltpu.SemaphoreType.DMA((2,)),
            pltpu.SemaphoreType.DMA((2,)),
            pltpu.SemaphoreType.DMA((1,)),
            pltpu.VMEM((inner,) + tile.shape, jnp.float32),
            pltpu.VMEM((outer, inner) + tile.shape, jnp.float32),
            pltpu.SemaphoreType.DMA((2,)),
            pltpu.SemaphoreType.DMA((inner,)),
            pltpu.SemaphoreType.DMA((inner,)),
            pltpu.SemaphoreType.DMA((outer,)),
            pltpu.SemaphoreType.DMA((outer,)),
        ],
        compiler_params=pltpu.CompilerParams(
            dimension_semantics=("arbitrary",), collective_id=0, has_side_effects=True
        ),
    )(local_vec, kmat, tile)


def per_device(points, noise_var, right_side, pattern):
    local_rows = points.shape[0]
    block_count = local_rows // BLK
    rim_rows = REACH * BLK
    kernel_scale = 1.0 / (4 * BLK)
    first_low = right_side.astype(jnp.bfloat16)
    points_t = points.T
    packed = jnp.concatenate([points_t, first_low], axis=0)
    count = lax.axis_size("pts")
    from_left = lax.ppermute(packed, "pts", [(i, i + 1) for i in range(count - 1)])
    from_right = lax.ppermute(packed, "pts", [(i + 1, i) for i in range(count - 1)])
    wide_points_t = jnp.concatenate([from_left[:F], points_t, from_right[:F]], axis=1)
    first_wide = jnp.concatenate([from_left[F:], first_low, from_right[F:]], axis=1)
    kmat = build_k(pattern, points, wide_points_t, block_count)

    rhs_count = lax.axis_size("rhs")
    rhs_index = lax.axis_index("rhs")

    def apply_operator(vector):
        vec_low = vector.astype(jnp.bfloat16)
        wide_vec = with_halo(vec_low, "pts", 1, rim_rows)
        image_part = apply_k(wide_vec, kmat)
        return noise_var[None, :] * vector + kernel_scale * image_part

    def apply_and_total(vector, parts):
        tile = jnp.zeros((8, 128), jnp.float32)
        tile = lax.dynamic_update_slice(tile, parts, (0, 0))
        vec_low = vector.astype(jnp.bfloat16)
        image_part, summed = apply_sum(vec_low, kmat, tile)
        image = noise_var[None, :] * vector + kernel_scale * image_part
        return image, summed[: parts.shape[0], : parts.shape[1]]

    solution = jnp.zeros_like(right_side)
    residual = right_side
    res_image = noise_var[None, :] * residual + kernel_scale * apply_k(first_wide, kmat)
    direction = jnp.zeros_like(right_side)
    dir_image = jnp.zeros_like(right_side)
    dir_twice = jnp.zeros_like(right_side)
    norm_prev = None
    step_prev = None
    for iteration in range(ITERS):
        square_image, sums = apply_and_total(
            res_image,
            jnp.stack([jnp.sum(residual * residual, axis=1), jnp.sum(res_image * residual, axis=1)]),
        )
        norm_now = sums[0][:, None]
        curvature = sums[1][:, None]
        if iteration == 0:
            step_len = norm_now / curvature
            direction = residual
            dir_image = res_image
            dir_twice = square_image
        else:
            mix_ratio = norm_now / norm_prev
            step_len = norm_now / (curvature - mix_ratio * norm_now / step_prev)
            direction = residual + mix_ratio * direction
            dir_image = res_image + mix_ratio * dir_image
            dir_twice = square_image + mix_ratio * dir_twice
        solution = solution + step_len * direction
        residual = residual - step_len * dir_image
        res_image = res_image - step_len * dir_twice
        norm_prev = norm_now
        step_prev = step_len
    return (solution, residual, res_image)


def solution(mesh):
    placed = (P("pts", None), P("pts"), P("rhs", "pts"), P("pts", None))
    return jax.shard_map(
        per_device,
        mesh=mesh,
        in_specs=placed,
        out_specs=(P("rhs", "pts"), P("rhs", "pts"), P("rhs", "pts")),
        check_vma=False,
    )
```

```python
import functools

import jax
import jax.numpy as jnp
from jax import lax
from jax.experimental import pallas as pl
from jax.experimental.pallas import tpu as pltpu
from jax.sharding import PartitionSpec as P

F = 32
BLK = 128
REACH = 16
ITERS = 2
WIDE = 33
WEXP = 18
MESH = pl.DeviceIdType.MESH


def with_halo(cells, axis, dim, width):
    count = lax.axis_size(axis)
    ends = count - 1
    head = lax.slice_in_dim(cells, 0, width, axis=dim)
    tail = lax.slice_in_dim(cells, cells.shape[dim] - width, cells.shape[dim], axis=dim)
    return jnp.concatenate(
        [
            lax.ppermute(tail, axis, [(i, (i + 1) % count) for i in range(ends)]),
            cells,
            lax.ppermute(head, axis, [((i + 1) % count, i) for i in range(ends)]),
        ],
        axis=dim,
    )


def profile_tile(sq_left, sq_right, cross):
    dist = jnp.maximum((sq_left + sq_right) + cross, 0.0)
    radius = jnp.sqrt(dist)
    base = jnp.maximum(1.0 - radius, 0.0)
    b2 = base * base
    b4 = b2 * b2
    b8 = b4 * b4
    b16 = b8 * b8
    return (b16 * b2) * (WEXP * radius + 1.0)


def build_kernel(pat_ref, pw_ref, pwt_ref, v_ref, k_ref, out_ref, mirror, cross_ref, sqr_ref):
    a = pl.program_id(0)
    blocks = pl.num_programs(0)
    start = pl.multiple_of(a * BLK, BLK)
    left = pw_ref[pl.ds(start, BLK), :]
    left_f = left.astype(jnp.float32)
    sq_left = jnp.sum(left_f * left_f, axis=1, keepdims=True)
    left_m2 = left * jnp.asarray(-2.0, jnp.bfloat16)
    window = pwt_ref[:, pl.ds(pl.multiple_of(a * BLK, BLK), WIDE * BLK)]
    cross_ref[...] = jnp.dot(left_m2, window, preferred_element_type=jnp.float32)
    window_f = window.astype(jnp.float32)
    sqr_ref[...] = jnp.sum(window_f * window_f, axis=0, keepdims=True)

    def body(o, carry):
        col = pl.multiple_of((a + o) * BLK, BLK)
        dst = pl.ds(pl.multiple_of(o * BLK, BLK), BLK)
        live = pat_ref[a, o] != 0
        other = a + o - REACH
        lower = jnp.logical_and(other >= 0, other < a)
        upper = jnp.logical_and(other > a, other < blocks)

        @pl.when(jnp.logical_and(live, lower))
        def _():
            k_ref[0, :, dst] = mirror[a, other]

        @pl.when(jnp.logical_and(live, jnp.logical_not(lower)))
        def _():
            sq_right = sqr_ref[:, dst]
            value = profile_tile(sq_left, sq_right, cross_ref[:, dst])
            k_ref[0, :, dst] = value.astype(jnp.bfloat16)

            @pl.when(upper)
            def _():
                mirror[other, a] = value.T.astype(jnp.bfloat16)

        @pl.when(jnp.logical_not(live))
        def _():
            k_ref[0, :, dst] = jnp.zeros((BLK, BLK), jnp.bfloat16)

        return carry

    lax.fori_loop(0, WIDE, body, 0)
    v_cat = v_ref[:, pl.ds(start, WIDE * BLK)]
    out_ref[...] = lax.dot_general(
        v_cat, k_ref[0], (((1,), (1,)), ((), ())), preferred_element_type=jnp.float32
    )


def apply_kernel(v_ref, k_ref, out_ref):
    a = pl.program_id(0)
    start = pl.multiple_of(a * BLK, BLK)
    v_cat = v_ref[:, pl.ds(start, WIDE * BLK)]
    out_ref[...] = lax.dot_general(
        v_cat, k_ref[0], (((1,), (1,)), ((), ())), preferred_element_type=jnp.float32
    )


def build_k(pattern, points, wide_points_t, first_wide, blocks):
    rows = points.shape[0]
    wide_cols = wide_points_t.shape[1]
    vec_rows = first_wide.shape[0]
    return pl.pallas_call(
        build_kernel,
        out_shape=(
            jax.ShapeDtypeStruct((blocks, BLK, WIDE * BLK), jnp.bfloat16),
            jax.ShapeDtypeStruct((vec_rows, blocks * BLK), jnp.float32),
        ),
        grid_spec=pltpu.PrefetchScalarGridSpec(
            num_scalar_prefetch=1,
            grid=(blocks,),
            in_specs=[
                pl.BlockSpec((rows, F), lambda a, p: (0, 0)),
                pl.BlockSpec((F, wide_cols), lambda a, p: (0, 0)),
                pl.BlockSpec((vec_rows, wide_cols), lambda a, p: (0, 0)),
            ],
            out_specs=(
                pl.BlockSpec((1, BLK, WIDE * BLK), lambda a, p: (a, 0, 0)),
                pl.BlockSpec((vec_rows, BLK), lambda a, p: (0, a)),
            ),
            scratch_shapes=[
                pltpu.VMEM((blocks, blocks, BLK, BLK), jnp.bfloat16),
                pltpu.VMEM((BLK, WIDE * BLK), jnp.float32),
                pltpu.VMEM((1, WIDE * BLK), jnp.float32),
            ],
        ),
        compiler_params=pltpu.CompilerParams(dimension_semantics=("arbitrary",)),
    )(pattern, points, wide_points_t, first_wide)


def apply_k(wide_vec, kmat):
    rows, wide_cols = wide_vec.shape
    blocks = kmat.shape[0]
    return pl.pallas_call(
        apply_kernel,
        out_shape=jax.ShapeDtypeStruct((rows, blocks * BLK), jnp.float32),
        grid=(blocks,),
        in_specs=[
            pl.BlockSpec((rows, wide_cols), lambda a: (0, 0)),
            pl.BlockSpec((1, BLK, WIDE * BLK), lambda a: (a, 0, 0)),
        ],
        out_specs=pl.BlockSpec((rows, BLK), lambda a: (0, a)),
        compiler_params=pltpu.CompilerParams(dimension_semantics=("arbitrary",)),
    )(wide_vec, kmat)


def reduction_steps(inner, outer, part_ref, stage1, stage2, local_sem, send1, recv1, send2, recv2):
    me = lax.axis_index("pts")
    row = lax.axis_index("rhs")
    zc = me // inner
    rc = me % inner

    def greet():
        barrier = pltpu.get_barrier_semaphore()

        def greet_inner(k, carry):
            peer = zc * inner + lax.rem(rc + k, inner)
            pl.semaphore_signal(barrier, inc=1, device_id=(peer, row), device_id_type=MESH)
            return carry

        def greet_outer(k, carry):
            peer = lax.rem(zc + k, outer) * inner + rc
            pl.semaphore_signal(barrier, inc=1, device_id=(peer, row), device_id_type=MESH)
            return carry

        lax.fori_loop(1, inner, greet_inner, 0)
        lax.fori_loop(1, outer, greet_outer, 0)

    def first(slot, other):
        return pltpu.make_async_remote_copy(
            src_ref=part_ref,
            dst_ref=stage1.at[slot],
            send_sem=send1.at[other],
            recv_sem=recv1.at[slot],
            device_id=(zc * inner + other, row),
            device_id_type=MESH,
        )

    def second(slot, other):
        return pltpu.make_async_remote_copy(
            src_ref=stage1,
            dst_ref=stage2.at[slot],
            send_sem=send2.at[other],
            recv_sem=recv2.at[slot],
            device_id=(other * inner + rc, row),
            device_id_type=MESH,
        )

    own1 = pltpu.make_async_copy(part_ref, stage1.at[rc], local_sem.at[0])
    own2 = pltpu.make_async_copy(stage1, stage2.at[zc], local_sem.at[1])

    def start_first():
        own1.start()

        def send_first(k, carry):
            first(rc, lax.rem(rc + k, inner)).start()
            return carry

        lax.fori_loop(1, inner, send_first, 0)

    def start_second():
        def finish_first(k, carry):
            other = lax.rem(rc + k, inner)
            first(rc, other).wait_send()
            first(other, other).wait_recv()
            return carry

        lax.fori_loop(1, inner, finish_first, 0)
        own1.wait()
        own2.start()

        def send_second(k, carry):
            second(zc, lax.rem(zc + k, outer)).start()
            return carry

        lax.fori_loop(1, outer, send_second, 0)

    def finish():
        def finish_second(k, carry):
            other = lax.rem(zc + k, outer)
            second(zc, other).wait_send()
            second(other, other).wait_recv()
            return carry

        lax.fori_loop(1, outer, finish_second, 0)
        own2.wait()
        return jnp.sum(jnp.sum(stage2[...], axis=0), axis=0)

    return greet, start_first, start_second, finish


def apply_sum_kernel(inner, outer, vloc_ref, k_ref, part_ref, out_ref, sum_ref, v_ref, halo_send, halo_recv, halo_local, *scratch):
    a = pl.program_id(0)
    last = pl.num_programs(0) - 1
    greet, start_first, start_second, finish = reduction_steps(inner, outer, part_ref, *scratch)
    me = lax.axis_index("pts")
    row = lax.axis_index("rhs")
    count = inner * outer
    rc = me % inner
    width = vloc_ref.shape[1]
    has_left = me > 0
    has_right = me < count - 1
    extra = jnp.logical_or(
        jnp.logical_and(rc == 0, has_left), jnp.logical_and(rc == inner - 1, has_right)
    )

    def to_right():
        return pltpu.make_async_remote_copy(
            src_ref=vloc_ref,
            dst_ref=v_ref.at[:, pl.ds(0, width)],
            send_sem=halo_send.at[0],
            recv_sem=halo_recv.at[0],
            device_id=(me + 1, row),
            device_id_type=MESH,
        )

    def to_left():
        return pltpu.make_async_remote_copy(
            src_ref=vloc_ref,
            dst_ref=v_ref.at[:, pl.ds(2 * width, width)],
            send_sem=halo_send.at[1],
            recv_sem=halo_recv.at[1],
            device_id=(me - 1, row),
            device_id_type=MESH,
        )

    def from_left():
        return pltpu.make_async_remote_copy(
            src_ref=vloc_ref,
            dst_ref=v_ref.at[:, pl.ds(0, width)],
            send_sem=halo_send.at[0],
            recv_sem=halo_recv.at[0],
            device_id=(me - 1, row),
            device_id_type=MESH,
        )

    def from_right():
        return pltpu.make_async_remote_copy(
            src_ref=vloc_ref,
            dst_ref=v_ref.at[:, pl.ds(2 * width, width)],
            send_sem=halo_send.at[1],
            recv_sem=halo_recv.at[1],
            device_id=(me + 1, row),
            device_id_type=MESH,
        )

    own = pltpu.make_async_copy(vloc_ref, v_ref.at[:, pl.ds(width, width)], halo_local.at[0])

    @pl.when(a == 0)
    def _():
        greet()
        barrier = pltpu.get_barrier_semaphore()

        @pl.when(jnp.logical_and(extra, rc == 0))
        def _():
            pl.semaphore_signal(barrier, inc=1, device_id=(me - 1, row), device_id_type=MESH)

        @pl.when(jnp.logical_and(extra, rc == inner - 1))
        def _():
            pl.semaphore_signal(barrier, inc=1, device_id=(me + 1, row), device_id_type=MESH)

        peers = (inner - 1) + (outer - 1)

        @pl.when(extra)
        def _():
            pl.semaphore_wait(barrier, peers + 1)

        @pl.when(jnp.logical_not(extra))
        def _():
            pl.semaphore_wait(barrier, peers)

        start_first()
        own.start()

        @pl.when(has_right)
        def _():
            to_right().start()

        @pl.when(has_left)
        def _():
            to_left().start()

        @pl.when(jnp.logical_not(has_left))
        def _():
            v_ref[:, pl.ds(0, width)] = jnp.zeros((v_ref.shape[0], width), v_ref.dtype)

        @pl.when(jnp.logical_not(has_right))
        def _():
            v_ref[:, pl.ds(2 * width, width)] = jnp.zeros((v_ref.shape[0], width), v_ref.dtype)

        own.wait()

        @pl.when(has_right)
        def _():
            to_right().wait_send()
            from_right().wait_recv()

        @pl.when(has_left)
        def _():
            to_left().wait_send()
            from_left().wait_recv()

    blocks = v_ref.shape[1] // BLK - 2 * REACH

    @pl.when(a == min(blocks // 2 - 2, blocks - 1))
    def _():
        start_second()

    start = pl.multiple_of(a * BLK, BLK)
    v_cat = v_ref[:, pl.ds(start, WIDE * BLK)]
    out_ref[...] = lax.dot_general(
        v_cat, k_ref[0], (((1,), (1,)), ((), ())), preferred_element_type=jnp.float32
    )

    @pl.when(a == last)
    def _():
        sum_ref[...] = finish()


def apply_sum(local_vec, kmat, tile):
    rows, width = local_vec.shape
    wide_cols = width + 2 * REACH * BLK
    blocks = kmat.shape[0]
    count = lax.axis_size("pts")
    inner = 8 if count % 8 == 0 else count
    outer = count // inner
    return pl.pallas_call(
        functools.partial(apply_sum_kernel, inner, outer),
        out_shape=(
            jax.ShapeDtypeStruct((rows, blocks * BLK), jnp.float32),
            jax.ShapeDtypeStruct(tile.shape, jnp.float32),
        ),
        grid=(blocks,),
        in_specs=[
            pl.BlockSpec((rows, width), lambda a: (0, 0)),
            pl.BlockSpec((1, BLK, WIDE * BLK), lambda a: (a, 0, 0)),
            pl.BlockSpec(tile.shape, lambda a: (0, 0)),
        ],
        out_specs=(
            pl.BlockSpec((rows, BLK), lambda a: (0, a)),
            pl.BlockSpec(tile.shape, lambda a: (0, 0)),
        ),
        scratch_shapes=[
            pltpu.VMEM((rows, wide_cols), local_vec.dtype),
            pltpu.SemaphoreType.DMA((2,)),
            pltpu.SemaphoreType.DMA((2,)),
            pltpu.SemaphoreType.DMA((1,)),
            pltpu.VMEM((inner,) + tile.shape, jnp.float32),
            pltpu.VMEM((outer, inner) + tile.shape, jnp.float32),
            pltpu.SemaphoreType.DMA((2,)),
            pltpu.SemaphoreType.DMA((inner,)),
            pltpu.SemaphoreType.DMA((inner,)),
            pltpu.SemaphoreType.DMA((outer,)),
            pltpu.SemaphoreType.DMA((outer,)),
        ],
        compiler_params=pltpu.CompilerParams(
            dimension_semantics=("arbitrary",), collective_id=0, has_side_effects=True
        ),
    )(local_vec, kmat, tile)


def per_device(points, noise_var, right_side, pattern):
    local_rows = points.shape[0]
    block_count = local_rows // BLK
    rim_rows = REACH * BLK
    kernel_scale = 1.0 / (4 * BLK)
    first_low = right_side.astype(jnp.bfloat16)
    points_t = points.T
    packed = jnp.concatenate([points_t, first_low], axis=0)
    count = lax.axis_size("pts")
    from_left = lax.ppermute(packed, "pts", [(i, i + 1) for i in range(count - 1)])
    from_right = lax.ppermute(packed, "pts", [(i + 1, i) for i in range(count - 1)])
    wide_points_t = jnp.concatenate([from_left[:F], points_t, from_right[:F]], axis=1)
    first_wide = jnp.concatenate([from_left[F:], first_low, from_right[F:]], axis=1)
    kmat, first_image = build_k(pattern, points, wide_points_t, first_wide, block_count)

    rhs_count = lax.axis_size("rhs")
    rhs_index = lax.axis_index("rhs")

    def apply_operator(vector):
        vec_low = vector.astype(jnp.bfloat16)
        wide_vec = with_halo(vec_low, "pts", 1, rim_rows)
        image_part = apply_k(wide_vec, kmat)
        return noise_var[None, :] * vector + kernel_scale * image_part

    def apply_and_total(vector, parts):
        tile = jnp.zeros((8, 128), jnp.float32)
        tile = lax.dynamic_update_slice(tile, parts, (0, 0))
        vec_low = vector.astype(jnp.bfloat16)
        image_part, summed = apply_sum(vec_low, kmat, tile)
        image = noise_var[None, :] * vector + kernel_scale * image_part
        return image, summed[: parts.shape[0], : parts.shape[1]]

    solution = jnp.zeros_like(right_side)
    residual = right_side
    res_image = noise_var[None, :] * residual + kernel_scale * first_image
    direction = jnp.zeros_like(right_side)
    dir_image = jnp.zeros_like(right_side)
    dir_twice = jnp.zeros_like(right_side)
    norm_prev = None
    step_prev = None
    for iteration in range(ITERS):
        square_image, sums = apply_and_total(
            res_image,
            jnp.stack([jnp.sum(residual * residual, axis=1), jnp.sum(res_image * residual, axis=1)]),
        )
        norm_now = sums[0][:, None]
        curvature = sums[1][:, None]
        if iteration == 0:
            step_len = norm_now / curvature
            direction = residual
            dir_image = res_image
            dir_twice = square_image
        else:
            mix_ratio = norm_now / norm_prev
            step_len = norm_now / (curvature - mix_ratio * norm_now / step_prev)
            direction = residual + mix_ratio * direction
            dir_image = res_image + mix_ratio * dir_image
            dir_twice = square_image + mix_ratio * dir_twice
        solution = solution + step_len * direction
        residual = residual - step_len * dir_image
        res_image = res_image - step_len * dir_twice
        norm_prev = norm_now
        step_prev = step_len
    return (solution, residual, res_image)


def solution(mesh):
    placed = (P("pts", None), P("pts"), P("rhs", "pts"), P("pts", None))
    return jax.shard_map(
        per_device,
        mesh=mesh,
        in_specs=placed,
        out_specs=(P("rhs", "pts"), P("rhs", "pts"), P("rhs", "pts")),
        check_vma=False,
    )
```

```python
import functools

import jax
import jax.numpy as jnp
from jax import lax
from jax.experimental import pallas as pl
from jax.experimental.pallas import tpu as pltpu
from jax.sharding import PartitionSpec as P

F = 32
BLK = 128
REACH = 16
ITERS = 2
WIDE = 33
WEXP = 18
MESH = pl.DeviceIdType.MESH


def with_halo(cells, axis, dim, width):
    count = lax.axis_size(axis)
    ends = count - 1
    head = lax.slice_in_dim(cells, 0, width, axis=dim)
    tail = lax.slice_in_dim(cells, cells.shape[dim] - width, cells.shape[dim], axis=dim)
    return jnp.concatenate(
        [
            lax.ppermute(tail, axis, [(i, (i + 1) % count) for i in range(ends)]),
            cells,
            lax.ppermute(head, axis, [((i + 1) % count, i) for i in range(ends)]),
        ],
        axis=dim,
    )


def profile_tile(sq_left, sq_right, cross):
    dist = jnp.maximum((sq_left + sq_right) + cross, 0.0)
    radius = jnp.sqrt(dist)
    base = jnp.maximum(1.0 - radius, 0.0)
    b2 = base * base
    b4 = b2 * b2
    b8 = b4 * b4
    b16 = b8 * b8
    return (b16 * b2) * (WEXP * radius + 1.0)


def build_kernel(pat_ref, pw_ref, pwt_ref, k_ref, mirror, cross_ref, sqr_ref):
    a = pl.program_id(0)
    blocks = pl.num_programs(0)
    start = pl.multiple_of(a * BLK, BLK)
    left = pw_ref[pl.ds(start, BLK), :]
    left_f = left.astype(jnp.float32)
    sq_left = jnp.sum(left_f * left_f, axis=1, keepdims=True)
    left_m2 = left * jnp.asarray(-2.0, jnp.bfloat16)
    window = pwt_ref[:, pl.ds(pl.multiple_of(a * BLK, BLK), WIDE * BLK)]
    cross_ref[...] = jnp.dot(left_m2, window, preferred_element_type=jnp.float32)
    window_f = window.astype(jnp.float32)
    sqr_ref[...] = jnp.sum(window_f * window_f, axis=0, keepdims=True)

    def body(o, carry):
        col = pl.multiple_of((a + o) * BLK, BLK)
        dst = pl.ds(pl.multiple_of(o * BLK, BLK), BLK)
        live = pat_ref[a, o] != 0
        other = a + o - REACH
        lower = jnp.logical_and(other >= 0, other < a)
        upper = jnp.logical_and(other > a, other < blocks)

        @pl.when(jnp.logical_and(live, lower))
        def _():
            k_ref[0, :, dst] = mirror[a, other]

        @pl.when(jnp.logical_and(live, jnp.logical_not(lower)))
        def _():
            sq_right = sqr_ref[:, dst]
            value = profile_tile(sq_left, sq_right, cross_ref[:, dst])
            k_ref[0, :, dst] = value.astype(jnp.bfloat16)

            @pl.when(upper)
            def _():
                mirror[other, a] = value.T.astype(jnp.bfloat16)

        @pl.when(jnp.logical_not(live))
        def _():
            k_ref[0, :, dst] = jnp.zeros((BLK, BLK), jnp.bfloat16)

        return carry

    lax.fori_loop(0, WIDE, body, 0)


def apply_kernel(v_ref, k_ref, out_ref):
    a = pl.program_id(0)
    start = pl.multiple_of(a * BLK, BLK)
    v_cat = v_ref[:, pl.ds(start, WIDE * BLK)]
    out_ref[...] = lax.dot_general(
        v_cat, k_ref[0], (((1,), (1,)), ((), ())), preferred_element_type=jnp.float32
    )


def build_k(pattern, points, wide_points_t, blocks):
    rows = points.shape[0]
    wide_cols = wide_points_t.shape[1]
    return pl.pallas_call(
        build_kernel,
        out_shape=jax.ShapeDtypeStruct((blocks, BLK, WIDE * BLK), jnp.bfloat16),
        grid_spec=pltpu.PrefetchScalarGridSpec(
            num_scalar_prefetch=1,
            grid=(blocks,),
            in_specs=[
                pl.BlockSpec((rows, F), lambda a, p: (0, 0)),
                pl.BlockSpec((F, wide_cols), lambda a, p: (0, 0)),
            ],
            out_specs=pl.BlockSpec((1, BLK, WIDE * BLK), lambda a, p: (a, 0, 0)),
            scratch_shapes=[
                pltpu.VMEM((blocks, blocks, BLK, BLK), jnp.bfloat16),
                pltpu.VMEM((BLK, WIDE * BLK), jnp.float32),
                pltpu.VMEM((1, WIDE * BLK), jnp.float32),
            ],
        ),
        compiler_params=pltpu.CompilerParams(dimension_semantics=("arbitrary",)),
    )(pattern, points, wide_points_t)


def apply_k(wide_vec, kmat):
    rows, wide_cols = wide_vec.shape
    blocks = kmat.shape[0]
    return pl.pallas_call(
        apply_kernel,
        out_shape=jax.ShapeDtypeStruct((rows, blocks * BLK), jnp.float32),
        grid=(blocks,),
        in_specs=[
            pl.BlockSpec((rows, wide_cols), lambda a: (0, 0)),
            pl.BlockSpec((1, BLK, WIDE * BLK), lambda a: (a, 0, 0)),
        ],
        out_specs=pl.BlockSpec((rows, BLK), lambda a: (0, a)),
        compiler_params=pltpu.CompilerParams(dimension_semantics=("arbitrary",)),
    )(wide_vec, kmat)


def reduction_steps(inner, outer, part_ref, stage1, stage2, local_sem, send1, recv1, send2, recv2):
    me = lax.axis_index("pts")
    row = lax.axis_index("rhs")
    zc = me // inner
    rc = me % inner

    def greet():
        barrier = pltpu.get_barrier_semaphore()

        def greet_inner(k, carry):
            peer = zc * inner + lax.rem(rc + k, inner)
            pl.semaphore_signal(barrier, inc=1, device_id=(peer, row), device_id_type=MESH)
            return carry

        def greet_outer(k, carry):
            peer = lax.rem(zc + k, outer) * inner + rc
            pl.semaphore_signal(barrier, inc=1, device_id=(peer, row), device_id_type=MESH)
            return carry

        lax.fori_loop(1, inner, greet_inner, 0)
        lax.fori_loop(1, outer, greet_outer, 0)

    def first(slot, other):
        return pltpu.make_async_remote_copy(
            src_ref=part_ref,
            dst_ref=stage1.at[slot],
            send_sem=send1.at[other],
            recv_sem=recv1.at[slot],
            device_id=(zc * inner + other, row),
            device_id_type=MESH,
        )

    def second(slot, other):
        return pltpu.make_async_remote_copy(
            src_ref=stage1,
            dst_ref=stage2.at[slot],
            send_sem=send2.at[other],
            recv_sem=recv2.at[slot],
            device_id=(other * inner + rc, row),
            device_id_type=MESH,
        )

    own1 = pltpu.make_async_copy(part_ref, stage1.at[rc], local_sem.at[0])
    own2 = pltpu.make_async_copy(stage1, stage2.at[zc], local_sem.at[1])

    def start_first():
        own1.start()

        def send_first(k, carry):
            first(rc, lax.rem(rc + k, inner)).start()
            return carry

        lax.fori_loop(1, inner, send_first, 0)

    def start_second():
        def finish_first(k, carry):
            other = lax.rem(rc + k, inner)
            first(rc, other).wait_send()
            first(other, other).wait_recv()
            return carry

        lax.fori_loop(1, inner, finish_first, 0)
        own1.wait()
        own2.start()

        def send_second(k, carry):
            second(zc, lax.rem(zc + k, outer)).start()
            return carry

        lax.fori_loop(1, outer, send_second, 0)

    def finish():
        def finish_second(k, carry):
            other = lax.rem(zc + k, outer)
            second(zc, other).wait_send()
            second(other, other).wait_recv()
            return carry

        lax.fori_loop(1, outer, finish_second, 0)
        own2.wait()
        return jnp.sum(jnp.sum(stage2[...], axis=0), axis=0)

    return greet, start_first, start_second, finish


def apply_sum_kernel(inner, outer, vloc_ref, k_ref, part_ref, out_ref, sum_ref, v_ref, halo_send, halo_recv, halo_local, *scratch):
    a = pl.program_id(0)
    last = pl.num_programs(0) - 1
    greet, start_first, start_second, finish = reduction_steps(inner, outer, part_ref, *scratch)
    me = lax.axis_index("pts")
    row = lax.axis_index("rhs")
    count = inner * outer
    rc = me % inner
    width = vloc_ref.shape[1]
    has_left = me > 0
    has_right = me < count - 1
    extra = jnp.logical_or(
        jnp.logical_and(rc == 0, has_left), jnp.logical_and(rc == inner - 1, has_right)
    )

    def to_right():
        return pltpu.make_async_remote_copy(
            src_ref=vloc_ref,
            dst_ref=v_ref.at[:, pl.ds(0, width)],
            send_sem=halo_send.at[0],
            recv_sem=halo_recv.at[0],
            device_id=(me + 1, row),
            device_id_type=MESH,
        )

    def to_left():
        return pltpu.make_async_remote_copy(
            src_ref=vloc_ref,
            dst_ref=v_ref.at[:, pl.ds(2 * width, width)],
            send_sem=halo_send.at[1],
            recv_sem=halo_recv.at[1],
            device_id=(me - 1, row),
            device_id_type=MESH,
        )

    def from_left():
        return pltpu.make_async_remote_copy(
            src_ref=vloc_ref,
            dst_ref=v_ref.at[:, pl.ds(0, width)],
            send_sem=halo_send.at[0],
            recv_sem=halo_recv.at[0],
            device_id=(me - 1, row),
            device_id_type=MESH,
        )

    def from_right():
        return pltpu.make_async_remote_copy(
            src_ref=vloc_ref,
            dst_ref=v_ref.at[:, pl.ds(2 * width, width)],
            send_sem=halo_send.at[1],
            recv_sem=halo_recv.at[1],
            device_id=(me + 1, row),
            device_id_type=MESH,
        )

    own = pltpu.make_async_copy(vloc_ref, v_ref.at[:, pl.ds(width, width)], halo_local.at[0])

    @pl.when(a == 0)
    def _():
        greet()
        barrier = pltpu.get_barrier_semaphore()

        @pl.when(jnp.logical_and(extra, rc == 0))
        def _():
            pl.semaphore_signal(barrier, inc=1, device_id=(me - 1, row), device_id_type=MESH)

        @pl.when(jnp.logical_and(extra, rc == inner - 1))
        def _():
            pl.semaphore_signal(barrier, inc=1, device_id=(me + 1, row), device_id_type=MESH)

        peers = (inner - 1) + (outer - 1)

        @pl.when(extra)
        def _():
            pl.semaphore_wait(barrier, peers + 1)

        @pl.when(jnp.logical_not(extra))
        def _():
            pl.semaphore_wait(barrier, peers)

        start_first()
        own.start()

        @pl.when(has_right)
        def _():
            to_right().start()

        @pl.when(has_left)
        def _():
            to_left().start()

        @pl.when(jnp.logical_not(has_left))
        def _():
            v_ref[:, pl.ds(0, width)] = jnp.zeros((v_ref.shape[0], width), v_ref.dtype)

        @pl.when(jnp.logical_not(has_right))
        def _():
            v_ref[:, pl.ds(2 * width, width)] = jnp.zeros((v_ref.shape[0], width), v_ref.dtype)

        own.wait()

        @pl.when(has_right)
        def _():
            to_right().wait_send()
            from_right().wait_recv()

        @pl.when(has_left)
        def _():
            to_left().wait_send()
            from_left().wait_recv()

    blocks = v_ref.shape[1] // BLK - 2 * REACH

    @pl.when(a == min(blocks // 2, blocks - 1))
    def _():
        start_second()

    start = pl.multiple_of(a * BLK, BLK)
    v_cat = v_ref[:, pl.ds(start, WIDE * BLK)]
    out_ref[...] = lax.dot_general(
        v_cat, k_ref[0], (((1,), (1,)), ((), ())), preferred_element_type=jnp.float32
    )

    @pl.when(a == last)
    def _():
        sum_ref[...] = finish()


def apply_sum(local_vec, kmat, tile):
    rows, width = local_vec.shape
    wide_cols = width + 2 * REACH * BLK
    blocks = kmat.shape[0]
    count = lax.axis_size("pts")
    inner = 8 if count % 8 == 0 else count
    outer = count // inner
    return pl.pallas_call(
        functools.partial(apply_sum_kernel, inner, outer),
        out_shape=(
            jax.ShapeDtypeStruct((rows, blocks * BLK), jnp.float32),
            jax.ShapeDtypeStruct(tile.shape, jnp.float32),
        ),
        grid=(blocks,),
        in_specs=[
            pl.BlockSpec((rows, width), lambda a: (0, 0)),
            pl.BlockSpec((1, BLK, WIDE * BLK), lambda a: (a, 0, 0)),
            pl.BlockSpec(tile.shape, lambda a: (0, 0)),
        ],
        out_specs=(
            pl.BlockSpec((rows, BLK), lambda a: (0, a)),
            pl.BlockSpec(tile.shape, lambda a: (0, 0)),
        ),
        scratch_shapes=[
            pltpu.VMEM((rows, wide_cols), local_vec.dtype),
            pltpu.SemaphoreType.DMA((2,)),
            pltpu.SemaphoreType.DMA((2,)),
            pltpu.SemaphoreType.DMA((1,)),
            pltpu.VMEM((inner,) + tile.shape, jnp.float32),
            pltpu.VMEM((outer, inner) + tile.shape, jnp.float32),
            pltpu.SemaphoreType.DMA((2,)),
            pltpu.SemaphoreType.DMA((inner,)),
            pltpu.SemaphoreType.DMA((inner,)),
            pltpu.SemaphoreType.DMA((outer,)),
            pltpu.SemaphoreType.DMA((outer,)),
        ],
        compiler_params=pltpu.CompilerParams(
            dimension_semantics=("arbitrary",), collective_id=0, has_side_effects=True
        ),
    )(local_vec, kmat, tile)


def per_device(points, noise_var, right_side, pattern):
    local_rows = points.shape[0]
    block_count = local_rows // BLK
    rim_rows = REACH * BLK
    kernel_scale = 1.0 / (4 * BLK)
    first_low = right_side.astype(jnp.bfloat16)
    points_t = points.T
    packed = jnp.concatenate([points_t, first_low], axis=0)
    count = lax.axis_size("pts")
    from_left = lax.ppermute(packed, "pts", [(i, i + 1) for i in range(count - 1)])
    from_right = lax.ppermute(packed, "pts", [(i + 1, i) for i in range(count - 1)])
    wide_points_t = jnp.concatenate([from_left[:F], points_t, from_right[:F]], axis=1)
    first_wide = jnp.concatenate([from_left[F:], first_low, from_right[F:]], axis=1)
    kmat = build_k(pattern, points, wide_points_t, block_count)

    rhs_count = lax.axis_size("rhs")
    rhs_index = lax.axis_index("rhs")

    def apply_operator(vector):
        vec_low = vector.astype(jnp.bfloat16)
        wide_vec = with_halo(vec_low, "pts", 1, rim_rows)
        image_part = apply_k(wide_vec, kmat)
        return noise_var[None, :] * vector + kernel_scale * image_part

    def apply_and_total(vector, parts):
        tile = jnp.zeros((8, 128), jnp.float32)
        tile = lax.dynamic_update_slice(tile, parts, (0, 0))
        vec_low = vector.astype(jnp.bfloat16)
        image_part, summed = apply_sum(vec_low, kmat, tile)
        image = noise_var[None, :] * vector + kernel_scale * image_part
        return image, summed[: parts.shape[0], : parts.shape[1]]

    solution = jnp.zeros_like(right_side)
    residual = right_side
    res_image = noise_var[None, :] * residual + kernel_scale * apply_k(first_wide, kmat)
    direction = jnp.zeros_like(right_side)
    dir_image = jnp.zeros_like(right_side)
    dir_twice = jnp.zeros_like(right_side)
    norm_prev = None
    step_prev = None
    for iteration in range(ITERS):
        square_image, sums = apply_and_total(
            res_image,
            jnp.stack([jnp.sum(residual * residual, axis=1), jnp.sum(res_image * residual, axis=1)]),
        )
        norm_now = sums[0][:, None]
        curvature = sums[1][:, None]
        if iteration == 0:
            step_len = norm_now / curvature
            direction = residual
            dir_image = res_image
            dir_twice = square_image
        else:
            mix_ratio = norm_now / norm_prev
            step_len = norm_now / (curvature - mix_ratio * norm_now / step_prev)
            direction = residual + mix_ratio * direction
            dir_image = res_image + mix_ratio * dir_image
            dir_twice = square_image + mix_ratio * dir_twice
        solution = solution + step_len * direction
        residual = residual - step_len * dir_image
        res_image = res_image - step_len * dir_twice
        norm_prev = norm_now
        step_prev = step_len
    return (solution, residual, res_image)


def solution(mesh):
    placed = (P("pts", None), P("pts"), P("rhs", "pts"), P("pts", None))
    return jax.shard_map(
        per_device,
        mesh=mesh,
        in_specs=placed,
        out_specs=(P("rhs", "pts"), P("rhs", "pts"), P("rhs", "pts")),
        check_vma=False,
    )
```

```python
import functools

import jax
import jax.numpy as jnp
from jax import lax
from jax.experimental import pallas as pl
from jax.experimental.pallas import tpu as pltpu
from jax.sharding import PartitionSpec as P

F = 32
BLK = 128
REACH = 16
ITERS = 2
WIDE = 33
WEXP = 18
MESH = pl.DeviceIdType.MESH


def with_halo(cells, axis, dim, width):
    count = lax.axis_size(axis)
    ends = count - 1
    head = lax.slice_in_dim(cells, 0, width, axis=dim)
    tail = lax.slice_in_dim(cells, cells.shape[dim] - width, cells.shape[dim], axis=dim)
    return jnp.concatenate(
        [
            lax.ppermute(tail, axis, [(i, (i + 1) % count) for i in range(ends)]),
            cells,
            lax.ppermute(head, axis, [((i + 1) % count, i) for i in range(ends)]),
        ],
        axis=dim,
    )


def profile_tile(sq_left, sq_right, cross):
    dist = jnp.maximum((sq_left + sq_right) + cross, 0.0)
    radius = jnp.sqrt(dist)
    base = jnp.maximum(1.0 - radius, 0.0)
    b2 = base * base
    b4 = b2 * b2
    b8 = b4 * b4
    b16 = b8 * b8
    return (b16 * b2) * (WEXP * radius + 1.0)


def build_kernel(pat_ref, pw_ref, pwt_ref, k_ref, mirror, cross_ref, sqr_ref):
    a = pl.program_id(0)
    blocks = pl.num_programs(0)
    start = pl.multiple_of(a * BLK, BLK)
    left = pw_ref[pl.ds(start, BLK), :]
    left_f = left.astype(jnp.float32)
    sq_left = jnp.sum(left_f * left_f, axis=1, keepdims=True)
    left_m2 = left * jnp.asarray(-2.0, jnp.bfloat16)
    window = pwt_ref[:, pl.ds(pl.multiple_of(a * BLK, BLK), WIDE * BLK)]
    cross_ref[...] = jnp.dot(left_m2, window, preferred_element_type=jnp.float32)
    window_f = window.astype(jnp.float32)
    sqr_ref[...] = jnp.sum(window_f * window_f, axis=0, keepdims=True)

    def body(o, carry):
        col = pl.multiple_of((a + o) * BLK, BLK)
        dst = pl.ds(pl.multiple_of(o * BLK, BLK), BLK)
        live = pat_ref[a, o] != 0
        other = a + o - REACH
        lower = jnp.logical_and(other >= 0, other < a)
        upper = jnp.logical_and(other > a, other < blocks)

        @pl.when(jnp.logical_and(live, lower))
        def _():
            k_ref[0, :, dst] = mirror[a, other]

        @pl.when(jnp.logical_and(live, jnp.logical_not(lower)))
        def _():
            sq_right = sqr_ref[:, dst]
            value = profile_tile(sq_left, sq_right, cross_ref[:, dst])
            k_ref[0, :, dst] = value.astype(jnp.bfloat16)

            @pl.when(upper)
            def _():
                mirror[other, a] = value.T.astype(jnp.bfloat16)

        @pl.when(jnp.logical_not(live))
        def _():
            k_ref[0, :, dst] = jnp.zeros((BLK, BLK), jnp.bfloat16)

        return carry

    lax.fori_loop(0, WIDE, body, 0)


def apply_kernel(v_ref, k_ref, out_ref):
    a = pl.program_id(0)
    start = pl.multiple_of(a * BLK, BLK)
    v_cat = v_ref[:, pl.ds(start, WIDE * BLK)]
    out_ref[...] = lax.dot_general(
        v_cat, k_ref[0], (((1,), (1,)), ((), ())), preferred_element_type=jnp.float32
    )


def build_k(pattern, points, wide_points_t, blocks):
    rows = points.shape[0]
    wide_cols = wide_points_t.shape[1]
    return pl.pallas_call(
        build_kernel,
        out_shape=jax.ShapeDtypeStruct((blocks, BLK, WIDE * BLK), jnp.bfloat16),
        grid_spec=pltpu.PrefetchScalarGridSpec(
            num_scalar_prefetch=1,
            grid=(blocks,),
            in_specs=[
                pl.BlockSpec((rows, F), lambda a, p: (0, 0)),
                pl.BlockSpec((F, wide_cols), lambda a, p: (0, 0)),
            ],
            out_specs=pl.BlockSpec((1, BLK, WIDE * BLK), lambda a, p: (a, 0, 0)),
            scratch_shapes=[
                pltpu.VMEM((blocks, blocks, BLK, BLK), jnp.bfloat16),
                pltpu.VMEM((BLK, WIDE * BLK), jnp.float32),
                pltpu.VMEM((1, WIDE * BLK), jnp.float32),
            ],
        ),
        compiler_params=pltpu.CompilerParams(dimension_semantics=("arbitrary",)),
    )(pattern, points, wide_points_t)


def apply_k(wide_vec, kmat):
    rows, wide_cols = wide_vec.shape
    blocks = kmat.shape[0]
    return pl.pallas_call(
        apply_kernel,
        out_shape=jax.ShapeDtypeStruct((rows, blocks * BLK), jnp.float32),
        grid=(blocks,),
        in_specs=[
            pl.BlockSpec((rows, wide_cols), lambda a: (0, 0)),
            pl.BlockSpec((1, BLK, WIDE * BLK), lambda a: (a, 0, 0)),
        ],
        out_specs=pl.BlockSpec((rows, BLK), lambda a: (0, a)),
        compiler_params=pltpu.CompilerParams(dimension_semantics=("arbitrary",)),
    )(wide_vec, kmat)


def reduction_steps(inner, outer, part_ref, stage1, stage2, local_sem, send1, recv1, send2, recv2):
    me = lax.axis_index("pts")
    row = lax.axis_index("rhs")
    zc = me // inner
    rc = me % inner

    def greet():
        barrier = pltpu.get_barrier_semaphore()

        def greet_inner(k, carry):
            peer = zc * inner + lax.rem(rc + k, inner)
            pl.semaphore_signal(barrier, inc=1, device_id=(peer, row), device_id_type=MESH)
            return carry

        def greet_outer(k, carry):
            peer = lax.rem(zc + k, outer) * inner + rc
            pl.semaphore_signal(barrier, inc=1, device_id=(peer, row), device_id_type=MESH)
            return carry

        lax.fori_loop(1, inner, greet_inner, 0)
        lax.fori_loop(1, outer, greet_outer, 0)

    def first(slot, other):
        return pltpu.make_async_remote_copy(
            src_ref=part_ref,
            dst_ref=stage1.at[slot],
            send_sem=send1.at[other],
            recv_sem=recv1.at[slot],
            device_id=(zc * inner + other, row),
            device_id_type=MESH,
        )

    def second(slot, other):
        return pltpu.make_async_remote_copy(
            src_ref=stage1,
            dst_ref=stage2.at[slot],
            send_sem=send2.at[other],
            recv_sem=recv2.at[slot],
            device_id=(other * inner + rc, row),
            device_id_type=MESH,
        )

    own1 = pltpu.make_async_copy(part_ref, stage1.at[rc], local_sem.at[0])
    own2 = pltpu.make_async_copy(stage1, stage2.at[zc], local_sem.at[1])

    def start_first():
        own1.start()

        def send_first(k, carry):
            first(rc, lax.rem(rc + k, inner)).start()
            return carry

        lax.fori_loop(1, inner, send_first, 0)

    def start_second():
        def finish_first(k, carry):
            other = lax.rem(rc + k, inner)
            first(rc, other).wait_send()
            first(other, other).wait_recv()
            return carry

        lax.fori_loop(1, inner, finish_first, 0)
        own1.wait()
        own2.start()

        def send_second(k, carry):
            second(zc, lax.rem(zc + k, outer)).start()
            return carry

        lax.fori_loop(1, outer, send_second, 0)

    def finish():
        def finish_second(k, carry):
            other = lax.rem(zc + k, outer)
            second(zc, other).wait_send()
            second(other, other).wait_recv()
            return carry

        lax.fori_loop(1, outer, finish_second, 0)
        own2.wait()
        return jnp.sum(jnp.sum(stage2[...], axis=0), axis=0)

    return greet, start_first, start_second, finish


def apply_sum_kernel(inner, outer, vloc_ref, k_ref, part_ref, out_ref, sum_ref, v_ref, halo_send, halo_recv, halo_local, *scratch):
    a = pl.program_id(0)
    last = pl.num_programs(0) - 1
    greet, start_first, start_second, finish = reduction_steps(inner, outer, part_ref, *scratch)
    me = lax.axis_index("pts")
    row = lax.axis_index("rhs")
    count = inner * outer
    rc = me % inner
    width = vloc_ref.shape[1]
    has_left = me > 0
    has_right = me < count - 1
    extra = jnp.logical_or(
        jnp.logical_and(rc == 0, has_left), jnp.logical_and(rc == inner - 1, has_right)
    )

    def to_right():
        return pltpu.make_async_remote_copy(
            src_ref=vloc_ref,
            dst_ref=v_ref.at[:, pl.ds(0, width)],
            send_sem=halo_send.at[0],
            recv_sem=halo_recv.at[0],
            device_id=(me + 1, row),
            device_id_type=MESH,
        )

    def to_left():
        return pltpu.make_async_remote_copy(
            src_ref=vloc_ref,
            dst_ref=v_ref.at[:, pl.ds(2 * width, width)],
            send_sem=halo_send.at[1],
            recv_sem=halo_recv.at[1],
            device_id=(me - 1, row),
            device_id_type=MESH,
        )

    def from_left():
        return pltpu.make_async_remote_copy(
            src_ref=vloc_ref,
            dst_ref=v_ref.at[:, pl.ds(0, width)],
            send_sem=halo_send.at[0],
            recv_sem=halo_recv.at[0],
            device_id=(me - 1, row),
            device_id_type=MESH,
        )

    def from_right():
        return pltpu.make_async_remote_copy(
            src_ref=vloc_ref,
            dst_ref=v_ref.at[:, pl.ds(2 * width, width)],
            send_sem=halo_send.at[1],
            recv_sem=halo_recv.at[1],
            device_id=(me + 1, row),
            device_id_type=MESH,
        )

    own = pltpu.make_async_copy(vloc_ref, v_ref.at[:, pl.ds(width, width)], halo_local.at[0])

    @pl.when(a == 0)
    def _():
        greet()
        barrier = pltpu.get_barrier_semaphore()

        @pl.when(jnp.logical_and(extra, rc == 0))
        def _():
            pl.semaphore_signal(barrier, inc=1, device_id=(me - 1, row), device_id_type=MESH)

        @pl.when(jnp.logical_and(extra, rc == inner - 1))
        def _():
            pl.semaphore_signal(barrier, inc=1, device_id=(me + 1, row), device_id_type=MESH)

        peers = (inner - 1) + (outer - 1)

        @pl.when(extra)
        def _():
            pl.semaphore_wait(barrier, peers + 1)

        @pl.when(jnp.logical_not(extra))
        def _():
            pl.semaphore_wait(barrier, peers)

        start_first()
        own.start()

        @pl.when(has_right)
        def _():
            to_right().start()

        @pl.when(has_left)
        def _():
            to_left().start()

        @pl.when(jnp.logical_not(has_left))
        def _():
            v_ref[:, pl.ds(0, width)] = jnp.zeros((v_ref.shape[0], width), v_ref.dtype)

        @pl.when(jnp.logical_not(has_right))
        def _():
            v_ref[:, pl.ds(2 * width, width)] = jnp.zeros((v_ref.shape[0], width), v_ref.dtype)

        own.wait()

        @pl.when(has_right)
        def _():
            to_right().wait_send()
            from_right().wait_recv()

        @pl.when(has_left)
        def _():
            to_left().wait_send()
            from_left().wait_recv()

    blocks = v_ref.shape[1] // BLK - 2 * REACH

    @pl.when(a == min(blocks // 4, blocks - 1))
    def _():
        start_second()

    start = pl.multiple_of(a * BLK, BLK)
    v_cat = v_ref[:, pl.ds(start, WIDE * BLK)]
    out_ref[...] = lax.dot_general(
        v_cat, k_ref[0], (((1,), (1,)), ((), ())), preferred_element_type=jnp.float32
    )

    @pl.when(a == last)
    def _():
        sum_ref[...] = finish()


def apply_sum(local_vec, kmat, tile):
    rows, width = local_vec.shape
    wide_cols = width + 2 * REACH * BLK
    blocks = kmat.shape[0]
    count = lax.axis_size("pts")
    inner = 8 if count % 8 == 0 else count
    outer = count // inner
    return pl.pallas_call(
        functools.partial(apply_sum_kernel, inner, outer),
        out_shape=(
            jax.ShapeDtypeStruct((rows, blocks * BLK), jnp.float32),
            jax.ShapeDtypeStruct(tile.shape, jnp.float32),
        ),
        grid=(blocks,),
        in_specs=[
            pl.BlockSpec((rows, width), lambda a: (0, 0)),
            pl.BlockSpec((1, BLK, WIDE * BLK), lambda a: (a, 0, 0)),
            pl.BlockSpec(tile.shape, lambda a: (0, 0)),
        ],
        out_specs=(
            pl.BlockSpec((rows, BLK), lambda a: (0, a)),
            pl.BlockSpec(tile.shape, lambda a: (0, 0)),
        ),
        scratch_shapes=[
            pltpu.VMEM((rows, wide_cols), local_vec.dtype),
            pltpu.SemaphoreType.DMA((2,)),
            pltpu.SemaphoreType.DMA((2,)),
            pltpu.SemaphoreType.DMA((1,)),
            pltpu.VMEM((inner,) + tile.shape, jnp.float32),
            pltpu.VMEM((outer, inner) + tile.shape, jnp.float32),
            pltpu.SemaphoreType.DMA((2,)),
            pltpu.SemaphoreType.DMA((inner,)),
            pltpu.SemaphoreType.DMA((inner,)),
            pltpu.SemaphoreType.DMA((outer,)),
            pltpu.SemaphoreType.DMA((outer,)),
        ],
        compiler_params=pltpu.CompilerParams(
            dimension_semantics=("arbitrary",), collective_id=0, has_side_effects=True
        ),
    )(local_vec, kmat, tile)


def per_device(points, noise_var, right_side, pattern):
    local_rows = points.shape[0]
    block_count = local_rows // BLK
    rim_rows = REACH * BLK
    kernel_scale = 1.0 / (4 * BLK)
    first_low = right_side.astype(jnp.bfloat16)
    points_t = points.T
    packed = jnp.concatenate([points_t, first_low], axis=0)
    count = lax.axis_size("pts")
    from_left = lax.ppermute(packed, "pts", [(i, i + 1) for i in range(count - 1)])
    from_right = lax.ppermute(packed, "pts", [(i + 1, i) for i in range(count - 1)])
    wide_points_t = jnp.concatenate([from_left[:F], points_t, from_right[:F]], axis=1)
    first_wide = jnp.concatenate([from_left[F:], first_low, from_right[F:]], axis=1)
    kmat = build_k(pattern, points, wide_points_t, block_count)

    rhs_count = lax.axis_size("rhs")
    rhs_index = lax.axis_index("rhs")

    def apply_operator(vector):
        vec_low = vector.astype(jnp.bfloat16)
        wide_vec = with_halo(vec_low, "pts", 1, rim_rows)
        image_part = apply_k(wide_vec, kmat)
        return noise_var[None, :] * vector + kernel_scale * image_part

    def apply_and_total(vector, parts):
        tile = jnp.zeros((8, 128), jnp.float32)
        tile = lax.dynamic_update_slice(tile, parts, (0, 0))
        vec_low = vector.astype(jnp.bfloat16)
        image_part, summed = apply_sum(vec_low, kmat, tile)
        image = noise_var[None, :] * vector + kernel_scale * image_part
        return image, summed[: parts.shape[0], : parts.shape[1]]

    solution = jnp.zeros_like(right_side)
    residual = right_side
    res_image = noise_var[None, :] * residual + kernel_scale * apply_k(first_wide, kmat)
    direction = jnp.zeros_like(right_side)
    dir_image = jnp.zeros_like(right_side)
    dir_twice = jnp.zeros_like(right_side)
    norm_prev = None
    step_prev = None
    for iteration in range(ITERS):
        square_image, sums = apply_and_total(
            res_image,
            jnp.stack([jnp.sum(residual * residual, axis=1), jnp.sum(res_image * residual, axis=1)]),
        )
        norm_now = sums[0][:, None]
        curvature = sums[1][:, None]
        if iteration == 0:
            step_len = norm_now / curvature
            direction = residual
            dir_image = res_image
            dir_twice = square_image
        else:
            mix_ratio = norm_now / norm_prev
            step_len = norm_now / (curvature - mix_ratio * norm_now / step_prev)
            direction = residual + mix_ratio * direction
            dir_image = res_image + mix_ratio * dir_image
            dir_twice = square_image + mix_ratio * dir_twice
        solution = solution + step_len * direction
        residual = residual - step_len * dir_image
        res_image = res_image - step_len * dir_twice
        norm_prev = norm_now
        step_prev = step_len
    return (solution, residual, res_image)


def solution(mesh):
    placed = (P("pts", None), P("pts"), P("rhs", "pts"), P("pts", None))
    return jax.shard_map(
        per_device,
        mesh=mesh,
        in_specs=placed,
        out_specs=(P("rhs", "pts"), P("rhs", "pts"), P("rhs", "pts")),
        check_vma=False,
    )
```

```python
import functools

import jax
import jax.numpy as jnp
from jax import lax
from jax.experimental import pallas as pl
from jax.experimental.pallas import tpu as pltpu
from jax.sharding import PartitionSpec as P

F = 32
BLK = 128
REACH = 16
ITERS = 2
WIDE = 33
WEXP = 18
MESH = pl.DeviceIdType.MESH


def with_halo(cells, axis, dim, width):
    count = lax.axis_size(axis)
    ends = count - 1
    head = lax.slice_in_dim(cells, 0, width, axis=dim)
    tail = lax.slice_in_dim(cells, cells.shape[dim] - width, cells.shape[dim], axis=dim)
    return jnp.concatenate(
        [
            lax.ppermute(tail, axis, [(i, (i + 1) % count) for i in range(ends)]),
            cells,
            lax.ppermute(head, axis, [((i + 1) % count, i) for i in range(ends)]),
        ],
        axis=dim,
    )


def profile_tile(sq_left, sq_right, cross):
    dist = jnp.maximum((sq_left + sq_right) + cross, 0.0)
    radius = jnp.sqrt(dist)
    base = jnp.maximum(1.0 - radius, 0.0)
    b2 = base * base
    b4 = b2 * b2
    b8 = b4 * b4
    b16 = b8 * b8
    return (b16 * b2) * (WEXP * radius + 1.0)


def build_kernel(pat_ref, pw_ref, pwt_ref, k_ref, mirror, cross_ref, sqr_ref):
    a = pl.program_id(0)
    blocks = pl.num_programs(0)
    start = pl.multiple_of(a * BLK, BLK)
    left = pw_ref[pl.ds(start, BLK), :]
    left_f = left.astype(jnp.float32)
    sq_left = jnp.sum(left_f * left_f, axis=1, keepdims=True)
    left_m2 = left * jnp.asarray(-2.0, jnp.bfloat16)
    window = pwt_ref[:, pl.ds(pl.multiple_of(a * BLK, BLK), WIDE * BLK)]
    cross_ref[...] = jnp.dot(left_m2, window, preferred_element_type=jnp.float32)
    window_f = window.astype(jnp.float32)
    sqr_ref[...] = jnp.sum(window_f * window_f, axis=0, keepdims=True)

    def body(o, carry):
        col = pl.multiple_of((a + o) * BLK, BLK)
        dst = pl.ds(pl.multiple_of(o * BLK, BLK), BLK)
        live = pat_ref[a, o] != 0
        other = a + o - REACH
        lower = jnp.logical_and(other >= 0, other < a)
        upper = jnp.logical_and(other > a, other < blocks)

        @pl.when(jnp.logical_and(live, lower))
        def _():
            k_ref[0, :, dst] = mirror[a, other]

        @pl.when(jnp.logical_and(live, jnp.logical_not(lower)))
        def _():
            sq_right = sqr_ref[:, dst]
            value = profile_tile(sq_left, sq_right, cross_ref[:, dst])
            k_ref[0, :, dst] = value.astype(jnp.bfloat16)

            @pl.when(upper)
            def _():
                mirror[other, a] = value.T.astype(jnp.bfloat16)

        @pl.when(jnp.logical_not(live))
        def _():
            k_ref[0, :, dst] = jnp.zeros((BLK, BLK), jnp.bfloat16)

        return carry

    lax.fori_loop(0, WIDE, body, 0)


def apply_kernel(v_ref, k_ref, out_ref):
    a = pl.program_id(0)
    start = pl.multiple_of(a * BLK, BLK)
    v_cat = v_ref[:, pl.ds(start, WIDE * BLK)]
    out_ref[...] = lax.dot_general(
        v_cat, k_ref[0], (((1,), (1,)), ((), ())), preferred_element_type=jnp.float32
    )


def build_k(pattern, points, wide_points_t, blocks):
    rows = points.shape[0]
    wide_cols = wide_points_t.shape[1]
    return pl.pallas_call(
        build_kernel,
        out_shape=jax.ShapeDtypeStruct((blocks, BLK, WIDE * BLK), jnp.bfloat16),
        grid_spec=pltpu.PrefetchScalarGridSpec(
            num_scalar_prefetch=1,
            grid=(blocks,),
            in_specs=[
                pl.BlockSpec((rows, F), lambda a, p: (0, 0)),
                pl.BlockSpec((F, wide_cols), lambda a, p: (0, 0)),
            ],
            out_specs=pl.BlockSpec((1, BLK, WIDE * BLK), lambda a, p: (a, 0, 0)),
            scratch_shapes=[
                pltpu.VMEM((blocks, blocks, BLK, BLK), jnp.bfloat16),
                pltpu.VMEM((BLK, WIDE * BLK), jnp.float32),
                pltpu.VMEM((1, WIDE * BLK), jnp.float32),
            ],
        ),
        compiler_params=pltpu.CompilerParams(dimension_semantics=("arbitrary",)),
    )(pattern, points, wide_points_t)


def apply_k(wide_vec, kmat):
    rows, wide_cols = wide_vec.shape
    blocks = kmat.shape[0]
    return pl.pallas_call(
        apply_kernel,
        out_shape=jax.ShapeDtypeStruct((rows, blocks * BLK), jnp.float32),
        grid=(blocks,),
        in_specs=[
            pl.BlockSpec((rows, wide_cols), lambda a: (0, 0)),
            pl.BlockSpec((1, BLK, WIDE * BLK), lambda a: (a, 0, 0)),
        ],
        out_specs=pl.BlockSpec((rows, BLK), lambda a: (0, a)),
        compiler_params=pltpu.CompilerParams(dimension_semantics=("arbitrary",)),
    )(wide_vec, kmat)


def reduction_steps(inner, outer, part_ref, stage1, stage2, local_sem, send1, recv1, send2, recv2):
    me = lax.axis_index("pts")
    row = lax.axis_index("rhs")
    zc = me // inner
    rc = me % inner

    def greet():
        barrier = pltpu.get_barrier_semaphore()

        def greet_inner(k, carry):
            peer = zc * inner + lax.rem(rc + k, inner)
            pl.semaphore_signal(barrier, inc=1, device_id=(peer, row), device_id_type=MESH)
            return carry

        def greet_outer(k, carry):
            peer = lax.rem(zc + k, outer) * inner + rc
            pl.semaphore_signal(barrier, inc=1, device_id=(peer, row), device_id_type=MESH)
            return carry

        lax.fori_loop(1, inner, greet_inner, 0)
        lax.fori_loop(1, outer, greet_outer, 0)

    def first(slot, other):
        return pltpu.make_async_remote_copy(
            src_ref=part_ref,
            dst_ref=stage1.at[pl.ds(slot, 1)],
            send_sem=send1.at[other],
            recv_sem=recv1.at[slot],
            device_id=(zc * inner + other, row),
            device_id_type=MESH,
        )

    def second(slot, other):
        return pltpu.make_async_remote_copy(
            src_ref=stage1,
            dst_ref=stage2.at[slot],
            send_sem=send2.at[other],
            recv_sem=recv2.at[slot],
            device_id=(other * inner + rc, row),
            device_id_type=MESH,
        )

    own1 = pltpu.make_async_copy(part_ref, stage1.at[pl.ds(rc, 1)], local_sem.at[0])
    own2 = pltpu.make_async_copy(stage1, stage2.at[zc], local_sem.at[1])

    def start_first():
        own1.start()

        def send_first(k, carry):
            first(rc, lax.rem(rc + k, inner)).start()
            return carry

        lax.fori_loop(1, inner, send_first, 0)

    def start_second():
        def finish_first(k, carry):
            other = lax.rem(rc + k, inner)
            first(rc, other).wait_send()
            first(other, other).wait_recv()
            return carry

        lax.fori_loop(1, inner, finish_first, 0)
        own1.wait()
        own2.start()

        def send_second(k, carry):
            second(zc, lax.rem(zc + k, outer)).start()
            return carry

        lax.fori_loop(1, outer, send_second, 0)

    def finish():
        def finish_second(k, carry):
            other = lax.rem(zc + k, outer)
            second(zc, other).wait_send()
            second(other, other).wait_recv()
            return carry

        lax.fori_loop(1, outer, finish_second, 0)
        own2.wait()
        return jnp.sum(jnp.sum(stage2[...], axis=0), axis=0, keepdims=True)

    return greet, start_first, start_second, finish


def apply_sum_kernel(inner, outer, vloc_ref, k_ref, part_ref, out_ref, sum_ref, v_ref, halo_send, halo_recv, halo_local, *scratch):
    a = pl.program_id(0)
    last = pl.num_programs(0) - 1
    greet, start_first, start_second, finish = reduction_steps(inner, outer, part_ref, *scratch)
    me = lax.axis_index("pts")
    row = lax.axis_index("rhs")
    count = inner * outer
    rc = me % inner
    width = vloc_ref.shape[1]
    has_left = me > 0
    has_right = me < count - 1
    extra = jnp.logical_or(
        jnp.logical_and(rc == 0, has_left), jnp.logical_and(rc == inner - 1, has_right)
    )

    def to_right():
        return pltpu.make_async_remote_copy(
            src_ref=vloc_ref,
            dst_ref=v_ref.at[:, pl.ds(0, width)],
            send_sem=halo_send.at[0],
            recv_sem=halo_recv.at[0],
            device_id=(me + 1, row),
            device_id_type=MESH,
        )

    def to_left():
        return pltpu.make_async_remote_copy(
            src_ref=vloc_ref,
            dst_ref=v_ref.at[:, pl.ds(2 * width, width)],
            send_sem=halo_send.at[1],
            recv_sem=halo_recv.at[1],
            device_id=(me - 1, row),
            device_id_type=MESH,
        )

    def from_left():
        return pltpu.make_async_remote_copy(
            src_ref=vloc_ref,
            dst_ref=v_ref.at[:, pl.ds(0, width)],
            send_sem=halo_send.at[0],
            recv_sem=halo_recv.at[0],
            device_id=(me - 1, row),
            device_id_type=MESH,
        )

    def from_right():
        return pltpu.make_async_remote_copy(
            src_ref=vloc_ref,
            dst_ref=v_ref.at[:, pl.ds(2 * width, width)],
            send_sem=halo_send.at[1],
            recv_sem=halo_recv.at[1],
            device_id=(me + 1, row),
            device_id_type=MESH,
        )

    own = pltpu.make_async_copy(vloc_ref, v_ref.at[:, pl.ds(width, width)], halo_local.at[0])

    @pl.when(a == 0)
    def _():
        greet()
        barrier = pltpu.get_barrier_semaphore()

        @pl.when(jnp.logical_and(extra, rc == 0))
        def _():
            pl.semaphore_signal(barrier, inc=1, device_id=(me - 1, row), device_id_type=MESH)

        @pl.when(jnp.logical_and(extra, rc == inner - 1))
        def _():
            pl.semaphore_signal(barrier, inc=1, device_id=(me + 1, row), device_id_type=MESH)

        peers = (inner - 1) + (outer - 1)

        @pl.when(extra)
        def _():
            pl.semaphore_wait(barrier, peers + 1)

        @pl.when(jnp.logical_not(extra))
        def _():
            pl.semaphore_wait(barrier, peers)

        start_first()
        own.start()

        @pl.when(has_right)
        def _():
            to_right().start()

        @pl.when(has_left)
        def _():
            to_left().start()

        @pl.when(jnp.logical_not(has_left))
        def _():
            v_ref[:, pl.ds(0, width)] = jnp.zeros((v_ref.shape[0], width), v_ref.dtype)

        @pl.when(jnp.logical_not(has_right))
        def _():
            v_ref[:, pl.ds(2 * width, width)] = jnp.zeros((v_ref.shape[0], width), v_ref.dtype)

        own.wait()

        @pl.when(has_right)
        def _():
            to_right().wait_send()
            from_right().wait_recv()

        @pl.when(has_left)
        def _():
            to_left().wait_send()
            from_left().wait_recv()

    blocks = v_ref.shape[1] // BLK - 2 * REACH

    @pl.when(a == min(blocks // 2 - 2, blocks - 1))
    def _():
        start_second()

    start = pl.multiple_of(a * BLK, BLK)
    v_cat = v_ref[:, pl.ds(start, WIDE * BLK)]
    out_ref[...] = lax.dot_general(
        v_cat, k_ref[0], (((1,), (1,)), ((), ())), preferred_element_type=jnp.float32
    )

    @pl.when(a == last)
    def _():
        sum_ref[...] = finish()


def apply_sum(local_vec, kmat, tile):
    rows, width = local_vec.shape
    wide_cols = width + 2 * REACH * BLK
    blocks = kmat.shape[0]
    count = lax.axis_size("pts")
    inner = 8 if count % 8 == 0 else count
    outer = count // inner
    return pl.pallas_call(
        functools.partial(apply_sum_kernel, inner, outer),
        out_shape=(
            jax.ShapeDtypeStruct((rows, blocks * BLK), jnp.float32),
            jax.ShapeDtypeStruct(tile.shape, jnp.float32),
        ),
        grid=(blocks,),
        in_specs=[
            pl.BlockSpec((rows, width), lambda a: (0, 0)),
            pl.BlockSpec((1, BLK, WIDE * BLK), lambda a: (a, 0, 0)),
            pl.BlockSpec(tile.shape, lambda a: (0, 0)),
        ],
        out_specs=(
            pl.BlockSpec((rows, BLK), lambda a: (0, a)),
            pl.BlockSpec(tile.shape, lambda a: (0, 0)),
        ),
        scratch_shapes=[
            pltpu.VMEM((rows, wide_cols), local_vec.dtype),
            pltpu.SemaphoreType.DMA((2,)),
            pltpu.SemaphoreType.DMA((2,)),
            pltpu.SemaphoreType.DMA((1,)),
            pltpu.VMEM((inner, tile.shape[1]), jnp.float32),
            pltpu.VMEM((outer, inner, tile.shape[1]), jnp.float32),
            pltpu.SemaphoreType.DMA((2,)),
            pltpu.SemaphoreType.DMA((inner,)),
            pltpu.SemaphoreType.DMA((inner,)),
            pltpu.SemaphoreType.DMA((outer,)),
            pltpu.SemaphoreType.DMA((outer,)),
        ],
        compiler_params=pltpu.CompilerParams(
            dimension_semantics=("arbitrary",), collective_id=0, has_side_effects=True
        ),
    )(local_vec, kmat, tile)


def per_device(points, noise_var, right_side, pattern):
    local_rows = points.shape[0]
    block_count = local_rows // BLK
    rim_rows = REACH * BLK
    kernel_scale = 1.0 / (4 * BLK)
    first_low = right_side.astype(jnp.bfloat16)
    points_t = points.T
    packed = jnp.concatenate([points_t, first_low], axis=0)
    count = lax.axis_size("pts")
    from_left = lax.ppermute(packed, "pts", [(i, i + 1) for i in range(count - 1)])
    from_right = lax.ppermute(packed, "pts", [(i + 1, i) for i in range(count - 1)])
    wide_points_t = jnp.concatenate([from_left[:F], points_t, from_right[:F]], axis=1)
    first_wide = jnp.concatenate([from_left[F:], first_low, from_right[F:]], axis=1)
    kmat = build_k(pattern, points, wide_points_t, block_count)

    rhs_count = lax.axis_size("rhs")
    rhs_index = lax.axis_index("rhs")

    def apply_operator(vector):
        vec_low = vector.astype(jnp.bfloat16)
        wide_vec = with_halo(vec_low, "pts", 1, rim_rows)
        image_part = apply_k(wide_vec, kmat)
        return noise_var[None, :] * vector + kernel_scale * image_part

    def apply_and_total(vector, parts):
        flat = parts.reshape(1, -1)
        tile = jnp.zeros((1, 128), jnp.float32)
        tile = lax.dynamic_update_slice(tile, flat, (0, 0))
        vec_low = vector.astype(jnp.bfloat16)
        image_part, summed = apply_sum(vec_low, kmat, tile)
        image = noise_var[None, :] * vector + kernel_scale * image_part
        return image, summed[0, : flat.shape[1]].reshape(parts.shape)

    solution = jnp.zeros_like(right_side)
    residual = right_side
    res_image = noise_var[None, :] * residual + kernel_scale * apply_k(first_wide, kmat)
    direction = jnp.zeros_like(right_side)
    dir_image = jnp.zeros_like(right_side)
    dir_twice = jnp.zeros_like(right_side)
    norm_prev = None
    step_prev = None
    for iteration in range(ITERS):
        square_image, sums = apply_and_total(
            res_image,
            jnp.stack([jnp.sum(residual * residual, axis=1), jnp.sum(res_image * residual, axis=1)]),
        )
        norm_now = sums[0][:, None]
        curvature = sums[1][:, None]
        if iteration == 0:
            step_len = norm_now / curvature
            direction = residual
            dir_image = res_image
            dir_twice = square_image
        else:
            mix_ratio = norm_now / norm_prev
            step_len = norm_now / (curvature - mix_ratio * norm_now / step_prev)
            direction = residual + mix_ratio * direction
            dir_image = res_image + mix_ratio * dir_image
            dir_twice = square_image + mix_ratio * dir_twice
        solution = solution + step_len * direction
        residual = residual - step_len * dir_image
        res_image = res_image - step_len * dir_twice
        norm_prev = norm_now
        step_prev = step_len
    return (solution, residual, res_image)


def solution(mesh):
    placed = (P("pts", None), P("pts"), P("rhs", "pts"), P("pts", None))
    return jax.shard_map(
        per_device,
        mesh=mesh,
        in_specs=placed,
        out_specs=(P("rhs", "pts"), P("rhs", "pts"), P("rhs", "pts")),
        check_vma=False,
    )
```

```python
import functools

import jax
import jax.numpy as jnp
from jax import lax
from jax.experimental import pallas as pl
from jax.experimental.pallas import tpu as pltpu
from jax.sharding import PartitionSpec as P

F = 32
BLK = 128
REACH = 16
ITERS = 2
WIDE = 33
WEXP = 18
MESH = pl.DeviceIdType.MESH


def with_halo(cells, axis, dim, width):
    count = lax.axis_size(axis)
    ends = count - 1
    head = lax.slice_in_dim(cells, 0, width, axis=dim)
    tail = lax.slice_in_dim(cells, cells.shape[dim] - width, cells.shape[dim], axis=dim)
    return jnp.concatenate(
        [
            lax.ppermute(tail, axis, [(i, (i + 1) % count) for i in range(ends)]),
            cells,
            lax.ppermute(head, axis, [((i + 1) % count, i) for i in range(ends)]),
        ],
        axis=dim,
    )


def profile_tile(sq_left, sq_right, cross):
    dist = jnp.maximum((sq_left + sq_right) + cross, 0.0)
    radius = jnp.sqrt(dist)
    base = jnp.maximum(1.0 - radius, 0.0)
    b2 = base * base
    b4 = b2 * b2
    b8 = b4 * b4
    b16 = b8 * b8
    return (b16 * b2) * (WEXP * radius + 1.0)


def build_kernel(pat_ref, pw_ref, pwt_ref, k_ref, mirror, cross_ref, sqr_ref):
    a = pl.program_id(0)
    blocks = pl.num_programs(0)
    start = pl.multiple_of(a * BLK, BLK)
    left = pw_ref[pl.ds(start, BLK), :]
    left_f = left.astype(jnp.float32)
    sq_left = jnp.sum(left_f * left_f, axis=1, keepdims=True)
    left_m2 = left * jnp.asarray(-2.0, jnp.bfloat16)
    window = pwt_ref[:, pl.ds(pl.multiple_of(a * BLK, BLK), WIDE * BLK)]
    cross_ref[...] = jnp.dot(left_m2, window, preferred_element_type=jnp.float32)
    window_f = window.astype(jnp.float32)
    sqr_ref[...] = jnp.sum(window_f * window_f, axis=0, keepdims=True)

    def body(o, carry):
        col = pl.multiple_of((a + o) * BLK, BLK)
        dst = pl.ds(pl.multiple_of(o * BLK, BLK), BLK)
        live = pat_ref[a, o] != 0
        other = a + o - REACH
        lower = jnp.logical_and(other >= 0, other < a)
        upper = jnp.logical_and(other > a, other < blocks)

        @pl.when(jnp.logical_and(live, lower))
        def _():
            k_ref[0, :, dst] = mirror[a, other]

        @pl.when(jnp.logical_and(live, jnp.logical_not(lower)))
        def _():
            sq_right = sqr_ref[:, dst]
            value = profile_tile(sq_left, sq_right, cross_ref[:, dst]).astype(jnp.bfloat16)
            k_ref[0, :, dst] = value

            @pl.when(upper)
            def _():
                mirror[other, a] = value.T

        @pl.when(jnp.logical_not(live))
        def _():
            k_ref[0, :, dst] = jnp.zeros((BLK, BLK), jnp.bfloat16)

        return carry

    lax.fori_loop(0, WIDE, body, 0)


def apply_kernel(v_ref, k_ref, out_ref):
    a = pl.program_id(0)
    start = pl.multiple_of(a * BLK, BLK)
    v_cat = v_ref[:, pl.ds(start, WIDE * BLK)]
    out_ref[...] = lax.dot_general(
        v_cat, k_ref[0], (((1,), (1,)), ((), ())), preferred_element_type=jnp.float32
    )


def build_k(pattern, points, wide_points_t, blocks):
    rows = points.shape[0]
    wide_cols = wide_points_t.shape[1]
    return pl.pallas_call(
        build_kernel,
        out_shape=jax.ShapeDtypeStruct((blocks, BLK, WIDE * BLK), jnp.bfloat16),
        grid_spec=pltpu.PrefetchScalarGridSpec(
            num_scalar_prefetch=1,
            grid=(blocks,),
            in_specs=[
                pl.BlockSpec((rows, F), lambda a, p: (0, 0)),
                pl.BlockSpec((F, wide_cols), lambda a, p: (0, 0)),
            ],
            out_specs=pl.BlockSpec((1, BLK, WIDE * BLK), lambda a, p: (a, 0, 0)),
            scratch_shapes=[
                pltpu.VMEM((blocks, blocks, BLK, BLK), jnp.bfloat16),
                pltpu.VMEM((BLK, WIDE * BLK), jnp.float32),
                pltpu.VMEM((1, WIDE * BLK), jnp.float32),
            ],
        ),
        compiler_params=pltpu.CompilerParams(dimension_semantics=("arbitrary",)),
    )(pattern, points, wide_points_t)


def apply_k(wide_vec, kmat):
    rows, wide_cols = wide_vec.shape
    blocks = kmat.shape[0]
    return pl.pallas_call(
        apply_kernel,
        out_shape=jax.ShapeDtypeStruct((rows, blocks * BLK), jnp.float32),
        grid=(blocks,),
        in_specs=[
            pl.BlockSpec((rows, wide_cols), lambda a: (0, 0)),
            pl.BlockSpec((1, BLK, WIDE * BLK), lambda a: (a, 0, 0)),
        ],
        out_specs=pl.BlockSpec((rows, BLK), lambda a: (0, a)),
        compiler_params=pltpu.CompilerParams(dimension_semantics=("arbitrary",)),
    )(wide_vec, kmat)


def reduction_steps(inner, outer, part_ref, stage1, stage2, local_sem, send1, recv1, send2, recv2):
    me = lax.axis_index("pts")
    row = lax.axis_index("rhs")
    zc = me // inner
    rc = me % inner

    def greet():
        barrier = pltpu.get_barrier_semaphore()

        def greet_inner(k, carry):
            peer = zc * inner + lax.rem(rc + k, inner)
            pl.semaphore_signal(barrier, inc=1, device_id=(peer, row), device_id_type=MESH)
            return carry

        def greet_outer(k, carry):
            peer = lax.rem(zc + k, outer) * inner + rc
            pl.semaphore_signal(barrier, inc=1, device_id=(peer, row), device_id_type=MESH)
            return carry

        lax.fori_loop(1, inner, greet_inner, 0)
        lax.fori_loop(1, outer, greet_outer, 0)

    def first(slot, other):
        return pltpu.make_async_remote_copy(
            src_ref=part_ref,
            dst_ref=stage1.at[slot],
            send_sem=send1.at[other],
            recv_sem=recv1.at[slot],
            device_id=(zc * inner + other, row),
            device_id_type=MESH,
        )

    def second(slot, other):
        return pltpu.make_async_remote_copy(
            src_ref=stage1,
            dst_ref=stage2.at[slot],
            send_sem=send2.at[other],
            recv_sem=recv2.at[slot],
            device_id=(other * inner + rc, row),
            device_id_type=MESH,
        )

    own1 = pltpu.make_async_copy(part_ref, stage1.at[rc], local_sem.at[0])
    own2 = pltpu.make_async_copy(stage1, stage2.at[zc], local_sem.at[1])

    def start_first():
        own1.start()

        def send_first(k, carry):
            first(rc, lax.rem(rc + k, inner)).start()
            return carry

        lax.fori_loop(1, inner, send_first, 0)

    def start_second():
        def finish_first(k, carry):
            other = lax.rem(rc + k, inner)
            first(rc, other).wait_send()
            first(other, other).wait_recv()
            return carry

        lax.fori_loop(1, inner, finish_first, 0)
        own1.wait()
        own2.start()

        def send_second(k, carry):
            second(zc, lax.rem(zc + k, outer)).start()
            return carry

        lax.fori_loop(1, outer, send_second, 0)

    def finish():
        def finish_second(k, carry):
            other = lax.rem(zc + k, outer)
            second(zc, other).wait_send()
            second(other, other).wait_recv()
            return carry

        lax.fori_loop(1, outer, finish_second, 0)
        own2.wait()
        return jnp.sum(jnp.sum(stage2[...], axis=0), axis=0)

    return greet, start_first, start_second, finish


def apply_sum_kernel(inner, outer, vloc_ref, k_ref, part_ref, out_ref, sum_ref, v_ref, halo_send, halo_recv, halo_local, *scratch):
    a = pl.program_id(0)
    last = pl.num_programs(0) - 1
    greet, start_first, start_second, finish = reduction_steps(inner, outer, part_ref, *scratch)
    me = lax.axis_index("pts")
    row = lax.axis_index("rhs")
    count = inner * outer
    rc = me % inner
    width = vloc_ref.shape[1]
    has_left = me > 0
    has_right = me < count - 1
    extra = jnp.logical_or(
        jnp.logical_and(rc == 0, has_left), jnp.logical_and(rc == inner - 1, has_right)
    )

    def to_right():
        return pltpu.make_async_remote_copy(
            src_ref=vloc_ref,
            dst_ref=v_ref.at[:, pl.ds(0, width)],
            send_sem=halo_send.at[0],
            recv_sem=halo_recv.at[0],
            device_id=(me + 1, row),
            device_id_type=MESH,
        )

    def to_left():
        return pltpu.make_async_remote_copy(
            src_ref=vloc_ref,
            dst_ref=v_ref.at[:, pl.ds(2 * width, width)],
            send_sem=halo_send.at[1],
            recv_sem=halo_recv.at[1],
            device_id=(me - 1, row),
            device_id_type=MESH,
        )

    def from_left():
        return pltpu.make_async_remote_copy(
            src_ref=vloc_ref,
            dst_ref=v_ref.at[:, pl.ds(0, width)],
            send_sem=halo_send.at[0],
            recv_sem=halo_recv.at[0],
            device_id=(me - 1, row),
            device_id_type=MESH,
        )

    def from_right():
        return pltpu.make_async_remote_copy(
            src_ref=vloc_ref,
            dst_ref=v_ref.at[:, pl.ds(2 * width, width)],
            send_sem=halo_send.at[1],
            recv_sem=halo_recv.at[1],
            device_id=(me + 1, row),
            device_id_type=MESH,
        )

    own = pltpu.make_async_copy(vloc_ref, v_ref.at[:, pl.ds(width, width)], halo_local.at[0])

    @pl.when(a == 0)
    def _():
        greet()
        barrier = pltpu.get_barrier_semaphore()

        @pl.when(jnp.logical_and(extra, rc == 0))
        def _():
            pl.semaphore_signal(barrier, inc=1, device_id=(me - 1, row), device_id_type=MESH)

        @pl.when(jnp.logical_and(extra, rc == inner - 1))
        def _():
            pl.semaphore_signal(barrier, inc=1, device_id=(me + 1, row), device_id_type=MESH)

        peers = (inner - 1) + (outer - 1)

        @pl.when(extra)
        def _():
            pl.semaphore_wait(barrier, peers + 1)

        @pl.when(jnp.logical_not(extra))
        def _():
            pl.semaphore_wait(barrier, peers)

        start_first()
        own.start()

        @pl.when(has_right)
        def _():
            to_right().start()

        @pl.when(has_left)
        def _():
            to_left().start()

        @pl.when(jnp.logical_not(has_left))
        def _():
            v_ref[:, pl.ds(0, width)] = jnp.zeros((v_ref.shape[0], width), v_ref.dtype)

        @pl.when(jnp.logical_not(has_right))
        def _():
            v_ref[:, pl.ds(2 * width, width)] = jnp.zeros((v_ref.shape[0], width), v_ref.dtype)

        own.wait()

        @pl.when(has_right)
        def _():
            to_right().wait_send()
            from_right().wait_recv()

        @pl.when(has_left)
        def _():
            to_left().wait_send()
            from_left().wait_recv()

    blocks = v_ref.shape[1] // BLK - 2 * REACH

    @pl.when(a == min(blocks // 2 - 2, blocks - 1))
    def _():
        start_second()

    start = pl.multiple_of(a * BLK, BLK)
    v_cat = v_ref[:, pl.ds(start, WIDE * BLK)]
    out_ref[...] = lax.dot_general(
        v_cat, k_ref[0], (((1,), (1,)), ((), ())), preferred_element_type=jnp.float32
    )

    @pl.when(a == last)
    def _():
        sum_ref[...] = finish()


def apply_sum(local_vec, kmat, tile):
    rows, width = local_vec.shape
    wide_cols = width + 2 * REACH * BLK
    blocks = kmat.shape[0]
    count = lax.axis_size("pts")
    inner = 8 if count % 8 == 0 else count
    outer = count // inner
    return pl.pallas_call(
        functools.partial(apply_sum_kernel, inner, outer),
        out_shape=(
            jax.ShapeDtypeStruct((rows, blocks * BLK), jnp.float32),
            jax.ShapeDtypeStruct(tile.shape, jnp.float32),
        ),
        grid=(blocks,),
        in_specs=[
            pl.BlockSpec((rows, width), lambda a: (0, 0)),
            pl.BlockSpec((1, BLK, WIDE * BLK), lambda a: (a, 0, 0)),
            pl.BlockSpec(tile.shape, lambda a: (0, 0)),
        ],
        out_specs=(
            pl.BlockSpec((rows, BLK), lambda a: (0, a)),
            pl.BlockSpec(tile.shape, lambda a: (0, 0)),
        ),
        scratch_shapes=[
            pltpu.VMEM((rows, wide_cols), local_vec.dtype),
            pltpu.SemaphoreType.DMA((2,)),
            pltpu.SemaphoreType.DMA((2,)),
            pltpu.SemaphoreType.DMA((1,)),
            pltpu.VMEM((inner,) + tile.shape, jnp.float32),
            pltpu.VMEM((outer, inner) + tile.shape, jnp.float32),
            pltpu.SemaphoreType.DMA((2,)),
            pltpu.SemaphoreType.DMA((inner,)),
            pltpu.SemaphoreType.DMA((inner,)),
            pltpu.SemaphoreType.DMA((outer,)),
            pltpu.SemaphoreType.DMA((outer,)),
        ],
        compiler_params=pltpu.CompilerParams(
            dimension_semantics=("arbitrary",), collective_id=0, has_side_effects=True
        ),
    )(local_vec, kmat, tile)


def per_device(points, noise_var, right_side, pattern):
    local_rows = points.shape[0]
    block_count = local_rows // BLK
    rim_rows = REACH * BLK
    kernel_scale = 1.0 / (4 * BLK)
    first_low = right_side.astype(jnp.bfloat16)
    points_t = points.T
    packed = jnp.concatenate([points_t, first_low], axis=0)
    count = lax.axis_size("pts")
    from_left = lax.ppermute(packed, "pts", [(i, i + 1) for i in range(count - 1)])
    from_right = lax.ppermute(packed, "pts", [(i + 1, i) for i in range(count - 1)])
    wide_points_t = jnp.concatenate([from_left[:F], points_t, from_right[:F]], axis=1)
    first_wide = jnp.concatenate([from_left[F:], first_low, from_right[F:]], axis=1)
    kmat = build_k(pattern, points, wide_points_t, block_count)

    rhs_count = lax.axis_size("rhs")
    rhs_index = lax.axis_index("rhs")

    def apply_operator(vector):
        vec_low = vector.astype(jnp.bfloat16)
        wide_vec = with_halo(vec_low, "pts", 1, rim_rows)
        image_part = apply_k(wide_vec, kmat)
        return noise_var[None, :] * vector + kernel_scale * image_part

    def apply_and_total(vector, parts):
        tile = jnp.zeros((8, 128), jnp.float32)
        tile = lax.dynamic_update_slice(tile, parts, (0, 0))
        vec_low = vector.astype(jnp.bfloat16)
        image_part, summed = apply_sum(vec_low, kmat, tile)
        image = noise_var[None, :] * vector + kernel_scale * image_part
        return image, summed[: parts.shape[0], : parts.shape[1]]

    solution = jnp.zeros_like(right_side)
    residual = right_side
    res_image = noise_var[None, :] * residual + kernel_scale * apply_k(first_wide, kmat)
    direction = jnp.zeros_like(right_side)
    dir_image = jnp.zeros_like(right_side)
    dir_twice = jnp.zeros_like(right_side)
    norm_prev = None
    step_prev = None
    for iteration in range(ITERS):
        square_image, sums = apply_and_total(
            res_image,
            jnp.stack([jnp.sum(residual * residual, axis=1), jnp.sum(res_image * residual, axis=1)]),
        )
        norm_now = sums[0][:, None]
        curvature = sums[1][:, None]
        if iteration == 0:
            step_len = norm_now / curvature
            direction = residual
            dir_image = res_image
            dir_twice = square_image
        else:
            mix_ratio = norm_now / norm_prev
            step_len = norm_now / (curvature - mix_ratio * norm_now / step_prev)
            direction = residual + mix_ratio * direction
            dir_image = res_image + mix_ratio * dir_image
            dir_twice = square_image + mix_ratio * dir_twice
        solution = solution + step_len * direction
        residual = residual - step_len * dir_image
        res_image = res_image - step_len * dir_twice
        norm_prev = norm_now
        step_prev = step_len
    return (solution, residual, res_image)


def solution(mesh):
    placed = (P("pts", None), P("pts"), P("rhs", "pts"), P("pts", None))
    return jax.shard_map(
        per_device,
        mesh=mesh,
        in_specs=placed,
        out_specs=(P("rhs", "pts"), P("rhs", "pts"), P("rhs", "pts")),
        check_vma=False,
    )
```

```python
import functools

import jax
import jax.numpy as jnp
from jax import lax
from jax.experimental import pallas as pl
from jax.experimental.pallas import tpu as pltpu
from jax.sharding import PartitionSpec as P

F = 32
BLK = 128
REACH = 16
ITERS = 2
WIDE = 33
WEXP = 18
MESH = pl.DeviceIdType.MESH


def with_halo(cells, axis, dim, width):
    count = lax.axis_size(axis)
    ends = count - 1
    head = lax.slice_in_dim(cells, 0, width, axis=dim)
    tail = lax.slice_in_dim(cells, cells.shape[dim] - width, cells.shape[dim], axis=dim)
    return jnp.concatenate(
        [
            lax.ppermute(tail, axis, [(i, (i + 1) % count) for i in range(ends)]),
            cells,
            lax.ppermute(head, axis, [((i + 1) % count, i) for i in range(ends)]),
        ],
        axis=dim,
    )


def profile_tile(sq_left, sq_right, cross):
    dist = jnp.maximum((sq_left + sq_right) + cross, 0.0)
    radius = jnp.sqrt(dist)
    base = jnp.maximum(1.0 - radius, 0.0)
    b2 = base * base
    b4 = b2 * b2
    b8 = b4 * b4
    b16 = b8 * b8
    return (b16 * b2) * (WEXP * radius + 1.0)


def build_kernel(pat_ref, pw_ref, pwt_ref, k_ref, mirror, cross_ref, sqr_ref):
    a = pl.program_id(0)
    blocks = pl.num_programs(0)
    start = pl.multiple_of(a * BLK, BLK)
    left = pw_ref[pl.ds(start, BLK), :]
    left_f = left.astype(jnp.float32)
    sq_left = jnp.sum(left_f * left_f, axis=1, keepdims=True)
    left_m2 = left * jnp.asarray(-2.0, jnp.bfloat16)
    window = pwt_ref[:, pl.ds(pl.multiple_of(a * BLK, BLK), WIDE * BLK)]
    cross_ref[...] = jnp.dot(left_m2, window, preferred_element_type=jnp.float32)
    window_f = window.astype(jnp.float32)
    sqr_ref[...] = jnp.sum(window_f * window_f, axis=0, keepdims=True)

    def body(o, carry):
        col = pl.multiple_of((a + o) * BLK, BLK)
        dst = pl.ds(pl.multiple_of(o * BLK, BLK), BLK)
        live = pat_ref[a, o] != 0
        other = a + o - REACH
        lower = jnp.logical_and(other >= 0, other < a)
        upper = jnp.logical_and(other > a, other < blocks)

        @pl.when(jnp.logical_and(live, lower))
        def _():
            k_ref[0, :, dst] = mirror[a, other]

        @pl.when(jnp.logical_and(live, jnp.logical_not(lower)))
        def _():
            sq_right = sqr_ref[:, dst]
            value = profile_tile(sq_left, sq_right, cross_ref[:, dst])
            k_ref[0, :, dst] = value.astype(jnp.bfloat16)

            @pl.when(upper)
            def _():
                mirror[other, a] = value.T.astype(jnp.bfloat16)

        @pl.when(jnp.logical_not(live))
        def _():
            k_ref[0, :, dst] = jnp.zeros((BLK, BLK), jnp.bfloat16)

        return carry

    lax.fori_loop(0, WIDE, body, 0)


def apply_kernel(v_ref, k_ref, out_ref):
    a = pl.program_id(0)
    start = pl.multiple_of(a * BLK, BLK)
    v_cat = v_ref[:, pl.ds(start, WIDE * BLK)]
    out_ref[...] = lax.dot_general(
        v_cat, k_ref[0], (((1,), (1,)), ((), ())), preferred_element_type=jnp.float32
    )


def build_k(pattern, points, wide_points_t, blocks):
    rows = points.shape[0]
    wide_cols = wide_points_t.shape[1]
    return pl.pallas_call(
        build_kernel,
        out_shape=jax.ShapeDtypeStruct((blocks, BLK, WIDE * BLK), jnp.bfloat16),
        grid_spec=pltpu.PrefetchScalarGridSpec(
            num_scalar_prefetch=1,
            grid=(blocks,),
            in_specs=[
                pl.BlockSpec((rows, F), lambda a, p: (0, 0)),
                pl.BlockSpec((F, wide_cols), lambda a, p: (0, 0)),
            ],
            out_specs=pl.BlockSpec((1, BLK, WIDE * BLK), lambda a, p: (a, 0, 0)),
            scratch_shapes=[
                pltpu.VMEM((blocks, blocks, BLK, BLK), jnp.bfloat16),
                pltpu.VMEM((BLK, WIDE * BLK), jnp.float32),
                pltpu.VMEM((1, WIDE * BLK), jnp.float32),
            ],
        ),
        compiler_params=pltpu.CompilerParams(dimension_semantics=("arbitrary",)),
    )(pattern, points, wide_points_t)


def apply_k(wide_vec, kmat):
    rows, wide_cols = wide_vec.shape
    blocks = kmat.shape[0]
    return pl.pallas_call(
        apply_kernel,
        out_shape=jax.ShapeDtypeStruct((rows, blocks * BLK), jnp.float32),
        grid=(blocks,),
        in_specs=[
            pl.BlockSpec((rows, wide_cols), lambda a: (0, 0)),
            pl.BlockSpec((1, BLK, WIDE * BLK), lambda a: (a, 0, 0)),
        ],
        out_specs=pl.BlockSpec((rows, BLK), lambda a: (0, a)),
        compiler_params=pltpu.CompilerParams(dimension_semantics=("arbitrary",)),
    )(wide_vec, kmat)


def reduction_steps(inner, outer, part_ref, stage1, stage2, local_sem, send1, recv1, send2, recv2):
    me = lax.axis_index("pts")
    row = lax.axis_index("rhs")
    zc = me // inner
    rc = me % inner

    def greet():
        barrier = pltpu.get_barrier_semaphore()

        def greet_inner(k, carry):
            peer = zc * inner + lax.rem(rc + k, inner)
            pl.semaphore_signal(barrier, inc=1, device_id=(peer, row), device_id_type=MESH)
            return carry

        def greet_outer(k, carry):
            peer = lax.rem(zc + k, outer) * inner + rc
            pl.semaphore_signal(barrier, inc=1, device_id=(peer, row), device_id_type=MESH)
            return carry

        [greet_inner(k, 0) for k in range(1, inner)]
        [greet_outer(k, 0) for k in range(1, outer)]

    def first(slot, other):
        return pltpu.make_async_remote_copy(
            src_ref=part_ref,
            dst_ref=stage1.at[slot],
            send_sem=send1.at[other],
            recv_sem=recv1.at[slot],
            device_id=(zc * inner + other, row),
            device_id_type=MESH,
        )

    def second(slot, other):
        return pltpu.make_async_remote_copy(
            src_ref=stage1,
            dst_ref=stage2.at[slot],
            send_sem=send2.at[other],
            recv_sem=recv2.at[slot],
            device_id=(other * inner + rc, row),
            device_id_type=MESH,
        )

    own1 = pltpu.make_async_copy(part_ref, stage1.at[rc], local_sem.at[0])
    own2 = pltpu.make_async_copy(stage1, stage2.at[zc], local_sem.at[1])

    def start_first():
        own1.start()

        def send_first(k, carry):
            first(rc, lax.rem(rc + k, inner)).start()
            return carry

        [send_first(k, 0) for k in range(1, inner)]

    def start_second():
        def finish_first(k, carry):
            other = lax.rem(rc + k, inner)
            first(rc, other).wait_send()
            first(other, other).wait_recv()
            return carry

        [finish_first(k, 0) for k in range(1, inner)]
        own1.wait()
        own2.start()

        def send_second(k, carry):
            second(zc, lax.rem(zc + k, outer)).start()
            return carry

        [send_second(k, 0) for k in range(1, outer)]

    def finish():
        def finish_second(k, carry):
            other = lax.rem(zc + k, outer)
            second(zc, other).wait_send()
            second(other, other).wait_recv()
            return carry

        [finish_second(k, 0) for k in range(1, outer)]
        own2.wait()
        return jnp.sum(jnp.sum(stage2[...], axis=0), axis=0)

    return greet, start_first, start_second, finish


def apply_sum_kernel(inner, outer, vloc_ref, k_ref, part_ref, out_ref, sum_ref, v_ref, halo_send, halo_recv, halo_local, *scratch):
    a = pl.program_id(0)
    last = pl.num_programs(0) - 1
    greet, start_first, start_second, finish = reduction_steps(inner, outer, part_ref, *scratch)
    me = lax.axis_index("pts")
    row = lax.axis_index("rhs")
    count = inner * outer
    rc = me % inner
    width = vloc_ref.shape[1]
    has_left = me > 0
    has_right = me < count - 1
    extra = jnp.logical_or(
        jnp.logical_and(rc == 0, has_left), jnp.logical_and(rc == inner - 1, has_right)
    )

    def to_right():
        return pltpu.make_async_remote_copy(
            src_ref=vloc_ref,
            dst_ref=v_ref.at[:, pl.ds(0, width)],
            send_sem=halo_send.at[0],
            recv_sem=halo_recv.at[0],
            device_id=(me + 1, row),
            device_id_type=MESH,
        )

    def to_left():
        return pltpu.make_async_remote_copy(
            src_ref=vloc_ref,
            dst_ref=v_ref.at[:, pl.ds(2 * width, width)],
            send_sem=halo_send.at[1],
            recv_sem=halo_recv.at[1],
            device_id=(me - 1, row),
            device_id_type=MESH,
        )

    def from_left():
        return pltpu.make_async_remote_copy(
            src_ref=vloc_ref,
            dst_ref=v_ref.at[:, pl.ds(0, width)],
            send_sem=halo_send.at[0],
            recv_sem=halo_recv.at[0],
            device_id=(me - 1, row),
            device_id_type=MESH,
        )

    def from_right():
        return pltpu.make_async_remote_copy(
            src_ref=vloc_ref,
            dst_ref=v_ref.at[:, pl.ds(2 * width, width)],
            send_sem=halo_send.at[1],
            recv_sem=halo_recv.at[1],
            device_id=(me + 1, row),
            device_id_type=MESH,
        )

    own = pltpu.make_async_copy(vloc_ref, v_ref.at[:, pl.ds(width, width)], halo_local.at[0])

    @pl.when(a == 0)
    def _():
        greet()
        barrier = pltpu.get_barrier_semaphore()

        @pl.when(jnp.logical_and(extra, rc == 0))
        def _():
            pl.semaphore_signal(barrier, inc=1, device_id=(me - 1, row), device_id_type=MESH)

        @pl.when(jnp.logical_and(extra, rc == inner - 1))
        def _():
            pl.semaphore_signal(barrier, inc=1, device_id=(me + 1, row), device_id_type=MESH)

        peers = (inner - 1) + (outer - 1)

        @pl.when(extra)
        def _():
            pl.semaphore_wait(barrier, peers + 1)

        @pl.when(jnp.logical_not(extra))
        def _():
            pl.semaphore_wait(barrier, peers)

        start_first()
        own.start()

        @pl.when(has_right)
        def _():
            to_right().start()

        @pl.when(has_left)
        def _():
            to_left().start()

        @pl.when(jnp.logical_not(has_left))
        def _():
            v_ref[:, pl.ds(0, width)] = jnp.zeros((v_ref.shape[0], width), v_ref.dtype)

        @pl.when(jnp.logical_not(has_right))
        def _():
            v_ref[:, pl.ds(2 * width, width)] = jnp.zeros((v_ref.shape[0], width), v_ref.dtype)

        own.wait()

        @pl.when(has_right)
        def _():
            to_right().wait_send()
            from_right().wait_recv()

        @pl.when(has_left)
        def _():
            to_left().wait_send()
            from_left().wait_recv()

    blocks = v_ref.shape[1] // BLK - 2 * REACH

    @pl.when(a == min(blocks // 2 - 2, blocks - 1))
    def _():
        start_second()

    start = pl.multiple_of(a * BLK, BLK)
    v_cat = v_ref[:, pl.ds(start, WIDE * BLK)]
    out_ref[...] = lax.dot_general(
        v_cat, k_ref[0], (((1,), (1,)), ((), ())), preferred_element_type=jnp.float32
    )

    @pl.when(a == last)
    def _():
        sum_ref[...] = finish()


def apply_sum(local_vec, kmat, tile):
    rows, width = local_vec.shape
    wide_cols = width + 2 * REACH * BLK
    blocks = kmat.shape[0]
    count = lax.axis_size("pts")
    inner = 8 if count % 8 == 0 else count
    outer = count // inner
    return pl.pallas_call(
        functools.partial(apply_sum_kernel, inner, outer),
        out_shape=(
            jax.ShapeDtypeStruct((rows, blocks * BLK), jnp.float32),
            jax.ShapeDtypeStruct(tile.shape, jnp.float32),
        ),
        grid=(blocks,),
        in_specs=[
            pl.BlockSpec((rows, width), lambda a: (0, 0)),
            pl.BlockSpec((1, BLK, WIDE * BLK), lambda a: (a, 0, 0)),
            pl.BlockSpec(tile.shape, lambda a: (0, 0)),
        ],
        out_specs=(
            pl.BlockSpec((rows, BLK), lambda a: (0, a)),
            pl.BlockSpec(tile.shape, lambda a: (0, 0)),
        ),
        scratch_shapes=[
            pltpu.VMEM((rows, wide_cols), local_vec.dtype),
            pltpu.SemaphoreType.DMA((2,)),
            pltpu.SemaphoreType.DMA((2,)),
            pltpu.SemaphoreType.DMA((1,)),
            pltpu.VMEM((inner,) + tile.shape, jnp.float32),
            pltpu.VMEM((outer, inner) + tile.shape, jnp.float32),
            pltpu.SemaphoreType.DMA((2,)),
            pltpu.SemaphoreType.DMA((inner,)),
            pltpu.SemaphoreType.DMA((inner,)),
            pltpu.SemaphoreType.DMA((outer,)),
            pltpu.SemaphoreType.DMA((outer,)),
        ],
        compiler_params=pltpu.CompilerParams(
            dimension_semantics=("arbitrary",), collective_id=0, has_side_effects=True
        ),
    )(local_vec, kmat, tile)


def per_device(points, noise_var, right_side, pattern):
    local_rows = points.shape[0]
    block_count = local_rows // BLK
    rim_rows = REACH * BLK
    kernel_scale = 1.0 / (4 * BLK)
    first_low = right_side.astype(jnp.bfloat16)
    points_t = points.T
    packed = jnp.concatenate([points_t, first_low], axis=0)
    count = lax.axis_size("pts")
    from_left = lax.ppermute(packed, "pts", [(i, i + 1) for i in range(count - 1)])
    from_right = lax.ppermute(packed, "pts", [(i + 1, i) for i in range(count - 1)])
    wide_points_t = jnp.concatenate([from_left[:F], points_t, from_right[:F]], axis=1)
    first_wide = jnp.concatenate([from_left[F:], first_low, from_right[F:]], axis=1)
    kmat = build_k(pattern, points, wide_points_t, block_count)

    rhs_count = lax.axis_size("rhs")
    rhs_index = lax.axis_index("rhs")

    def apply_operator(vector):
        vec_low = vector.astype(jnp.bfloat16)
        wide_vec = with_halo(vec_low, "pts", 1, rim_rows)
        image_part = apply_k(wide_vec, kmat)
        return noise_var[None, :] * vector + kernel_scale * image_part

    def apply_and_total(vector, parts):
        tile = jnp.zeros((8, 128), jnp.float32)
        tile = lax.dynamic_update_slice(tile, parts, (0, 0))
        vec_low = vector.astype(jnp.bfloat16)
        image_part, summed = apply_sum(vec_low, kmat, tile)
        image = noise_var[None, :] * vector + kernel_scale * image_part
        return image, summed[: parts.shape[0], : parts.shape[1]]

    solution = jnp.zeros_like(right_side)
    residual = right_side
    res_image = noise_var[None, :] * residual + kernel_scale * apply_k(first_wide, kmat)
    direction = jnp.zeros_like(right_side)
    dir_image = jnp.zeros_like(right_side)
    dir_twice = jnp.zeros_like(right_side)
    norm_prev = None
    step_prev = None
    for iteration in range(ITERS):
        square_image, sums = apply_and_total(
            res_image,
            jnp.stack([jnp.sum(residual * residual, axis=1), jnp.sum(res_image * residual, axis=1)]),
        )
        norm_now = sums[0][:, None]
        curvature = sums[1][:, None]
        if iteration == 0:
            step_len = norm_now / curvature
            direction = residual
            dir_image = res_image
            dir_twice = square_image
        else:
            mix_ratio = norm_now / norm_prev
            step_len = norm_now / (curvature - mix_ratio * norm_now / step_prev)
            direction = residual + mix_ratio * direction
            dir_image = res_image + mix_ratio * dir_image
            dir_twice = square_image + mix_ratio * dir_twice
        solution = solution + step_len * direction
        residual = residual - step_len * dir_image
        res_image = res_image - step_len * dir_twice
        norm_prev = norm_now
        step_prev = step_len
    return (solution, residual, res_image)


def solution(mesh):
    placed = (P("pts", None), P("pts"), P("rhs", "pts"), P("pts", None))
    return jax.shard_map(
        per_device,
        mesh=mesh,
        in_specs=placed,
        out_specs=(P("rhs", "pts"), P("rhs", "pts"), P("rhs", "pts")),
        check_vma=False,
    )
```

```python
import functools

import jax
import jax.numpy as jnp
from jax import lax
from jax.experimental import pallas as pl
from jax.experimental.pallas import tpu as pltpu
from jax.sharding import PartitionSpec as P

F = 32
BLK = 128
REACH = 16
ITERS = 2
WIDE = 33
WEXP = 18
MESH = pl.DeviceIdType.MESH


def with_halo(cells, axis, dim, width):
    count = lax.axis_size(axis)
    ends = count - 1
    head = lax.slice_in_dim(cells, 0, width, axis=dim)
    tail = lax.slice_in_dim(cells, cells.shape[dim] - width, cells.shape[dim], axis=dim)
    return jnp.concatenate(
        [
            lax.ppermute(tail, axis, [(i, (i + 1) % count) for i in range(ends)]),
            cells,
            lax.ppermute(head, axis, [((i + 1) % count, i) for i in range(ends)]),
        ],
        axis=dim,
    )


def profile_tile(sq_left, sq_right, cross):
    dist = jnp.maximum((sq_left + sq_right) + cross, 0.0)
    radius = jnp.sqrt(dist)
    base = jnp.maximum(1.0 - radius, 0.0)
    b2 = base * base
    b4 = b2 * b2
    b8 = b4 * b4
    b16 = b8 * b8
    return (b16 * b2) * (WEXP * radius + 1.0)


def build_kernel(pat_ref, pw_ref, pwt_ref, k_ref, mirror, cross_ref, sqr_ref):
    a = pl.program_id(0)
    blocks = pl.num_programs(0)
    start = pl.multiple_of(a * BLK, BLK)
    left = pw_ref[pl.ds(start, BLK), :]
    left_f = left.astype(jnp.float32)
    sq_left = jnp.sum(left_f * left_f, axis=1, keepdims=True)
    left_m2 = left * jnp.asarray(-2.0, jnp.bfloat16)
    window = pwt_ref[:, pl.ds(pl.multiple_of(a * BLK, BLK), WIDE * BLK)]
    cross_ref[...] = jnp.dot(left_m2, window, preferred_element_type=jnp.float32)

    @pl.when(a == 0)
    def _():
        wide_f = pwt_ref[...].astype(jnp.float32)
        sqr_ref[...] = jnp.sum(wide_f * wide_f, axis=0, keepdims=True)

    def body(o, carry):
        col = pl.multiple_of((a + o) * BLK, BLK)
        dst = pl.ds(pl.multiple_of(o * BLK, BLK), BLK)
        live = pat_ref[a, o] != 0
        other = a + o - REACH
        lower = jnp.logical_and(other >= 0, other < a)
        upper = jnp.logical_and(other > a, other < blocks)

        @pl.when(jnp.logical_and(live, lower))
        def _():
            k_ref[0, :, dst] = mirror[a, other]

        @pl.when(jnp.logical_and(live, jnp.logical_not(lower)))
        def _():
            sq_right = sqr_ref[:, pl.ds(col, BLK)]
            value = profile_tile(sq_left, sq_right, cross_ref[:, dst])
            k_ref[0, :, dst] = value.astype(jnp.bfloat16)

            @pl.when(upper)
            def _():
                mirror[other, a] = value.T.astype(jnp.bfloat16)

        @pl.when(jnp.logical_not(live))
        def _():
            k_ref[0, :, dst] = jnp.zeros((BLK, BLK), jnp.bfloat16)

        return carry

    lax.fori_loop(0, WIDE, body, 0)


def apply_kernel(v_ref, k_ref, out_ref):
    a = pl.program_id(0)
    start = pl.multiple_of(a * BLK, BLK)
    v_cat = v_ref[:, pl.ds(start, WIDE * BLK)]
    out_ref[...] = lax.dot_general(
        v_cat, k_ref[0], (((1,), (1,)), ((), ())), preferred_element_type=jnp.float32
    )


def build_k(pattern, points, wide_points_t, blocks):
    rows = points.shape[0]
    wide_cols = wide_points_t.shape[1]
    return pl.pallas_call(
        build_kernel,
        out_shape=jax.ShapeDtypeStruct((blocks, BLK, WIDE * BLK), jnp.bfloat16),
        grid_spec=pltpu.PrefetchScalarGridSpec(
            num_scalar_prefetch=1,
            grid=(blocks,),
            in_specs=[
                pl.BlockSpec((rows, F), lambda a, p: (0, 0)),
                pl.BlockSpec((F, wide_cols), lambda a, p: (0, 0)),
            ],
            out_specs=pl.BlockSpec((1, BLK, WIDE * BLK), lambda a, p: (a, 0, 0)),
            scratch_shapes=[
                pltpu.VMEM((blocks, blocks, BLK, BLK), jnp.bfloat16),
                pltpu.VMEM((BLK, WIDE * BLK), jnp.float32),
                pltpu.VMEM((1, wide_cols), jnp.float32),
            ],
        ),
        compiler_params=pltpu.CompilerParams(dimension_semantics=("arbitrary",)),
    )(pattern, points, wide_points_t)


def apply_k(wide_vec, kmat):
    rows, wide_cols = wide_vec.shape
    blocks = kmat.shape[0]
    return pl.pallas_call(
        apply_kernel,
        out_shape=jax.ShapeDtypeStruct((rows, blocks * BLK), jnp.float32),
        grid=(blocks,),
        in_specs=[
            pl.BlockSpec((rows, wide_cols), lambda a: (0, 0)),
            pl.BlockSpec((1, BLK, WIDE * BLK), lambda a: (a, 0, 0)),
        ],
        out_specs=pl.BlockSpec((rows, BLK), lambda a: (0, a)),
        compiler_params=pltpu.CompilerParams(dimension_semantics=("arbitrary",)),
    )(wide_vec, kmat)


def reduction_steps(inner, outer, part_ref, stage1, stage2, local_sem, send1, recv1, send2, recv2):
    me = lax.axis_index("pts")
    row = lax.axis_index("rhs")
    zc = me // inner
    rc = me % inner

    def greet():
        barrier = pltpu.get_barrier_semaphore()

        def greet_inner(k, carry):
            peer = zc * inner + lax.rem(rc + k, inner)
            pl.semaphore_signal(barrier, inc=1, device_id=(peer, row), device_id_type=MESH)
            return carry

        def greet_outer(k, carry):
            peer = lax.rem(zc + k, outer) * inner + rc
            pl.semaphore_signal(barrier, inc=1, device_id=(peer, row), device_id_type=MESH)
            return carry

        lax.fori_loop(1, inner, greet_inner, 0)
        lax.fori_loop(1, outer, greet_outer, 0)

    def first(slot, other):
        return pltpu.make_async_remote_copy(
            src_ref=part_ref,
            dst_ref=stage1.at[slot],
            send_sem=send1.at[other],
            recv_sem=recv1.at[slot],
            device_id=(zc * inner + other, row),
            device_id_type=MESH,
        )

    def second(slot, other):
        return pltpu.make_async_remote_copy(
            src_ref=stage1,
            dst_ref=stage2.at[slot],
            send_sem=send2.at[other],
            recv_sem=recv2.at[slot],
            device_id=(other * inner + rc, row),
            device_id_type=MESH,
        )

    own1 = pltpu.make_async_copy(part_ref, stage1.at[rc], local_sem.at[0])
    own2 = pltpu.make_async_copy(stage1, stage2.at[zc], local_sem.at[1])

    def start_first():
        own1.start()

        def send_first(k, carry):
            first(rc, lax.rem(rc + k, inner)).start()
            return carry

        lax.fori_loop(1, inner, send_first, 0)

    def start_second():
        def finish_first(k, carry):
            other = lax.rem(rc + k, inner)
            first(rc, other).wait_send()
            first(other, other).wait_recv()
            return carry

        lax.fori_loop(1, inner, finish_first, 0)
        own1.wait()
        own2.start()

        def send_second(k, carry):
            second(zc, lax.rem(zc + k, outer)).start()
            return carry

        lax.fori_loop(1, outer, send_second, 0)

    def finish():
        def finish_second(k, carry):
            other = lax.rem(zc + k, outer)
            second(zc, other).wait_send()
            second(other, other).wait_recv()
            return carry

        lax.fori_loop(1, outer, finish_second, 0)
        own2.wait()
        return jnp.sum(jnp.sum(stage2[...], axis=0), axis=0)

    return greet, start_first, start_second, finish


def apply_sum_kernel(inner, outer, vloc_ref, k_ref, part_ref, out_ref, sum_ref, v_ref, halo_send, halo_recv, halo_local, *scratch):
    a = pl.program_id(0)
    last = pl.num_programs(0) - 1
    greet, start_first, start_second, finish = reduction_steps(inner, outer, part_ref, *scratch)
    me = lax.axis_index("pts")
    row = lax.axis_index("rhs")
    count = inner * outer
    rc = me % inner
    width = vloc_ref.shape[1]
    has_left = me > 0
    has_right = me < count - 1
    extra = jnp.logical_or(
        jnp.logical_and(rc == 0, has_left), jnp.logical_and(rc == inner - 1, has_right)
    )

    def to_right():
        return pltpu.make_async_remote_copy(
            src_ref=vloc_ref,
            dst_ref=v_ref.at[:, pl.ds(0, width)],
            send_sem=halo_send.at[0],
            recv_sem=halo_recv.at[0],
            device_id=(me + 1, row),
            device_id_type=MESH,
        )

    def to_left():
        return pltpu.make_async_remote_copy(
            src_ref=vloc_ref,
            dst_ref=v_ref.at[:, pl.ds(2 * width, width)],
            send_sem=halo_send.at[1],
            recv_sem=halo_recv.at[1],
            device_id=(me - 1, row),
            device_id_type=MESH,
        )

    def from_left():
        return pltpu.make_async_remote_copy(
            src_ref=vloc_ref,
            dst_ref=v_ref.at[:, pl.ds(0, width)],
            send_sem=halo_send.at[0],
            recv_sem=halo_recv.at[0],
            device_id=(me - 1, row),
            device_id_type=MESH,
        )

    def from_right():
        return pltpu.make_async_remote_copy(
            src_ref=vloc_ref,
            dst_ref=v_ref.at[:, pl.ds(2 * width, width)],
            send_sem=halo_send.at[1],
            recv_sem=halo_recv.at[1],
            device_id=(me + 1, row),
            device_id_type=MESH,
        )

    own = pltpu.make_async_copy(vloc_ref, v_ref.at[:, pl.ds(width, width)], halo_local.at[0])

    @pl.when(a == 0)
    def _():
        greet()
        barrier = pltpu.get_barrier_semaphore()

        @pl.when(jnp.logical_and(extra, rc == 0))
        def _():
            pl.semaphore_signal(barrier, inc=1, device_id=(me - 1, row), device_id_type=MESH)

        @pl.when(jnp.logical_and(extra, rc == inner - 1))
        def _():
            pl.semaphore_signal(barrier, inc=1, device_id=(me + 1, row), device_id_type=MESH)

        peers = (inner - 1) + (outer - 1)

        @pl.when(extra)
        def _():
            pl.semaphore_wait(barrier, peers + 1)

        @pl.when(jnp.logical_not(extra))
        def _():
            pl.semaphore_wait(barrier, peers)

        start_first()
        own.start()

        @pl.when(has_right)
        def _():
            to_right().start()

        @pl.when(has_left)
        def _():
            to_left().start()

        @pl.when(jnp.logical_not(has_left))
        def _():
            v_ref[:, pl.ds(0, width)] = jnp.zeros((v_ref.shape[0], width), v_ref.dtype)

        @pl.when(jnp.logical_not(has_right))
        def _():
            v_ref[:, pl.ds(2 * width, width)] = jnp.zeros((v_ref.shape[0], width), v_ref.dtype)

        own.wait()

        @pl.when(has_right)
        def _():
            to_right().wait_send()
            from_right().wait_recv()

        @pl.when(has_left)
        def _():
            to_left().wait_send()
            from_left().wait_recv()

    blocks = v_ref.shape[1] // BLK - 2 * REACH

    @pl.when(a == min(blocks // 2 - 2, blocks - 1))
    def _():
        start_second()

    start = pl.multiple_of(a * BLK, BLK)
    v_cat = v_ref[:, pl.ds(start, WIDE * BLK)]
    out_ref[...] = lax.dot_general(
        v_cat, k_ref[0], (((1,), (1,)), ((), ())), preferred_element_type=jnp.float32
    )

    @pl.when(a == last)
    def _():
        sum_ref[...] = finish()


def apply_sum(local_vec, kmat, tile):
    rows, width = local_vec.shape
    wide_cols = width + 2 * REACH * BLK
    blocks = kmat.shape[0]
    count = lax.axis_size("pts")
    inner = 8 if count % 8 == 0 else count
    outer = count // inner
    return pl.pallas_call(
        functools.partial(apply_sum_kernel, inner, outer),
        out_shape=(
            jax.ShapeDtypeStruct((rows, blocks * BLK), jnp.float32),
            jax.ShapeDtypeStruct(tile.shape, jnp.float32),
        ),
        grid=(blocks,),
        in_specs=[
            pl.BlockSpec((rows, width), lambda a: (0, 0)),
            pl.BlockSpec((1, BLK, WIDE * BLK), lambda a: (a, 0, 0)),
            pl.BlockSpec(tile.shape, lambda a: (0, 0)),
        ],
        out_specs=(
            pl.BlockSpec((rows, BLK), lambda a: (0, a)),
            pl.BlockSpec(tile.shape, lambda a: (0, 0)),
        ),
        scratch_shapes=[
            pltpu.VMEM((rows, wide_cols), local_vec.dtype),
            pltpu.SemaphoreType.DMA((2,)),
            pltpu.SemaphoreType.DMA((2,)),
            pltpu.SemaphoreType.DMA((1,)),
            pltpu.VMEM((inner,) + tile.shape, jnp.float32),
            pltpu.VMEM((outer, inner) + tile.shape, jnp.float32),
            pltpu.SemaphoreType.DMA((2,)),
            pltpu.SemaphoreType.DMA((inner,)),
            pltpu.SemaphoreType.DMA((inner,)),
            pltpu.SemaphoreType.DMA((outer,)),
            pltpu.SemaphoreType.DMA((outer,)),
        ],
        compiler_params=pltpu.CompilerParams(
            dimension_semantics=("arbitrary",), collective_id=0, has_side_effects=True
        ),
    )(local_vec, kmat, tile)


def per_device(points, noise_var, right_side, pattern):
    local_rows = points.shape[0]
    block_count = local_rows // BLK
    rim_rows = REACH * BLK
    kernel_scale = 1.0 / (4 * BLK)
    first_low = right_side.astype(jnp.bfloat16)
    points_t = points.T
    packed = jnp.concatenate([points_t, first_low], axis=0)
    count = lax.axis_size("pts")
    from_left = lax.ppermute(packed, "pts", [(i, i + 1) for i in range(count - 1)])
    from_right = lax.ppermute(packed, "pts", [(i + 1, i) for i in range(count - 1)])
    wide_points_t = jnp.concatenate([from_left[:F], points_t, from_right[:F]], axis=1)
    first_wide = jnp.concatenate([from_left[F:], first_low, from_right[F:]], axis=1)
    kmat = build_k(pattern, points, wide_points_t, block_count)

    rhs_count = lax.axis_size("rhs")
    rhs_index = lax.axis_index("rhs")

    def apply_operator(vector):
        vec_low = vector.astype(jnp.bfloat16)
        wide_vec = with_halo(vec_low, "pts", 1, rim_rows)
        image_part = apply_k(wide_vec, kmat)
        return noise_var[None, :] * vector + kernel_scale * image_part

    def apply_and_total(vector, parts):
        tile = jnp.zeros((8, 128), jnp.float32)
        tile = lax.dynamic_update_slice(tile, parts, (0, 0))
        vec_low = vector.astype(jnp.bfloat16)
        image_part, summed = apply_sum(vec_low, kmat, tile)
        image = noise_var[None, :] * vector + kernel_scale * image_part
        return image, summed[: parts.shape[0], : parts.shape[1]]

    solution = jnp.zeros_like(right_side)
    residual = right_side
    res_image = noise_var[None, :] * residual + kernel_scale * apply_k(first_wide, kmat)
    direction = jnp.zeros_like(right_side)
    dir_image = jnp.zeros_like(right_side)
    dir_twice = jnp.zeros_like(right_side)
    norm_prev = None
    step_prev = None
    for iteration in range(ITERS):
        square_image, sums = apply_and_total(
            res_image,
            jnp.stack([jnp.sum(residual * residual, axis=1), jnp.sum(res_image * residual, axis=1)]),
        )
        norm_now = sums[0][:, None]
        curvature = sums[1][:, None]
        if iteration == 0:
            step_len = norm_now / curvature
            direction = residual
            dir_image = res_image
            dir_twice = square_image
        else:
            mix_ratio = norm_now / norm_prev
            step_len = norm_now / (curvature - mix_ratio * norm_now / step_prev)
            direction = residual + mix_ratio * direction
            dir_image = res_image + mix_ratio * dir_image
            dir_twice = square_image + mix_ratio * dir_twice
        solution = solution + step_len * direction
        residual = residual - step_len * dir_image
        res_image = res_image - step_len * dir_twice
        norm_prev = norm_now
        step_prev = step_len
    return (solution, residual, res_image)


def solution(mesh):
    placed = (P("pts", None), P("pts"), P("rhs", "pts"), P("pts", None))
    return jax.shard_map(
        per_device,
        mesh=mesh,
        in_specs=placed,
        out_specs=(P("rhs", "pts"), P("rhs", "pts"), P("rhs", "pts")),
        check_vma=False,
    )
```
